32 devices in a mesh: dp: 16 (over z, y, core), seq: 2 (over x).
Axes of the slice: x: 2, y: 2, z: 4, core: 2. Of those that a mesh axis runs over, the one named last changes fastest.
Arguments:
- tokens: bfloat16 [16, 1024, 768], P('dp', 'seq'), may hold values from -6 to 6
- cotangent: bfloat16 [16, 1024, 768], P('dp', 'seq'), may hold values from -6 to 6
- lengths: int32 [16], P('dp'), may hold values from 256 to 1024, as said below
- rel_bucket: int32 [2047], replicated, may hold values from 0 to 31, as said below
- gain_attn: bfloat16 [768], P('dp'), may hold values from 0.25 to 1.75
- w_query: bfloat16 [768, 768], P('dp'), may hold values from -0.109375 to 0.109375
- w_key: bfloat16 [768, 768], P('dp'), may hold values from -0.109375 to 0.109375
- w_value: bfloat16 [768, 768], P('dp'), may hold values from -0.21875 to 0.21875
- w_out: bfloat16 [768, 768], P('dp'), may hold values from -0.875 to 0.875
- gain_ff: bfloat16 [768], P('dp'), may hold values from 0.25 to 1.75
- w_in: bfloat16 [768, 3072], P('dp'), may hold values from -0.21875 to 0.21875
- w_back: bfloat16 [3072, 768], P('dp'), may hold values from -0.15625 to 0.15625
- bias_table: float32 [32, 12], P(None, 'seq'), may hold values from -4 to 4
Outputs:
- out: bfloat16 [16, 1024, 768], P('dp', 'seq')
- grad_tokens: bfloat16 [16, 1024, 768], P('dp', 'seq')
- grad_gain_attn: float32 [768], P(('dp', 'seq'))
- grad_w_query: float32 [768, 768], P(('dp', 'seq'))
- grad_w_key: float32 [768, 768], P(('dp', 'seq'))
- grad_w_value: float32 [768, 768], P(('dp', 'seq'))
- grad_w_out: float32 [768, 768], P(('dp', 'seq'))
- grad_gain_ff: float32 [768], P(('dp', 'seq'))
- grad_w_in: float32 [768, 3072], P(('dp', 'seq'))
- grad_w_back: float32 [3072, 768], P(('dp', 'seq'))
- grad_bias_table: float32 [32, 12], P(None, 'seq')
The draws below stay inside these ranges and needn't reach their ends.
Inputs may be any that keep to these rules, and one draw needn't show every extreme that they name: `lengths`: valid positions of each slot; some slot holds 1024 and some slot 256. `rel_bucket`: entry r + 1023 is the bucket of relative offset r, a key's position minus the query's.
All inputs are finite; a program needn't handle non-finite values.
Results may differ from the reference program's by a relative error of at most 0.014.
The reference program's roundings to bfloat16 on the way count: a program that leaves them out, or rounds other values in their place, can miss the bound.
Values may be sent and summed in bfloat16 or wider, within the bound.
No kernel may reach another device: no remote copies, remote signals or barrier semaphores. Data moves between devices by JAX's collectives and lax.ppermute only.
A program may use at most 192 MiB of HBM per device.

```python
import jax
import jax.numpy as jnp
from jax import lax

D = 768
H = 12
DH = 64
FF = 3072
NB = 32
LEN = 1024
SLOTS = 16


def draw_lengths(key, part):
    key_len, key_pick = jax.random.split(jax.random.fold_in(key, 11))
    length_draw = jax.random.randint(key_len, (SLOTS,), LEN // 4, LEN + 1, dtype=jnp.int32)
    slot_order = jax.random.permutation(key_pick, SLOTS)
    length_draw = length_draw.at[slot_order[0]].set(LEN)
    length_draw = length_draw.at[slot_order[1]].set(LEN // 4)
    return length_draw.astype(jnp.int32)


def draw_rel_bucket(key, part):
    half_count = NB // 2
    exact_count = half_count // 2 - 1
    spread_count = half_count - 1 - exact_count
    exact_bounds = jnp.arange(1, exact_count + 1, dtype=jnp.int32)
    chosen = jax.random.permutation(jax.random.fold_in(key, 23), LEN - exact_count - 1)[:spread_count] + exact_count + 1
    bounds = jnp.concatenate([exact_bounds, jnp.sort(chosen).astype(jnp.int32)])
    offsets = jnp.arange(2 * LEN - 1, dtype=jnp.int32) - (LEN - 1)
    magnitude = jnp.abs(offsets)
    level = jnp.sum((magnitude[:, None] >= bounds[None, :]).astype(jnp.int32), axis=1)
    return (level + half_count * (offsets > 0).astype(jnp.int32)).astype(jnp.int32)


def level_of(key, extent, cuts, low, high):
    loudness = 1.0
    for dim, shards_of in cuts:
        steps = jax.random.uniform(jax.random.fold_in(jax.random.fold_in(key, 6), dim), (shards_of,), jnp.float32, low / len(cuts), high / len(cuts))
        loudness = loudness * jnp.repeat(jnp.exp(steps), extent[dim] // shards_of).reshape((-1,) + (1,) * (len(extent) - 1 - dim))
    return loudness


def normal_values(stream_key, extent, deviation, most, cuts=(), kind=jnp.bfloat16):
    array = jax.random.normal(stream_key, extent, jnp.float32) * deviation
    if len(cuts) > 0:
        array = level_of(stream_key, extent, cuts, -0.22, 0.18) * array
    return jnp.clip(array, min=-most, max=most).astype(kind)


def setup_inputs(seed: int = 0) -> dict:
    arg_keys = jax.random.split(jax.random.key(seed), 14)
    return {
        "tokens": normal_values(arg_keys[0], (SLOTS, LEN, D), 1.0, 6.0, ((0, 16), (1, 2))),
        "cotangent": normal_values(arg_keys[1], (SLOTS, LEN, D), 1.0, 6.0, ((0, 16), (1, 2))),
        "lengths": draw_lengths(jax.random.fold_in(arg_keys[13], 71), 0),
        "rel_bucket": draw_rel_bucket(jax.random.fold_in(arg_keys[13], 71), 0),
        "gain_attn": jnp.clip(1.0 + 0.15 * jax.random.normal(arg_keys[4], (D,), jnp.float32), 0.25, 1.75).astype(jnp.bfloat16),
        "w_query": normal_values(arg_keys[5], (D, D), (4 * D) ** -0.5, 0.109375, ((0, 16),)),
        "w_key": normal_values(arg_keys[6], (D, D), (4 * D) ** -0.5, 0.109375, ((0, 16),)),
        "w_value": normal_values(arg_keys[7], (D, D), D ** -0.5, 0.21875, ((0, 16),)),
        "w_out": normal_values(arg_keys[8], (D, D), (D // 16) ** -0.5, 0.875, ((0, 16),)),
        "gain_ff": jnp.clip(1.0 + 0.15 * jax.random.normal(arg_keys[9], (D,), jnp.float32), 0.25, 1.75).astype(jnp.bfloat16),
        "w_in": normal_values(arg_keys[10], (D, FF), D ** -0.5, 0.21875, ((0, 16),)),
        "w_back": normal_values(arg_keys[11], (FF, D), (FF // 2) ** -0.5, 0.15625, ((0, 16),)),
        "bias_table": normal_values(arg_keys[12], (NB, H), 1.0, 4.0, ((1, 2),), jnp.float32),
    }


@jax.custom_vjp
def low(v):
    return lax.optimization_barrier(v.astype(jnp.bfloat16)).astype(jnp.float32)

@jax.custom_vjp
def low_back(v):
    return v

def low_keep(v):
    return (low(v), None)

def low_pass(kept, grad):
    return (grad,)

def back_keep(v):
    return (v, None)

def back_low(kept, grad):
    return (low(grad),)
low.defvjp(low_keep, low_pass)
low_back.defvjp(back_keep, back_low)
epsilon = 1e-06
masked_score = -1e+30
precise = lax.Precision.HIGHEST

def rms_norm(values, gain_vec):
    return values * lax.rsqrt(lax.optimization_barrier(jnp.mean(values * values, axis=-1, keepdims=True)) + epsilon) * gain_vec

def smooth_gate(values):
    return jax.nn.gelu(values, approximate=True)

def reference(tokens, cotangent, lengths, rel_bucket, gain_attn, w_query, w_key, w_value, w_out, gain_ff, w_in, w_back, bias_table):
    positions = jnp.arange(LEN, dtype=jnp.int32)
    offsets = (positions[None, :] - positions[:, None] + jnp.int32(LEN - 1)).astype(jnp.int32)
    buckets = jnp.take(rel_bucket.astype(jnp.int32), offsets, axis=0).astype(jnp.int32)
    lengths_int = lengths.astype(jnp.int32)
    row_valid = (positions[None, :] < lengths_int[:, None]).astype(jnp.float32)
    inputs_all = tokens.astype(jnp.float32)
    grads_all = cotangent.astype(jnp.float32) * row_valid[:, :, None]
    weights = tuple((param.astype(jnp.float32) for param in (gain_attn, w_query, w_key, w_value, w_out, gain_ff, w_in, w_back, bias_table)))

    def forward(slot_length, slot_inputs, gain_first, query_w, key_w, value_w, out_w, gain_second, in_w, back_w, table):
        bias_full = jnp.transpose(jnp.take(table, buckets, axis=0), (2, 0, 1))
        normed = low(rms_norm(slot_inputs, gain_first))
        query = low_back(low(jnp.dot(normed, query_w, precision=precise))).reshape(LEN, H, DH)
        keys = low_back(low(jnp.dot(normed, key_w, precision=precise))).reshape(LEN, H, DH)
        values_h = low_back(low(jnp.dot(normed, value_w, precision=precise))).reshape(LEN, H, DH)
        scores = low_back(jnp.einsum('ihd,jhd->hij', query, keys, precision=precise) + bias_full)
        key_valid = positions < slot_length
        filler = jnp.full(scores.shape, masked_score, dtype=scores.dtype)
        scores = jnp.where(key_valid[None, None, :], scores, filler)
        attn_weights = low(jax.nn.softmax(scores, axis=-1))
        mixed = low_back(low(jnp.einsum('hij,jhd->ihd', attn_weights, values_h, precision=precise).reshape(LEN, D)))
        attn_out = low_back(jnp.dot(mixed, out_w, precision=precise))
        middle = slot_inputs + attn_out
        normed_ff = low(rms_norm(middle, gain_second))
        hidden_pre = low_back(jnp.dot(normed_ff, in_w, precision=precise))
        hidden = low(smooth_gate(hidden_pre))
        return middle + low_back(jnp.dot(hidden, back_w, precision=precise))

    def one_slot(totals, slot_args):
        slot_inputs, slot_grads, slot_length = slot_args
        slot_length = slot_length.astype(jnp.int32)

        def bound(*rest):
            return forward(slot_length, *rest)
        outputs, pullback = jax.vjp(bound, slot_inputs, *weights)
        gradients = pullback(slot_grads)
        new_totals = tuple((total + grad.astype(total.dtype) for total, grad in zip(totals, gradients[1:])))
        return (new_totals, (outputs, gradients[0]))
    zero_totals = tuple((jnp.zeros_like(weight) for weight in weights))
    totals, (outputs, grad_inputs) = lax.scan(one_slot, zero_totals, (inputs_all, grads_all, lengths_int))
    return (outputs.astype(jnp.bfloat16), grad_inputs.astype(jnp.bfloat16), totals[0], totals[1], totals[2], totals[3], totals[4], totals[5], totals[6], totals[7], totals[8])
```

```python
import functools

import jax
import jax.numpy as jnp
from jax import lax
from jax.experimental import pallas as pl
from jax.experimental.pallas import tpu as pltpu
from jax.sharding import PartitionSpec as P

DH = 64
PAIR = 2 * DH
LANES = 128
BLOCKS = 16
NT = (((1,), (1,)), ((), ()))
TN = (((0,), (0,)), ((), ()))
epsilon = 1e-06
masked_score = -1e30
precise = lax.Precision.HIGHEST
f32 = jnp.float32
bf16 = jnp.bfloat16
MiB = 2**20


def dot(a, b):
    return jnp.dot(a, b, preferred_element_type=f32)


def dot_nt(a, b):
    return lax.dot_general(a, b, NT, preferred_element_type=f32)


def dot_tn(a, b):
    return lax.dot_general(a, b, TN, preferred_element_type=f32)


def aligned(value, unit):
    return pl.multiple_of(value, unit)


def head_lanes(shape, dim, head):
    index = lax.broadcasted_iota(jnp.int32, shape, dim)
    return (index < DH) if head == 0 else (index >= DH)


def flag_lane(head):
    return DH if head == 0 else 0


def fill_bias(offsets_ref, head, bias_tile):
    row = jnp.broadcast_to(offsets_ref[0, head : head + 1, :], bias_tile.shape)
    bias_tile[...] = pltpu.roll(row, 0, 1, stride=1, stride_axis=0)


def masked_keys(keys, head, length):
    lane = lax.broadcasted_iota(jnp.int32, keys.shape, 1)
    position = lax.broadcasted_iota(jnp.int32, keys.shape, 0)
    other = jnp.where((lane == flag_lane(head)) & (position >= length), masked_score, 0.0)
    return jnp.where(head_lanes(keys.shape, 1, head), keys.astype(f32), other).astype(bf16)


def only_head(rows, head):
    return jnp.where(head_lanes(rows.shape, 1, head), rows.astype(f32), 0.0).astype(bf16)


def flagged(rows, head):
    lane = lax.broadcasted_iota(jnp.int32, rows.shape, 1)
    flag = jnp.where(lane == flag_lane(head), 1.0, 0.0)
    return jnp.where(head_lanes(rows.shape, 1, head), rows.astype(f32), flag).astype(bf16)


def bias_columns(bias_tile, first, count, key_tiles):
    parts = []
    for tile in range(key_tiles):
        start = aligned((key_tiles - 1 - tile) * LANES + first, LANES)
        parts.append(bias_tile[:, pl.ds(start, count)])
    return jnp.concatenate(parts, axis=0)


def attend_body(block, scal, q_ref, k_ref, v_ref, offsets_ref, out_ref, lse_ref, bias_tile):
    row0, length = scal[0], scal[1]
    rows, key_tiles = q_ref.shape[0], k_ref.shape[0] // LANES
    values_t = jnp.transpose(v_ref[...].astype(f32))
    outs = [[] for _ in range(rows // block)]
    for head in range(2):
        fill_bias(offsets_ref, head, bias_tile)
        keys = masked_keys(k_ref[...], head, length)
        values_h = jnp.where(head_lanes(values_t.shape, 0, head), values_t, 1.0).astype(bf16)
        for b in range(rows // block):
            rs = slice(b * block, (b + 1) * block)
            scores = dot_nt(keys, flagged(q_ref[rs, :], head))
            scores = scores + bias_columns(bias_tile, row0 + b * block, block, key_tiles)
            top = jnp.max(scores, axis=0, keepdims=True)
            weights = jnp.exp(scores - top).astype(bf16)
            mixed_t = dot(values_h, weights)
            total = mixed_t[flag_lane(head) : flag_lane(head) + 1]
            mine = mixed_t[:DH] if head == 0 else mixed_t[DH:]
            outs[b].append(mine / total)
            lse_ref[0, head : head + 1, rs] = top + jnp.log(total)
    for b in range(rows // block):
        joined = jnp.transpose(jnp.concatenate(outs[b], axis=0))
        out_ref[b * block : (b + 1) * block, :] = joined.astype(bf16)


def attend(scal, half, queries, keys, values, offsets):
    rows, width = queries.shape[1:]
    seq_len, pairs, span = keys.shape[0], width // PAIR, offsets.shape[2]
    block = min(256, rows)
    tokens_spec = pl.BlockSpec((rows, PAIR), lambda g, s: (0, g))
    keys_spec = pl.BlockSpec((seq_len, PAIR), lambda g, s: (0, g))
    work = rows * seq_len * width
    return pl.pallas_call(
        functools.partial(attend_body, block),
        out_shape=(
            jax.ShapeDtypeStruct((rows, width), bf16),
            jax.ShapeDtypeStruct((pairs, 2, rows), f32),
        ),
        grid_spec=pltpu.PrefetchScalarGridSpec(
            num_scalar_prefetch=1,
            grid=(pairs,),
            in_specs=[
                pl.BlockSpec((pl.Squeezed(), rows, PAIR), lambda g, s: (half, 0, g)),
                keys_spec,
                keys_spec,
                pl.BlockSpec((1, 2, span), lambda g, s: (g, 0, 0)),
            ],
            out_specs=[tokens_spec, pl.BlockSpec((1, 2, rows), lambda g, s: (g, 0, 0))],
            scratch_shapes=[pltpu.VMEM((LANES, span), f32)],
        ),
        compiler_params=pltpu.CompilerParams(vmem_limit_bytes=40 * MiB),
        cost_estimate=pl.CostEstimate(
            flops=16 * work, transcendentals=work // DH, bytes_accessed=4 * seq_len * width
        ),
        name="attend",
    )(scal, queries, keys, values, offsets)


def diagonal_sums(tile):
    span = tile.shape[1]
    size = tile.shape[0] // 2
    while size >= 8:
        tile = tile[:size] + pltpu.roll(tile[size:], span - size, 1)
        size //= 2
    row = lax.broadcasted_iota(jnp.int32, tile.shape, 0)
    for bit in (1, 2, 4):
        tile = jnp.where((row & bit) != 0, pltpu.roll(tile, span - bit, 1), tile)
    return jnp.sum(tile, axis=0, keepdims=True)


def attend_back_body(block, carry, scal, *refs):
    q_ref, k_ref, v_ref, g_ref, o_ref, lse_ref, offsets_ref = refs[:7]
    dq_ref, dk_ref, dv_ref, diag_ref, bias_tile, diag_tile, dk_sum, dv_sum = refs[-8:]
    row0, length = scal[0], scal[1]
    rows, key_tiles = q_ref.shape[0], k_ref.shape[0] // LANES
    if carry:
        dk_sum[...] = refs[7][...]
        dv_sum[...] = refs[8][...]
    else:
        dk_sum[...] = jnp.zeros_like(dk_sum)
        dv_sum[...] = jnp.zeros_like(dv_sum)
    keys_t = jnp.transpose(k_ref[...].astype(f32)).astype(bf16)
    count = rows // block
    dqs = [[] for _ in range(count)]
    deltas = []
    for b in range(count):
        rs = slice(b * block, (b + 1) * block)
        product = jnp.transpose(g_ref[rs, :].astype(f32) * o_ref[rs, :].astype(f32))
        deltas.append(
            (
                jnp.sum(product[:DH], axis=0, keepdims=True),
                jnp.sum(product[DH:], axis=0, keepdims=True),
            )
        )
    for head in range(2):
        fill_bias(offsets_ref, head, bias_tile)
        diag_tile[...] = jnp.zeros_like(diag_tile)
        keys = masked_keys(k_ref[...], head, length)
        for b in range(count):
            rs = slice(b * block, (b + 1) * block)
            queries = q_ref[rs, :]
            grads = only_head(g_ref[rs, :], head)
            scores = dot_nt(keys, flagged(queries, head))
            scores = scores + bias_columns(bias_tile, row0 + b * block, block, key_tiles)
            probs = jnp.exp(scores - lse_ref[0, head : head + 1, rs])
            grad_probs = dot_nt(v_ref[...], grads)
            grad_scores = probs * (grad_probs - deltas[b][head])
            for tile in range(key_tiles):
                start = aligned((key_tiles - 1 - tile) * LANES + row0 + b * block, LANES)
                diag_tile[:, pl.ds(start, block)] += grad_scores[tile * LANES : (tile + 1) * LANES]
            grad_scores = grad_scores.astype(bf16)
            dv_sum[...] += dot(probs.astype(bf16), grads)
            dk_sum[...] += dot(grad_scores, only_head(queries, head))
            dq_t = dot(keys_t, grad_scores)
            dqs[b].append(dq_t[:DH] if head == 0 else dq_t[DH:])
        diag_ref[0, head : head + 1, :] = diagonal_sums(diag_tile[...])
    for b in range(count):
        joined = jnp.transpose(jnp.concatenate(dqs[b], axis=0))
        dq_ref[b * block : (b + 1) * block, :] = joined.astype(bf16)
    dk_ref[...] = dk_sum[...].astype(dk_ref.dtype)
    dv_ref[...] = dv_sum[...].astype(dv_ref.dtype)


def attend_back(scal, half, queries, keys, values, grads, outs, lse, offsets, carry):
    rows, width = queries.shape[1:]
    seq_len, pairs, span = keys.shape[0], width // PAIR, offsets.shape[2]
    block = min(256, rows)
    rows_spec = pl.BlockSpec((rows, PAIR), lambda g, s: (0, g))
    keys_spec = pl.BlockSpec((seq_len, PAIR), lambda g, s: (0, g))
    offsets_spec = pl.BlockSpec((1, 2, span), lambda g, s: (g, 0, 0))
    specs = [
        pl.BlockSpec((pl.Squeezed(), rows, PAIR), lambda g, s: (half, 0, g)),
        keys_spec,
        keys_spec,
        rows_spec,
        rows_spec,
        pl.BlockSpec((1, 2, rows), lambda g, s: (g, 0, 0)),
        offsets_spec,
    ]
    kind = f32
    if carry:
        specs += [keys_spec, keys_spec]
        kind = bf16
    work = rows * seq_len * width
    return pl.pallas_call(
        functools.partial(attend_back_body, block, bool(carry)),
        out_shape=(
            jax.ShapeDtypeStruct((rows, width), bf16),
            jax.ShapeDtypeStruct((seq_len, width), kind),
            jax.ShapeDtypeStruct((seq_len, width), kind),
            jax.ShapeDtypeStruct(offsets.shape, f32),
        ),
        grid_spec=pltpu.PrefetchScalarGridSpec(
            num_scalar_prefetch=1,
            grid=(pairs,),
            in_specs=specs,
            out_specs=[rows_spec, keys_spec, keys_spec, offsets_spec],
            scratch_shapes=[
                pltpu.VMEM((LANES, span), f32),
                pltpu.VMEM((LANES, span), f32),
                pltpu.VMEM((seq_len, PAIR), f32),
                pltpu.VMEM((seq_len, PAIR), f32),
            ],
        ),
        compiler_params=pltpu.CompilerParams(vmem_limit_bytes=48 * MiB),
        cost_estimate=pl.CostEstimate(
            flops=40 * work, transcendentals=work // DH, bytes_accessed=12 * seq_len * width
        ),
        name="attend_back",
    )(scal, queries, keys, values, grads, outs, lse, offsets, *carry)


def normed_rows(values, gain_row):
    inverse = lax.rsqrt(jnp.mean(values * values, axis=-1, keepdims=True) + epsilon)
    return values * inverse * gain_row, inverse


def project_body(scal, own_ref, peer_ref, w0_ref, w1_ref, normed_ref, q_ref, k_ref, v_ref, w_ref, gain_ref):
    own_p = scal[2]
    side, step = pl.program_id(0), pl.program_id(1)
    rows, width = w0_ref.shape[1], q_ref.shape[1]

    @pl.when((side == 0) & (step == 0))
    def gather_weights():
        for core, piece in enumerate((w0_ref, w1_ref)):
            for high in range(BLOCKS // 2):
                part = ((high << 1) | core) ^ own_p
                start = aligned(part * rows, 16)
                w_ref[pl.ds(start, rows), :] = piece[high, :, : 3 * width]
                gain_ref[pl.ds(start, rows), :] = piece[high, :, 3 * width :].astype(f32)

    gain_row = jnp.transpose(gain_ref[...])[0:1, :]
    values = jnp.where(side == 0, own_ref[...].astype(f32), peer_ref[...].astype(f32))
    normed = normed_rows(values, gain_row)[0].astype(bf16)
    normed_ref[...] = normed
    made = dot(normed, w_ref[...]).astype(bf16)
    q_ref[...] = made[:, :width]
    k_ref[...] = made[:, width : 2 * width]
    v_ref[...] = made[:, 2 * width :]


def project(scal, own, peer, pieces, width):
    rows, depth = own.shape
    block = min(256, rows)
    steps = rows // block
    whole = pl.BlockSpec(pieces[0].shape, lambda h, b, s: (0, 0, 0))
    by_half = pl.BlockSpec((pl.Squeezed(), block, width), lambda h, b, s: (h, b, 0))
    by_place = pl.BlockSpec((pl.Squeezed(), block, width), lambda h, b, s: (h ^ s[3], b, 0))
    stacked = jax.ShapeDtypeStruct((2, rows, width), bf16)
    return pl.pallas_call(
        project_body,
        out_shape=(
            jax.ShapeDtypeStruct((2, rows, depth), bf16),
            stacked,
            stacked,
            stacked,
            jax.ShapeDtypeStruct((depth, 3 * width), bf16),
            jax.ShapeDtypeStruct((depth, LANES), f32),
        ),
        grid_spec=pltpu.PrefetchScalarGridSpec(
            num_scalar_prefetch=1,
            grid=(2, steps),
            in_specs=[
                pl.BlockSpec((block, depth), lambda h, b, s: (b * (1 - h) + (steps - 1) * h, 0)),
                pl.BlockSpec((block, depth), lambda h, b, s: (b * h, 0)),
                whole,
                whole,
            ],
            out_specs=[
                pl.BlockSpec((pl.Squeezed(), block, depth), lambda h, b, s: (h, b, 0)),
                by_half,
                by_place,
                by_place,
                pl.BlockSpec((depth, 3 * width), lambda h, b, s: (0, 0)),
                pl.BlockSpec((depth, LANES), lambda h, b, s: (0, 0)),
            ],
        ),
        compiler_params=pltpu.CompilerParams(vmem_limit_bytes=32 * MiB),
        cost_estimate=pl.CostEstimate(
            flops=12 * rows * depth * width, transcendentals=0, bytes_accessed=10 * rows * depth
        ),
        name="project",
    )(scal, own, peer, *pieces)


def gelu_parts(values):
    scale = 0.7978845608028654
    square = values * values
    bend = jnp.tanh(scale * (values + 0.044715 * (values * square)))
    half = 0.5 * (1.0 + bend)
    slope = half + (0.5 * scale) * values * (1.0 - bend * bend) * (1.0 + 0.134145 * square)
    return values * half, slope


def store_blocks(keep_ref, send_ref, total, own_r, rows):
    for rel in range(2 * BLOCKS):
        start = aligned((rel ^ own_r) * rows, 8)
        piece = total[pl.ds(start, rows), :].astype(bf16)
        side, core, mid, low, high = rel & 1, (rel >> 1) & 1, (rel >> 2) & 1, (rel >> 3) & 1, rel >> 4
        target = send_ref if core else keep_ref
        target[side, mid, low, high] = piece


def feed_body(scal, *refs):
    tok_ref, cot_ref, mine_ref, theirs_ref, gain_ref = refs[:5]
    wo_refs, wi_refs, wb_refs = refs[5:9], refs[9:13], refs[13:17]
    out_ref, mid_grad_ref, mix_own_ref, mix_peer_ref, gain_grad_ref = refs[17:22]
    in_keep, in_send, back_keep, back_send, proj_keep, proj_send = refs[22:28]
    mid_s, nff_s, nff_t, rows_s, out_s, nff_grad, wi_s, wb_s, wo_s, mix_s, total = refs[28:]
    row0, length, own_p, me = scal[0], scal[1], scal[2], scal[3]
    own_r = own_p * 2 + me
    step = pl.program_id(0)
    rows, depth = tok_ref.shape
    half = depth // 2
    gain_row = jnp.transpose(gain_ref[...])[1:2, :]

    def assemble(pieces, target, shard):
        for core in range(2):
            for side in range(2):
                piece = pieces[2 * core + side]
                column = aligned((side ^ me) * half, LANES)
                for high in range(BLOCKS // 2):
                    part = ((high << 1) | core) ^ own_p
                    target[pl.ds(aligned(part * shard, 16), shard), pl.ds(column, half)] = piece[high]

    @pl.when(step == 0)
    def start():
        assemble(wo_refs, wo_s, depth // BLOCKS)
        mix_s[:, pl.ds(aligned(me * half, LANES), half)] = mine_ref[...]
        mix_s[:, pl.ds(aligned((1 - me) * half, LANES), half)] = theirs_ref[...]
        middle = tok_ref[...].astype(f32) + dot(mix_s[...], wo_s[...])
        mid_s[...] = middle
        normed = normed_rows(middle, gain_row)[0].astype(bf16)
        nff_s[...] = normed
        nff_t[...] = jnp.transpose(normed.astype(f32)).astype(bf16)
        position = row0 + lax.broadcasted_iota(jnp.int32, (rows, depth), 0)
        rows_s[...] = jnp.where(position < length, cot_ref[...].astype(f32), 0.0).astype(bf16)
        out_s[...] = middle
        nff_grad[...] = jnp.zeros_like(nff_grad)

    assemble(wi_refs, wi_s, depth // BLOCKS)
    quarter = own_p & 3
    for core in range(2):
        for side in range(2):
            piece = wb_refs[2 * core + side]
            column = aligned((side ^ me) * half, LANES)
            shard = piece.shape[2]
            for mid in range(2):
                part = ((mid << 1) | core) ^ quarter
                wb_s[pl.ds(aligned(part * shard, 16), shard), pl.ds(column, half)] = piece[0, mid]

    pre = dot(nff_s[...], wi_s[...])
    hidden, slope = gelu_parts(pre)
    hidden = hidden.astype(bf16)
    out_s[...] += dot(hidden, wb_s[...])
    pre_grad = (dot_nt(rows_s[...], wb_s[...]) * slope).astype(bf16)
    total[...] = dot_tn(hidden, rows_s[...])
    block_rows = back_keep.shape[4]
    low = own_r & 7
    for rel in range(8):
        start_row = aligned((rel ^ low) * block_rows, 8)
        target = back_send if (rel >> 1) & 1 else back_keep
        target[rel >> 2, rel & 1, 0, 0] = total[pl.ds(start_row, block_rows), :].astype(bf16)
    nff_grad[...] += dot_nt(pre_grad, wi_s[...])
    total[...] = dot(nff_t[...], pre_grad)
    store_blocks(in_keep, in_send, total, own_r, in_keep.shape[4])

    @pl.when(step == pl.num_programs(0) - 1)
    def finish():
        out_ref[...] = out_s[...].astype(bf16)
        middle = mid_s[...]
        inverse = lax.rsqrt(jnp.mean(middle * middle, axis=-1, keepdims=True) + epsilon)
        grads = nff_grad[...]
        gain_sum = jnp.sum(grads * middle * inverse, axis=0, keepdims=True)
        gain_grad_ref[...] = jnp.broadcast_to(gain_sum, gain_grad_ref.shape)
        scaled = grads * gain_row
        inner = jnp.sum(scaled * middle, axis=-1, keepdims=True)
        mid_grad = (
            rows_s[...].astype(f32)
            + inverse * scaled
            - middle * (inverse * inverse * inverse) * (inner / depth)
        )
        mid_grad_ref[...] = mid_grad
        attn_grad = mid_grad.astype(bf16)
        total[...] = dot_tn(mix_s[...], attn_grad)
        store_blocks(proj_keep, proj_send, total, own_r, proj_keep.shape[4])
        mix_s[...] = dot_nt(attn_grad, wo_s[...]).astype(bf16)
        mix_own_ref[...] = mix_s[:, pl.ds(aligned(me * half, LANES), half)]
        mix_peer_ref[...] = mix_s[:, pl.ds(aligned((1 - me) * half, LANES), half)]


def feed(scal, tokens, cotangent, mine, theirs, gains, out_pieces, in_pieces, back_pieces):
    rows, depth = tokens.shape
    half = depth // 2
    high, shard, _ = in_pieces[0].shape
    back_shard = back_pieces[0].shape[2]
    steps = in_pieces[0].shape[2] // half
    hidden = steps * depth
    row_count = depth // (2 * BLOCKS)
    fixed = lambda *shape: pl.BlockSpec(shape, lambda f, s: (0,) * len(shape))
    in_out = pl.BlockSpec((2, 2, 2, 2, row_count, depth), lambda f, s: (0, 0, 0, 0, 0, f))
    back_out = pl.BlockSpec(
        (2, 2, 1, 1, hidden // (2 * BLOCKS), depth),
        lambda f, s: (0, 0, (f ^ (s[2] >> 2)) & 1, (f ^ (s[2] >> 2)) >> 1, 0, 0),
    )
    in_shape = jax.ShapeDtypeStruct((2, 2, 2, 2, row_count, hidden), bf16)
    back_shape = jax.ShapeDtypeStruct((2, 2, 2, 2, hidden // (2 * BLOCKS), depth), bf16)
    proj_shape = jax.ShapeDtypeStruct((2, 2, 2, 2, row_count, depth), bf16)
    half_shape = jax.ShapeDtypeStruct((rows, half), bf16)
    return pl.pallas_call(
        feed_body,
        out_shape=(
            jax.ShapeDtypeStruct((rows, depth), bf16),
            jax.ShapeDtypeStruct((rows, depth), f32),
            half_shape,
            half_shape,
            jax.ShapeDtypeStruct((8, depth), f32),
            in_shape,
            in_shape,
            back_shape,
            back_shape,
            proj_shape,
            proj_shape,
        ),
        grid_spec=pltpu.PrefetchScalarGridSpec(
            num_scalar_prefetch=1,
            grid=(steps,),
            in_specs=[
                fixed(rows, depth),
                fixed(rows, depth),
                fixed(rows, half),
                fixed(rows, half),
                fixed(depth, LANES),
            ]
            + [fixed(high, shard, half)] * 4
            + [pl.BlockSpec((high, shard, half), lambda f, s: (0, 0, f))] * 4
            + [
                pl.BlockSpec((1, 2, back_shard, half), lambda f, s: (f ^ (s[2] >> 2), 0, 0, 0)),
            ]
            * 4,
            out_specs=[
                fixed(rows, depth),
                fixed(rows, depth),
                fixed(rows, half),
                fixed(rows, half),
                fixed(8, depth),
                in_out,
                in_out,
                back_out,
                back_out,
                fixed(2, 2, 2, 2, row_count, depth),
                fixed(2, 2, 2, 2, row_count, depth),
            ],
            scratch_shapes=[
                pltpu.VMEM((rows, depth), f32),
                pltpu.VMEM((rows, depth), bf16),
                pltpu.VMEM((depth, rows), bf16),
                pltpu.VMEM((rows, depth), bf16),
                pltpu.VMEM((rows, depth), f32),
                pltpu.VMEM((rows, depth), f32),
                pltpu.VMEM((depth, depth), bf16),
                pltpu.VMEM((depth, depth), bf16),
                pltpu.VMEM((depth, depth), bf16),
                pltpu.VMEM((rows, depth), bf16),
                pltpu.VMEM((depth, depth), f32),
            ],
        ),
        compiler_params=pltpu.CompilerParams(vmem_limit_bytes=56 * MiB),
        cost_estimate=pl.CostEstimate(
            flops=12 * rows * depth * hidden, transcendentals=rows * hidden, bytes_accessed=40 * MiB
        ),
        name="feed",
    )(scal, tokens, cotangent, mine, theirs, gains, *out_pieces, *in_pieces, *back_pieces)


def project_back_body(
    scal, tok_ref, peer_ref, normed_ref, dq0_ref, dq1_ref, dk_ref, dv_ref, w_ref, gain_ref, ff_ref,
    own_ref, send_ref, keep_ref, away_ref, total, gain_s, joined
):
    own_p = scal[2]
    side = pl.program_id(0)
    rows, width = dq0_ref.shape
    depth = tok_ref.shape[1]

    @pl.when(side == 0)
    def clear():
        total[...] = jnp.zeros_like(total)
        gain_s[...] = jnp.zeros_like(gain_s)
        gain_s[1:2, :] = ff_ref[0:1, :]
        joined[:, :width] = dq1_ref[...]

    @pl.when(side == 1)
    def swap():
        joined[:, :width] = dq0_ref[...]

    joined[:, width : 2 * width] = dk_ref[...]
    joined[:, 2 * width :] = dv_ref[...]
    grads = dot_nt(joined[...], w_ref[...])
    values = jnp.where(side == 0, peer_ref[...].astype(f32), tok_ref[...].astype(f32))
    inverse = lax.rsqrt(jnp.mean(values * values, axis=-1, keepdims=True) + epsilon)
    gain_s[0:1, :] += jnp.sum(grads * values * inverse, axis=0, keepdims=True)
    total[:, : 3 * width] += dot_tn(normed_ref[...], joined[...])

    @pl.when(side == 0)
    def outgoing():
        send_ref[...] = grads.astype(bf16)

    @pl.when(side == 1)
    def staying():
        own_ref[...] = grads
        gains = jnp.concatenate([gain_s[...], jnp.zeros((LANES - 8, depth), f32)], axis=0)
        total[:, 3 * width :] = jnp.transpose(gains)
        shard = depth // BLOCKS
        for rel in range(BLOCKS):
            start = aligned((rel ^ own_p) * shard, 16)
            target = away_ref if rel & 1 else keep_ref
            target[(rel >> 1) & 1, (rel >> 2) & 1, rel >> 3] = total[pl.ds(start, shard), :].astype(bf16)


def project_back(scal, tokens, peer, normed, dq_own, dq_peer, dk, dv, weights, gains, ff_gain):
    rows, depth = tokens.shape
    width = dq_own.shape[1]
    wide = 3 * width + LANES
    shard = depth // BLOCKS
    fixed = lambda *shape: pl.BlockSpec(shape, lambda h, s: (0,) * len(shape))
    place = pl.BlockSpec((rows, width), lambda h, s: (1 - h ^ s[3], 0))
    blocks = jax.ShapeDtypeStruct((2, 2, 2, shard, wide), bf16)
    return pl.pallas_call(
        project_back_body,
        out_shape=(
            jax.ShapeDtypeStruct((rows, depth), f32),
            jax.ShapeDtypeStruct((rows, depth), bf16),
            blocks,
            blocks,
        ),
        grid_spec=pltpu.PrefetchScalarGridSpec(
            num_scalar_prefetch=1,
            grid=(2,),
            in_specs=[
                fixed(rows, depth),
                fixed(rows, depth),
                pl.BlockSpec((pl.Squeezed(), rows, depth), lambda h, s: (1 - h, 0, 0)),
                fixed(rows, width),
                fixed(rows, width),
                place,
                place,
                fixed(depth, 3 * width),
                fixed(depth, LANES),
                fixed(8, depth),
            ],
            out_specs=[
                fixed(rows, depth),
                fixed(rows, depth),
                fixed(2, 2, 2, shard, wide),
                fixed(2, 2, 2, shard, wide),
            ],
            scratch_shapes=[
                pltpu.VMEM((depth, wide), f32),
                pltpu.VMEM((8, depth), f32),
                pltpu.VMEM((rows, 3 * width), bf16),
            ],
        ),
        compiler_params=pltpu.CompilerParams(vmem_limit_bytes=48 * MiB),
        cost_estimate=pl.CostEstimate(
            flops=24 * rows * depth * width, transcendentals=0, bytes_accessed=16 * MiB
        ),
        name="project_back",
    )(scal, tokens, peer, normed, dq_own, dq_peer, dk, dv, weights, gains, ff_gain)


def last_body(tok_ref, mid_ref, own_ref, come_ref, gain_ref, out_ref):
    depth = tok_ref.shape[1]
    gain_row = jnp.transpose(gain_ref[...])[0:1, :]
    values = tok_ref[...].astype(f32)
    inverse = lax.rsqrt(jnp.mean(values * values, axis=-1, keepdims=True) + epsilon)
    scaled = (own_ref[...] + come_ref[...].astype(f32)) * gain_row
    inner = jnp.sum(scaled * values, axis=-1, keepdims=True)
    grads = inverse * scaled - values * (inverse * inverse * inverse) * (inner / depth)
    out_ref[...] = (mid_ref[...] + grads).astype(bf16)


def last(tokens, mid_grad, own, come, gains):
    rows, depth = tokens.shape
    block = min(128, rows)
    spec = pl.BlockSpec((block, depth), lambda b: (b, 0))
    return pl.pallas_call(
        last_body,
        out_shape=jax.ShapeDtypeStruct((rows, depth), bf16),
        grid=(rows // block,),
        in_specs=[spec, spec, spec, spec, pl.BlockSpec((depth, LANES), lambda b: (0, 0))],
        out_specs=spec,
        cost_estimate=pl.CostEstimate(
            flops=16 * rows * depth, transcendentals=0, bytes_accessed=12 * rows * depth
        ),
        name="last",
    )(tokens, mid_grad, own, come, gains)


def swap(value, bit):
    size = lax.axis_size("dp")
    return lax.ppermute(value, "dp", [(i, i ^ bit) for i in range(size)])


def cross(value):
    return lax.ppermute(value, "seq", [(0, 1), (1, 0)])


def high_bits():
    size = lax.axis_size("dp")
    return [1 << k for k in range(1, size.bit_length() - 1)]


def gather_bits(shard, bits, lead=0):
    for bit in bits:
        shard = jnp.stack([shard, swap(shard, bit)], axis=lead)
        lead += 1
    return shard


def merged(value, lead):
    return value.reshape((-1,) + value.shape[lead:])


def absolute_pieces(pieces):
    size = lax.axis_size("dp")
    both = jnp.stack(pieces)
    sides = both.shape[0] // 2
    both = both.reshape((2, sides) + both.shape[1:])
    rows, width = both.shape[3:]
    both = both.transpose(2, 0, 1, 3, 4).reshape(size, sides, rows, width)
    both = jnp.take(both, lax.axis_index("dp") ^ jnp.arange(size), axis=0)
    both = both.transpose(0, 2, 1, 3).reshape(BLOCKS // 2, 2, -1, sides, width)
    both = both.transpose(1, 3, 0, 2, 4)
    return [both[core, side] for core in range(2) for side in range(sides)]


def fold(keep, come, hops):
    for hop in hops:
        away = (keep[1].astype(f32) + come[1].astype(f32)).astype(bf16)
        keep = (keep[0].astype(f32) + come[0].astype(f32)).astype(bf16)
        come = hop(away)
    return keep.astype(f32) + come.astype(f32)


def reduce_blocks(keep, send, order):
    size = lax.axis_size("dp")
    if size == BLOCKS:
        hops = [cross if bit == 0 else functools.partial(swap, bit=bit) for bit in order]
        return fold(keep, swap(send, 1), hops)
    me = lax.axis_index("seq")
    rank = sorted(range(len(order)), key=lambda i: order[i])
    axes = [i + 1 for i in rank]
    sides = 1 if order and 0 in order else 0
    axes.insert(sides, 0)
    both = jnp.stack([keep, send])
    width = both.shape[-1]
    both = both.transpose(axes[::-1] + [both.ndim - 2, both.ndim - 1])
    both = both.reshape((-1,) + both.shape[-2:])
    if sides:
        both = jnp.take(both, me ^ jnp.arange(both.shape[0]), axis=0)
    spots = size * (2 if sides else 1)
    own = lax.axis_index("dp") * 2 + me if sides else lax.axis_index("dp")
    both = both.reshape(spots, -1, width)
    both = jnp.take(both, own ^ jnp.arange(spots), axis=0)
    bits = [1 << k for k in range(size.bit_length() - 1)][::-1]
    hops = [functools.partial(swap, bit=bit) for bit in bits] + ([cross] if sides else [])
    both = both.reshape((2,) * len(hops) + both.shape[1:])
    return fold(both[0], hops[0](both[1]), hops[1:])


def local(
    tokens,
    cotangent,
    lengths,
    rel_bucket,
    gain_attn,
    w_query,
    w_key,
    w_value,
    w_out,
    gain_ff,
    w_in,
    w_back,
    bias_table,
):
    size = lax.axis_size("dp")
    place, me = lax.axis_index("dp"), lax.axis_index("seq")
    own, cot = tokens[0], cotangent[0]
    rows, depth = own.shape
    seq_len = rows * 2
    width = depth // 2
    hidden = w_in.shape[1]
    near = size == BLOCKS
    length = lengths[0]
    part = place if near else jnp.int32(0)
    info = jnp.stack([me * rows, length, part, me]).astype(jnp.int32)
    far_info = jnp.stack([(1 - me) * rows, length, part, me]).astype(jnp.int32)
    bits = high_bits()
    down = bits[::-1]

    peer = cross(own)
    columns = [lax.dynamic_slice_in_dim(w, me * width, width, 1) for w in (w_query, w_key, w_value)]
    gains = jnp.pad(jnp.stack([gain_attn, gain_ff], axis=1), ((0, 0), (0, LANES - 2)))
    first = merged(gather_bits(jnp.concatenate(columns + [gains], axis=1), down), len(down))
    first = [first, swap(first, 1)]

    in_half = w_in.reshape(-1, hidden // depth, 2, width)
    in_half = lax.dynamic_index_in_dim(in_half, me, 2, keepdims=False).reshape(-1, hidden // 2)
    out_half = lax.dynamic_slice_in_dim(w_out, me * width, width, 1)
    back_half = lax.dynamic_slice_in_dim(w_back, me * width, width, 1)
    out_mine = merged(gather_bits(out_half, down), len(down))
    in_mine = merged(gather_bits(in_half, down), len(down))
    out_mine = [out_mine, cross(out_mine)]
    in_mine = [in_mine, cross(in_mine)]
    back_mine = gather_bits(back_half, down[:-1])
    back_mine = [back_mine, cross(back_mine)]
    back_mine = [merged(gather_bits(b, down[-1:], len(down) - 1), len(down)) for b in back_mine]
    out_pieces = out_mine + [swap(b, 1) for b in out_mine]
    in_pieces = in_mine + [swap(b, 1) for b in in_mine]
    back_pieces = back_mine + [swap(b, 1) for b in back_mine]
    if not near:
        first, out_pieces = absolute_pieces(first), absolute_pieces(out_pieces)
        in_pieces, back_pieces = absolute_pieces(in_pieces), absolute_pieces(back_pieces)
    back_pieces = [b.reshape((4, 2) + b.shape[1:]) for b in back_pieces]

    padded = jnp.pad(rel_bucket, (0, 1), constant_values=-1)[::-1]
    padded = jnp.concatenate([padded[LANES:], padded[:LANES]])
    choice = jnp.arange(bias_table.shape[0], dtype=jnp.int32)[:, None] == padded[None, :]
    choice = choice.astype(f32)
    offsets = lax.dot_general(bias_table, choice, TN, precision=precise)
    offsets = offsets.reshape(-1, 2, 2 * seq_len)

    normed, query, keys, values, weights, gain_cols = project(info, own, peer, first, width)
    keys, values = keys.reshape(seq_len, width), values.reshape(seq_len, width)
    far_out, far_lse = attend(far_info, 1, query, keys, values, offsets)
    theirs = cross(far_out)
    near_out, near_lse = attend(info, 0, query, keys, values, offsets)
    (
        result,
        mid_grad,
        mix_own,
        mix_peer,
        ff_gain,
        in_keep,
        in_send,
        back_keep,
        back_send,
        proj_keep,
        proj_send,
    ) = feed(info, own, cot, near_out, theirs, gain_cols, out_pieces, in_pieces, back_pieces)
    far_grads = cross(mix_peer)
    grad_back = reduce_blocks(back_keep, back_send, (2, 0, 4, 8))
    grad_in = reduce_blocks(in_keep, in_send, (0, 2, 4, 8))
    grad_out = reduce_blocks(proj_keep, proj_send, (0, 2, 4, 8))
    dq_own, dk, dv, diag_own = attend_back(
        info, 0, query, keys, values, mix_own, near_out, near_lse, offsets, ()
    )
    dq_peer, dk, dv, diag_peer = attend_back(
        far_info, 1, query, keys, values, far_grads, far_out, far_lse, offsets, (dk, dv)
    )
    stay, leave, w_keep, w_send = project_back(
        info, own, peer, normed, dq_own, dq_peer, dk, dv, weights, gain_cols, ff_gain
    )
    come = cross(leave)
    grad_first = reduce_blocks(w_keep, w_send, (2, 4, 8))
    diag = (diag_own + diag_peer).reshape(-1, 2 * seq_len)
    table = lax.dot_general(choice, diag, NT, precision=precise)
    for bit in [1] + bits:
        table = table + swap(table, bit)
    grad_tokens = last(own, mid_grad, stay, come, gain_cols)

    count = grad_first.shape[0] // 2
    mine = lax.dynamic_slice_in_dim(grad_first, me * count, count, 0)
    theirs = cross(lax.dynamic_slice_in_dim(grad_first, (1 - me) * count, count, 0))
    swapped = me == 1
    low, high = jnp.where(swapped, theirs, mine), jnp.where(swapped, mine, theirs)
    full = [
        jnp.concatenate([low[:, i * width : (i + 1) * width], high[:, i * width : (i + 1) * width]], 1)
        for i in range(3)
    ]
    gain_sums = low[:, 3 * width :] + high[:, 3 * width :]
    return (
        result[None],
        grad_tokens[None],
        gain_sums[:, 0],
        full[0],
        full[1],
        full[2],
        grad_out,
        gain_sums[:, 1],
        grad_in,
        grad_back,
        table,
    )


def solution(mesh):
    return jax.shard_map(
        local,
        mesh=mesh,
        in_specs=(
            P("dp", "seq", None),
            P("dp", "seq", None),
            P("dp"),
            P(),
            P("dp"),
            P("dp", None),
            P("dp", None),
            P("dp", None),
            P("dp", None),
            P("dp"),
            P("dp", None),
            P("dp", None),
            P(None, "seq"),
        ),
        out_specs=(
            P("dp", "seq", None),
            P("dp", "seq", None),
            P(("dp", "seq")),
            P(("dp", "seq"), None),
            P(("dp", "seq"), None),
            P(("dp", "seq"), None),
            P(("dp", "seq"), None),
            P(("dp", "seq")),
            P(("dp", "seq"), None),
            P(("dp", "seq"), None),
            P(None, "seq"),
        ),
        check_vma=False,
    )
```

```python
import functools

import jax
import jax.numpy as jnp
from jax import lax
from jax.experimental import pallas as pl
from jax.experimental.pallas import tpu as pltpu
from jax.sharding import PartitionSpec as P

DH = 64
PAIR = 2 * DH
LANES = 128
BLOCKS = 16
NT = (((1,), (1,)), ((), ()))
TN = (((0,), (0,)), ((), ()))
epsilon = 1e-06
masked_score = -1e30
precise = lax.Precision.HIGHEST
f32 = jnp.float32
bf16 = jnp.bfloat16
MiB = 2**20


def dot(a, b):
    return jnp.dot(a, b, preferred_element_type=f32)


def dot_nt(a, b):
    return lax.dot_general(a, b, NT, preferred_element_type=f32)


def dot_tn(a, b):
    return lax.dot_general(a, b, TN, preferred_element_type=f32)


def aligned(value, unit):
    return pl.multiple_of(value, unit)


def head_lanes(shape, dim, head):
    index = lax.broadcasted_iota(jnp.int32, shape, dim)
    return (index < DH) if head == 0 else (index >= DH)


def flag_lane(head):
    return DH if head == 0 else 0


def fill_bias(offsets_ref, head, bias_tile):
    row = jnp.broadcast_to(offsets_ref[0, head : head + 1, :], bias_tile.shape)
    bias_tile[...] = pltpu.roll(row, 0, 1, stride=1, stride_axis=0)


def masked_keys(keys, head, length):
    lane = lax.broadcasted_iota(jnp.int32, keys.shape, 1)
    position = lax.broadcasted_iota(jnp.int32, keys.shape, 0)
    other = jnp.where((lane == flag_lane(head)) & (position >= length), masked_score, 0.0)
    return jnp.where(head_lanes(keys.shape, 1, head), keys.astype(f32), other).astype(bf16)


def only_head(rows, head):
    return jnp.where(head_lanes(rows.shape, 1, head), rows.astype(f32), 0.0).astype(bf16)


def flagged(rows, head):
    lane = lax.broadcasted_iota(jnp.int32, rows.shape, 1)
    flag = jnp.where(lane == flag_lane(head), 1.0, 0.0)
    return jnp.where(head_lanes(rows.shape, 1, head), rows.astype(f32), flag).astype(bf16)


def bias_columns(bias_tile, first, count, key_tiles):
    parts = []
    for tile in range(key_tiles):
        start = aligned((key_tiles - 1 - tile) * LANES + first, LANES)
        parts.append(bias_tile[:, pl.ds(start, count)])
    return jnp.concatenate(parts, axis=0)


def attend_body(block, scal, q_ref, k_ref, v_ref, offsets_ref, out_ref, lse_ref, bias_tile):
    row0, length = scal[0], scal[1]
    rows, key_tiles = q_ref.shape[0], k_ref.shape[0] // LANES
    values_t = jnp.transpose(v_ref[...].astype(f32))
    outs = [[] for _ in range(rows // block)]
    for head in range(2):
        fill_bias(offsets_ref, head, bias_tile)
        keys = masked_keys(k_ref[...], head, length)
        values_h = jnp.where(head_lanes(values_t.shape, 0, head), values_t, 1.0).astype(bf16)
        for b in range(rows // block):
            rs = slice(b * block, (b + 1) * block)
            scores = dot_nt(keys, flagged(q_ref[rs, :], head))
            scores = scores + bias_columns(bias_tile, row0 + b * block, block, key_tiles)
            top = jnp.max(scores, axis=0, keepdims=True)
            weights = jnp.exp(scores - top).astype(bf16)
            mixed_t = dot(values_h, weights)
            total = mixed_t[flag_lane(head) : flag_lane(head) + 1]
            mine = mixed_t[:DH] if head == 0 else mixed_t[DH:]
            outs[b].append(mine / total)
            lse_ref[0, head : head + 1, rs] = top + jnp.log(total)
    for b in range(rows // block):
        joined = jnp.transpose(jnp.concatenate(outs[b], axis=0))
        out_ref[b * block : (b + 1) * block, :] = joined.astype(bf16)


def attend(scal, half, queries, keys, values, offsets):
    rows, width = queries.shape[1:]
    seq_len, pairs, span = keys.shape[0], width // PAIR, offsets.shape[2]
    block = min(256, rows)
    tokens_spec = pl.BlockSpec((rows, PAIR), lambda g, s: (0, g))
    keys_spec = pl.BlockSpec((seq_len, PAIR), lambda g, s: (0, g))
    work = rows * seq_len * width
    return pl.pallas_call(
        functools.partial(attend_body, block),
        out_shape=(
            jax.ShapeDtypeStruct((rows, width), bf16),
            jax.ShapeDtypeStruct((pairs, 2, rows), f32),
        ),
        grid_spec=pltpu.PrefetchScalarGridSpec(
            num_scalar_prefetch=1,
            grid=(pairs,),
            in_specs=[
                pl.BlockSpec((pl.Squeezed(), rows, PAIR), lambda g, s: (half, 0, g)),
                keys_spec,
                keys_spec,
                pl.BlockSpec((1, 2, span), lambda g, s: (g, 0, 0)),
            ],
            out_specs=[tokens_spec, pl.BlockSpec((1, 2, rows), lambda g, s: (g, 0, 0))],
            scratch_shapes=[pltpu.VMEM((LANES, span), f32)],
        ),
        compiler_params=pltpu.CompilerParams(vmem_limit_bytes=60 * MiB),
        cost_estimate=pl.CostEstimate(
            flops=16 * work, transcendentals=work // DH, bytes_accessed=4 * seq_len * width
        ),
        name="attend",
    )(scal, queries, keys, values, offsets)


def diagonal_sums(tile):
    span = tile.shape[1]
    size = tile.shape[0] // 2
    while size >= 8:
        tile = tile[:size] + pltpu.roll(tile[size:], span - size, 1)
        size //= 2
    row = lax.broadcasted_iota(jnp.int32, tile.shape, 0)
    for bit in (1, 2, 4):
        tile = jnp.where((row & bit) != 0, pltpu.roll(tile, span - bit, 1), tile)
    return jnp.sum(tile, axis=0, keepdims=True)


def attend_back_body(block, carry, scal, *refs):
    q_ref, k_ref, v_ref, g_ref, o_ref, lse_ref, offsets_ref = refs[:7]
    dq_ref, dk_ref, dv_ref, diag_ref, bias_tile, diag_tile, dk_sum, dv_sum = refs[-8:]
    row0, length = scal[0], scal[1]
    rows, key_tiles = q_ref.shape[0], k_ref.shape[0] // LANES
    if carry:
        dk_sum[...] = refs[7][...]
        dv_sum[...] = refs[8][...]
    else:
        dk_sum[...] = jnp.zeros_like(dk_sum)
        dv_sum[...] = jnp.zeros_like(dv_sum)
    keys_t = jnp.transpose(k_ref[...].astype(f32)).astype(bf16)
    count = rows // block
    dqs = [[] for _ in range(count)]
    deltas = []
    for b in range(count):
        rs = slice(b * block, (b + 1) * block)
        product = jnp.transpose(g_ref[rs, :].astype(f32) * o_ref[rs, :].astype(f32))
        deltas.append(
            (
                jnp.sum(product[:DH], axis=0, keepdims=True),
                jnp.sum(product[DH:], axis=0, keepdims=True),
            )
        )
    for head in range(2):
        fill_bias(offsets_ref, head, bias_tile)
        diag_tile[...] = jnp.zeros_like(diag_tile)
        keys = masked_keys(k_ref[...], head, length)
        for b in range(count):
            rs = slice(b * block, (b + 1) * block)
            queries = q_ref[rs, :]
            grads = only_head(g_ref[rs, :], head)
            scores = dot_nt(keys, flagged(queries, head))
            scores = scores + bias_columns(bias_tile, row0 + b * block, block, key_tiles)
            probs = jnp.exp(scores - lse_ref[0, head : head + 1, rs])
            grad_probs = dot_nt(v_ref[...], grads)
            grad_scores = probs * (grad_probs - deltas[b][head])
            for tile in range(key_tiles):
                start = aligned((key_tiles - 1 - tile) * LANES + row0 + b * block, LANES)
                diag_tile[:, pl.ds(start, block)] += grad_scores[tile * LANES : (tile + 1) * LANES]
            grad_scores = grad_scores.astype(bf16)
            dv_sum[...] += dot(probs.astype(bf16), grads)
            dk_sum[...] += dot(grad_scores, only_head(queries, head))
            dq_t = dot(keys_t, grad_scores)
            dqs[b].append(dq_t[:DH] if head == 0 else dq_t[DH:])
        diag_ref[0, head : head + 1, :] = diagonal_sums(diag_tile[...])
    for b in range(count):
        joined = jnp.transpose(jnp.concatenate(dqs[b], axis=0))
        dq_ref[b * block : (b + 1) * block, :] = joined.astype(bf16)
    dk_ref[...] = dk_sum[...].astype(dk_ref.dtype)
    dv_ref[...] = dv_sum[...].astype(dv_ref.dtype)


def attend_back(scal, half, queries, keys, values, grads, outs, lse, offsets, carry):
    rows, width = queries.shape[1:]
    seq_len, pairs, span = keys.shape[0], width // PAIR, offsets.shape[2]
    block = min(256, rows)
    rows_spec = pl.BlockSpec((rows, PAIR), lambda g, s: (0, g))
    keys_spec = pl.BlockSpec((seq_len, PAIR), lambda g, s: (0, g))
    offsets_spec = pl.BlockSpec((1, 2, span), lambda g, s: (g, 0, 0))
    specs = [
        pl.BlockSpec((pl.Squeezed(), rows, PAIR), lambda g, s: (half, 0, g)),
        keys_spec,
        keys_spec,
        rows_spec,
        rows_spec,
        pl.BlockSpec((1, 2, rows), lambda g, s: (g, 0, 0)),
        offsets_spec,
    ]
    kind = f32
    if carry:
        specs += [keys_spec, keys_spec]
        kind = bf16
    work = rows * seq_len * width
    return pl.pallas_call(
        functools.partial(attend_back_body, block, bool(carry)),
        out_shape=(
            jax.ShapeDtypeStruct((rows, width), bf16),
            jax.ShapeDtypeStruct((seq_len, width), kind),
            jax.ShapeDtypeStruct((seq_len, width), kind),
            jax.ShapeDtypeStruct(offsets.shape, f32),
        ),
        grid_spec=pltpu.PrefetchScalarGridSpec(
            num_scalar_prefetch=1,
            grid=(pairs,),
            in_specs=specs,
            out_specs=[rows_spec, keys_spec, keys_spec, offsets_spec],
            scratch_shapes=[
                pltpu.VMEM((LANES, span), f32),
                pltpu.VMEM((LANES, span), f32),
                pltpu.VMEM((seq_len, PAIR), f32),
                pltpu.VMEM((seq_len, PAIR), f32),
            ],
        ),
        compiler_params=pltpu.CompilerParams(vmem_limit_bytes=60 * MiB),
        cost_estimate=pl.CostEstimate(
            flops=40 * work, transcendentals=work // DH, bytes_accessed=12 * seq_len * width
        ),
        name="attend_back",
    )(scal, queries, keys, values, grads, outs, lse, offsets, *carry)


def normed_rows(values, gain_row):
    inverse = lax.rsqrt(jnp.mean(values * values, axis=-1, keepdims=True) + epsilon)
    return values * inverse * gain_row, inverse


def project_body(scal, own_ref, peer_ref, w0_ref, w1_ref, normed_ref, q_ref, k_ref, v_ref, w_ref, gain_ref):
    own_p = scal[2]
    side, step = pl.program_id(0), pl.program_id(1)
    rows, width = w0_ref.shape[1], q_ref.shape[1]

    @pl.when((side == 0) & (step == 0))
    def gather_weights():
        for core, piece in enumerate((w0_ref, w1_ref)):
            for high in range(BLOCKS // 2):
                part = ((high << 1) | core) ^ own_p
                start = aligned(part * rows, 16)
                w_ref[pl.ds(start, rows), :] = piece[high, :, : 3 * width]
                gain_ref[pl.ds(start, rows), :] = piece[high, :, 3 * width :].astype(f32)

    gain_row = jnp.transpose(gain_ref[...])[0:1, :]
    values = jnp.where(side == 0, own_ref[...].astype(f32), peer_ref[...].astype(f32))
    normed = normed_rows(values, gain_row)[0].astype(bf16)
    normed_ref[...] = normed
    made = dot(normed, w_ref[...]).astype(bf16)
    q_ref[...] = made[:, :width]
    k_ref[...] = made[:, width : 2 * width]
    v_ref[...] = made[:, 2 * width :]


def project(scal, own, peer, pieces, width):
    rows, depth = own.shape
    block = min(256, rows)
    steps = rows // block
    whole = pl.BlockSpec(pieces[0].shape, lambda h, b, s: (0, 0, 0))
    by_half = pl.BlockSpec((pl.Squeezed(), block, width), lambda h, b, s: (h, b, 0))
    by_place = pl.BlockSpec((pl.Squeezed(), block, width), lambda h, b, s: (h ^ s[3], b, 0))
    stacked = jax.ShapeDtypeStruct((2, rows, width), bf16)
    return pl.pallas_call(
        project_body,
        out_shape=(
            jax.ShapeDtypeStruct((2, rows, depth), bf16),
            stacked,
            stacked,
            stacked,
            jax.ShapeDtypeStruct((depth, 3 * width), bf16),
            jax.ShapeDtypeStruct((depth, LANES), f32),
        ),
        grid_spec=pltpu.PrefetchScalarGridSpec(
            num_scalar_prefetch=1,
            grid=(2, steps),
            in_specs=[
                pl.BlockSpec((block, depth), lambda h, b, s: (b * (1 - h) + (steps - 1) * h, 0)),
                pl.BlockSpec((block, depth), lambda h, b, s: (b * h, 0)),
                whole,
                whole,
            ],
            out_specs=[
                pl.BlockSpec((pl.Squeezed(), block, depth), lambda h, b, s: (h, b, 0)),
                by_half,
                by_place,
                by_place,
                pl.BlockSpec((depth, 3 * width), lambda h, b, s: (0, 0)),
                pl.BlockSpec((depth, LANES), lambda h, b, s: (0, 0)),
            ],
        ),
        compiler_params=pltpu.CompilerParams(vmem_limit_bytes=60 * MiB),
        cost_estimate=pl.CostEstimate(
            flops=12 * rows * depth * width, transcendentals=0, bytes_accessed=10 * rows * depth
        ),
        name="project",
    )(scal, own, peer, *pieces)


def gelu_parts(values):
    scale = 0.7978845608028654
    square = values * values
    bend = jnp.tanh(scale * (values + 0.044715 * (values * square)))
    half = 0.5 * (1.0 + bend)
    slope = half + (0.5 * scale) * values * (1.0 - bend * bend) * (1.0 + 0.134145 * square)
    return values * half, slope


def place_of(rel):
    return (((rel >> 2) & 1) << 1) | (rel & 1), rel >> 3


def assemble_rows(pieces, first_column, target, own_p, me):
    half = target.shape[1] // 2
    for core, piece in enumerate(pieces):
        shard = piece.shape[2]
        for plane in range(4):
            for level in range(4):
                part = ((level << 2) | ((plane >> 1) << 1) | core) ^ own_p
                row = aligned(part * shard, 16)
                column = aligned(((plane & 1) ^ me) * half, LANES)
                source = piece[plane, level, :, pl.ds(first_column, half)]
                target[pl.ds(row, shard), pl.ds(column, half)] = source


def feed_body(leading, direct, scal, *refs):
    refs = list(refs)
    take = lambda count: [refs.pop(0) for _ in range(count)]
    if leading:
        tok_ref, cot_ref, mine_ref, theirs_ref, gain_ref = take(5)
    else:
        rows_in, mid_in, nff_in, out_in, grad_in, mix_in, wo_in, gain_ref = take(8)
    if direct:
        wo_ref = take(1)[0] if leading else None
        wi_ref, *wb_refs = take(3)
    else:
        pieces = take(2)
    if leading:
        rows_s, mid_s, nff_s, out_s, nff_grad, mix_s, wo_s = take(7)
    else:
        out_ref, mid_grad_ref, mix_own_ref, mix_peer_ref, gain_grad_ref = take(5)
    keep_ref, send_ref = take(2)
    if not leading:
        rows_s, mid_s, nff_s, mix_s, wo_s = rows_in, mid_in, nff_in, mix_in, wo_in
        out_s, nff_grad = take(2)
    nff_t, wi_s, wb_s, total = take(4)
    row0, length, own_p, me = scal[0], scal[1], scal[2], scal[3]
    own_r = own_p * 2 + me
    step = pl.program_id(0)
    rows, depth = rows_s.shape
    half = depth // 2
    steps, skip = 2, 1 if leading else 0
    count = depth // (2 * BLOCKS)
    gain_row = jnp.transpose(gain_ref[...])[1:2, :]

    def store_rows(column):
        for rel in range(2 * BLOCKS):
            start = aligned((rel ^ own_r) * count, 8)
            plane, level = place_of(rel)
            target = send_ref if (rel >> 1) & 1 else keep_ref
            piece = total[pl.ds(start, count), :].astype(bf16)
            target[plane, level, :, pl.ds(column, depth)] = piece

    @pl.when(step == 0)
    def start():
        if leading:
            if direct:
                wo_s[...] = wo_ref[...]
            else:
                assemble_rows(pieces, 0, wo_s, own_p, me)
            mix_s[:, pl.ds(aligned(me * half, LANES), half)] = mine_ref[...]
            mix_s[:, pl.ds(aligned((1 - me) * half, LANES), half)] = theirs_ref[...]
            middle = tok_ref[...].astype(f32) + dot(mix_s[...], wo_s[...])
            mid_s[...] = middle
            nff_s[...] = normed_rows(middle, gain_row)[0].astype(bf16)
            position = row0 + lax.broadcasted_iota(jnp.int32, (rows, depth), 0)
            rows_s[...] = jnp.where(position < length, cot_ref[...].astype(f32), 0.0).astype(bf16)
            out_s[...] = middle
            nff_grad[...] = jnp.zeros_like(nff_grad)
        else:
            out_s[...] = out_in[...]
            nff_grad[...] = grad_in[...]
        nff_t[...] = jnp.transpose(nff_s[...].astype(f32)).astype(bf16)

    def hidden_block():
        shard = depth // BLOCKS
        if direct:
            wi_s[...] = wi_ref[...]
            for part in range(BLOCKS // 2):
                for side in range(2):
                    row = (2 * part + side) * shard
                    wb_s[row : row + shard, :] = wb_refs[side][part * shard : (part + 1) * shard, :]
        else:
            assemble_rows(pieces, aligned((skip + step) * half, LANES), wi_s, own_p, me)
            zone = (step ^ (own_p >> 3)) * 2
            for core, piece in enumerate(pieces):
                for plane in range(4):
                    for low in range(2):
                        part = ((low << 2) | ((plane >> 1) << 1) | core) ^ (own_p & 7)
                        column = aligned(((plane & 1) ^ me) * half, LANES)
                        for side in range(2):
                            column_in = (skip + 2 + side) * half
                            source = piece[plane, zone + low, :, column_in : column_in + half]
                            row = aligned((2 * part + side) * shard, 16)
                            wb_s[pl.ds(row, shard), pl.ds(column, half)] = source
        pre = dot(nff_s[...], wi_s[...])
        hidden, slope = gelu_parts(pre)
        hidden = hidden.astype(bf16)
        out_s[...] += dot(hidden, wb_s[...])
        pre_grad = (dot_nt(rows_s[...], wb_s[...]) * slope).astype(bf16)
        total[...] = dot_tn(hidden, rows_s[...])
        zone = (step ^ (own_p >> 3)) * 2
        for rel in range(BLOCKS):
            plane, low = place_of(rel)
            target = send_ref if (rel >> 1) & 1 else keep_ref
            for side in range(2):
                row = aligned((rel ^ (own_r & 15)) * (2 * count) + side * count, 8)
                piece = total[pl.ds(row, count), :].astype(bf16)
                column = (steps + side) * depth
                target[plane, zone + low, :, column : column + depth] = piece
        nff_grad[...] += dot_nt(pre_grad, wi_s[...])
        total[...] = dot(nff_t[...], pre_grad)
        store_rows(aligned(step * depth, LANES))

    if leading:
        hidden_block()
        return
    pl.when(step < steps)(hidden_block)

    @pl.when(step == steps)
    def finish():
        out_ref[...] = out_s[...].astype(bf16)
        middle = mid_s[...]
        inverse = lax.rsqrt(jnp.mean(middle * middle, axis=-1, keepdims=True) + epsilon)
        grads = nff_grad[...]
        gain_sum = jnp.sum(grads * middle * inverse, axis=0, keepdims=True)
        gain_grad_ref[...] = jnp.broadcast_to(gain_sum, gain_grad_ref.shape)
        scaled = grads * gain_row
        inner = jnp.sum(scaled * middle, axis=-1, keepdims=True)
        mid_grad = (
            rows_s[...].astype(f32)
            + inverse * scaled
            - middle * (inverse * inverse * inverse) * (inner / depth)
        )
        mid_grad_ref[...] = mid_grad
        attn_grad = mid_grad.astype(bf16)
        total[...] = dot_tn(mix_s[...], attn_grad)
        store_rows((steps + 2) * depth)
        turned = dot_nt(attn_grad, wo_s[...])
        first, second = turned[:, :half], turned[:, half:]
        mix_own_ref[...] = jnp.where(me == 0, first, second).astype(bf16)
        mix_peer_ref[...] = jnp.where(me == 0, second, first).astype(bf16)


def fixed(*shape):
    return pl.BlockSpec(shape, lambda *_: (0,) * len(shape))


def direct_specs(depth, skip):
    by_step = lambda f: jnp.minimum(f, 1)
    in_spec = pl.BlockSpec((depth, depth), lambda f, s: (0, by_step(f) + skip))
    low_spec = pl.BlockSpec((depth // 2, depth), lambda f, s: (by_step(f), 2 + skip))
    high_spec = pl.BlockSpec((depth // 2, depth), lambda f, s: (by_step(f), 3 + skip))
    return [fixed(depth, depth)] * skip + [in_spec, low_spec, high_spec]


def feed_call(leading, direct, scal, inputs, in_specs, outputs, chunk, scratch, name):
    rows, depth = outputs[0][0]
    count = depth // (2 * BLOCKS)
    sums = jax.ShapeDtypeStruct((4, 4, count, chunk * depth), bf16)
    return pl.pallas_call(
        functools.partial(feed_body, leading, direct),
        out_shape=[jax.ShapeDtypeStruct(*o) for o in outputs] + [sums] * 2,
        grid_spec=pltpu.PrefetchScalarGridSpec(
            num_scalar_prefetch=1,
            grid=(2 if leading else 3,),
            in_specs=in_specs,
            out_specs=[fixed(*o[0]) for o in outputs] + [fixed(*sums.shape)] * 2,
            scratch_shapes=scratch
            + [
                pltpu.VMEM((depth, rows), bf16),
                pltpu.VMEM((depth, depth), bf16),
                pltpu.VMEM((depth, depth), bf16),
                pltpu.VMEM((depth, depth), f32),
            ],
        ),
        compiler_params=pltpu.CompilerParams(vmem_limit_bytes=60 * MiB),
        cost_estimate=pl.CostEstimate(
            flops=24 * rows * depth * depth,
            transcendentals=2 * rows * depth,
            bytes_accessed=20 * MiB,
        ),
        name=name,
    )(scal, *inputs)


def feed_first(scal, tokens, cotangent, mine, theirs, gains, weights, direct):
    rows, depth = tokens.shape
    inputs = [tokens, cotangent, mine, theirs, gains]
    specs = [fixed(*v.shape) for v in inputs]
    if direct:
        inputs += [weights] * 4
        specs += direct_specs(depth, 1)
    else:
        inputs += weights
        specs += [fixed(*w.shape) for w in weights]
    whole = [(rows, depth)] * 6 + [(depth, depth)]
    outputs = list(zip(whole, [bf16, f32, bf16, f32, f32, bf16, bf16]))
    return feed_call(True, direct, scal, inputs, specs, outputs, 4, [], "feed_first")


def feed_second(scal, state, gains, weights, direct):
    rows, depth = state[0].shape
    half = depth // 2
    inputs = list(state) + [gains]
    specs = [fixed(*v.shape) for v in inputs]
    if direct:
        inputs += [weights] * 3
        specs += direct_specs(depth, 0)
    else:
        inputs += weights
        specs += [fixed(*w.shape) for w in weights]
    whole = [(rows, depth), (rows, depth), (rows, half), (rows, half), (8, depth)]
    outputs = list(zip(whole, [bf16, f32, bf16, bf16, f32]))
    scratch = [pltpu.VMEM((rows, depth), f32)] * 2
    return feed_call(False, direct, scal, inputs, specs, outputs, 5, scratch, "feed_second")


def project_back_body(
    scal, tok_ref, peer_ref, normed_ref, dq0_ref, dq1_ref, dk_ref, dv_ref, w_ref, gain_ref, ff_ref,
    table_ref, own_ref, send_ref, keep_ref, away_ref, total, gain_s, joined
):
    own_p = scal[2]
    side = pl.program_id(0)
    rows, width = dq0_ref.shape
    depth = tok_ref.shape[1]

    @pl.when(side == 0)
    def clear():
        total[...] = jnp.zeros_like(total)
        gain_s[...] = jnp.zeros_like(gain_s)
        gain_s[1:2, :] = ff_ref[0:1, :]
        joined[:, :width] = dq1_ref[...]

    @pl.when(side == 1)
    def swap():
        joined[:, :width] = dq0_ref[...]

    joined[:, width : 2 * width] = dk_ref[...]
    joined[:, 2 * width :] = dv_ref[...]
    grads = dot_nt(joined[...], w_ref[...])
    values = jnp.where(side == 0, peer_ref[...].astype(f32), tok_ref[...].astype(f32))
    inverse = lax.rsqrt(jnp.mean(values * values, axis=-1, keepdims=True) + epsilon)
    gain_s[0:1, :] += jnp.sum(grads * values * inverse, axis=0, keepdims=True)
    total[:, : 3 * width] += dot_tn(normed_ref[...], joined[...])

    @pl.when(side == 0)
    def outgoing():
        send_ref[...] = grads.astype(bf16)

    @pl.when(side == 1)
    def staying():
        own_ref[...] = grads
        gains = jnp.concatenate([gain_s[...], jnp.zeros((LANES - 8, depth), f32)], axis=0)
        total[:, 3 * width :] = jnp.transpose(gains)
        shard = depth // BLOCKS
        for rel in range(BLOCKS):
            start = aligned((rel ^ own_p) * shard, 16)
            target = away_ref if rel & 1 else keep_ref
            whole = jnp.concatenate(
                [
                    total[pl.ds(start, shard), : 3 * width],
                    total[pl.ds(start, shard), 3 * width :] + table_ref[...],
                ],
                axis=1,
            )
            target[(rel >> 1) & 1, rel >> 2] = whole.astype(bf16)


def project_back(
    scal, tokens, peer, normed, dq_own, dq_peer, dk, dv, weights, gains, ff_gain, table
):
    rows, depth = tokens.shape
    width = dq_own.shape[1]
    wide = 3 * width + LANES
    shard = depth // BLOCKS
    place = pl.BlockSpec((rows, width), lambda h, s: (1 - h ^ s[3], 0))
    blocks = jax.ShapeDtypeStruct((2, 4, shard, wide), bf16)
    return pl.pallas_call(
        project_back_body,
        out_shape=(
            jax.ShapeDtypeStruct((rows, depth), f32),
            jax.ShapeDtypeStruct((rows, depth), bf16),
            blocks,
            blocks,
        ),
        grid_spec=pltpu.PrefetchScalarGridSpec(
            num_scalar_prefetch=1,
            grid=(2,),
            in_specs=[
                fixed(rows, depth),
                fixed(rows, depth),
                pl.BlockSpec((pl.Squeezed(), rows, depth), lambda h, s: (1 - h, 0, 0)),
                fixed(rows, width),
                fixed(rows, width),
                place,
                place,
                fixed(depth, 3 * width),
                fixed(depth, LANES),
                fixed(8, depth),
                fixed(shard, LANES),
            ],
            out_specs=[
                fixed(rows, depth),
                fixed(rows, depth),
                fixed(2, 4, shard, wide),
                fixed(2, 4, shard, wide),
            ],
            scratch_shapes=[
                pltpu.VMEM((depth, wide), f32),
                pltpu.VMEM((8, depth), f32),
                pltpu.VMEM((rows, 3 * width), bf16),
            ],
        ),
        compiler_params=pltpu.CompilerParams(vmem_limit_bytes=60 * MiB),
        cost_estimate=pl.CostEstimate(
            flops=24 * rows * depth * width, transcendentals=0, bytes_accessed=16 * MiB
        ),
        name="project_back",
    )(scal, tokens, peer, normed, dq_own, dq_peer, dk, dv, weights, gains, ff_gain, table)


def last_body(tok_ref, mid_ref, own_ref, come_ref, gain_ref, out_ref):
    depth = tok_ref.shape[1]
    gain_row = jnp.transpose(gain_ref[...])[0:1, :]
    values = tok_ref[...].astype(f32)
    inverse = lax.rsqrt(jnp.mean(values * values, axis=-1, keepdims=True) + epsilon)
    scaled = (own_ref[...] + come_ref[...].astype(f32)) * gain_row
    inner = jnp.sum(scaled * values, axis=-1, keepdims=True)
    grads = inverse * scaled - values * (inverse * inverse * inverse) * (inner / depth)
    out_ref[...] = (mid_ref[...] + grads).astype(bf16)


def last(tokens, mid_grad, own, come, gains):
    rows, depth = tokens.shape
    block = min(128, rows)
    spec = pl.BlockSpec((block, depth), lambda b: (b, 0))
    return pl.pallas_call(
        last_body,
        out_shape=jax.ShapeDtypeStruct((rows, depth), bf16),
        grid=(rows // block,),
        in_specs=[spec, spec, spec, spec, pl.BlockSpec((depth, LANES), lambda b: (0, 0))],
        out_specs=spec,
        compiler_params=pltpu.CompilerParams(vmem_limit_bytes=60 * MiB),
        cost_estimate=pl.CostEstimate(
            flops=16 * rows * depth, transcendentals=0, bytes_accessed=12 * rows * depth
        ),
        name="last",
    )(tokens, mid_grad, own, come, gains)


def chosen(me, low, high):
    return jnp.where(me == 0, low.astype(f32), high.astype(f32)).astype(low.dtype)


def column_of(row):
    count = row.shape[1]
    square = lax.broadcasted_iota(jnp.int32, (count, count), 0)
    other = lax.broadcasted_iota(jnp.int32, (count, count), 1)
    return jnp.sum(jnp.where(square == other, row.astype(f32), 0.0), axis=1, keepdims=True)


def ready_first_body(scal, q_ref, k_ref, v_ref, attn_ref, ff_ref, out_ref):
    me = scal[3]
    width = q_ref.shape[1] // 2
    for i, ref in enumerate((q_ref, k_ref, v_ref)):
        half = chosen(me, ref[:, :width], ref[:, width:])
        out_ref[:, i * width : (i + 1) * width] = half
    lane = lax.broadcasted_iota(jnp.int32, (q_ref.shape[0], LANES), 1)
    gains = jnp.where(lane == 0, column_of(attn_ref[...]), 0.0)
    gains = jnp.where(lane == 1, column_of(ff_ref[...]), gains)
    out_ref[:, 3 * width :] = gains.astype(bf16)


def ready_first(scal, w_query, w_key, w_value, gain_attn, gain_ff):
    rows, depth = w_query.shape
    inputs = [w_query, w_key, w_value, gain_attn[None], gain_ff[None]]
    shape = (rows, 3 * (depth // 2) + LANES)
    return pl.pallas_call(
        ready_first_body,
        out_shape=jax.ShapeDtypeStruct(shape, bf16),
        grid_spec=pltpu.PrefetchScalarGridSpec(
            num_scalar_prefetch=1,
            grid=(1,),
            in_specs=[fixed(*v.shape) for v in inputs],
            out_specs=fixed(*shape),
        ),
        compiler_params=pltpu.CompilerParams(vmem_limit_bytes=60 * MiB),
        name="ready_first",
    )(scal, *inputs)


def ready_rest_body(scal, out_ref, in_ref, back_ref, one_ref, two_ref):
    me = scal[3]
    depth = out_ref.shape[1]
    half = depth // 2
    shard = back_ref.shape[0] // 4
    columns = in_ref[...].astype(f32)
    step = columns.shape[1] // (4 * BLOCKS)
    chunks = []
    for chunk in range(2):
        pieces = [columns[:, (2 * r + chunk) * step : (2 * r + chunk + 1) * step] for r in range(2 * BLOCKS)]
        chunks.append(jnp.concatenate(pieces, axis=1).astype(bf16))
    one_ref[:, :half] = chosen(me, out_ref[:, :half], out_ref[:, half:])
    for f in range(2):
        block = chunks[0][:, f * depth : (f + 1) * depth]
        one_ref[:, (f + 1) * half : (f + 2) * half] = chosen(me, block[:, :half], block[:, half:])
        block = chunks[1][:, f * depth : (f + 1) * depth]
        two_ref[:, f * half : (f + 1) * half] = chosen(me, block[:, :half], block[:, half:])
    for side in range(2):
        rows = back_ref[2 * side * shard : (2 * side + 1) * shard, :]
        one_ref[:, (side + 3) * half : (side + 4) * half] = chosen(me, rows[:, :half], rows[:, half:])
        rows = back_ref[(2 * side + 1) * shard : (2 * side + 2) * shard, :]
        two_ref[:, (side + 2) * half : (side + 3) * half] = chosen(me, rows[:, :half], rows[:, half:])


def ready_rest(scal, w_out, w_in, w_back):
    rows, depth = w_out.shape
    inputs = [w_out, w_in, w_back]
    shapes = [(rows, 5 * depth // 2), (rows, 2 * depth)]
    return pl.pallas_call(
        ready_rest_body,
        out_shape=[jax.ShapeDtypeStruct(s, bf16) for s in shapes],
        grid_spec=pltpu.PrefetchScalarGridSpec(
            num_scalar_prefetch=1,
            grid=(1,),
            in_specs=[fixed(*v.shape) for v in inputs],
            out_specs=[fixed(*s) for s in shapes],
        ),
        compiler_params=pltpu.CompilerParams(vmem_limit_bytes=60 * MiB),
        name="ready_rest",
    )(scal, *inputs)


def summed_refs(refs, start, stop):
    total = refs[0][:, start:stop].astype(f32)
    for ref in refs[1:]:
        total = total + ref[:, start:stop].astype(f32)
    return total


def place_grads_body(count_one, *refs):
    one_refs, two_refs = refs[:count_one], refs[count_one:-3]
    in_ref, back_ref, out_ref = refs[-3:]
    rows, depth = out_ref.shape
    parts = [summed_refs(r, 0, 2 * depth) for r in (one_refs, two_refs)]
    step = 2 * depth // (2 * BLOCKS)
    pieces = []
    for r in range(2 * BLOCKS):
        for part in parts:
            pieces.append(part[:, r * step : (r + 1) * step])
    in_ref[...] = jnp.concatenate(pieces, axis=1)
    for chunk, r in enumerate((one_refs, two_refs)):
        for side in range(2):
            row = (2 * chunk + side) * rows
            back_ref[row : row + rows, :] = summed_refs(r, (2 + side) * depth, (3 + side) * depth)
    out_ref[...] = summed_refs(two_refs, 4 * depth, 5 * depth)


def place_grads(one_parts, two_parts, depth):
    rows = one_parts[0].shape[0]
    inputs = one_parts + two_parts
    shapes = [(rows, 4 * depth), (4 * rows, depth), (rows, depth)]
    return pl.pallas_call(
        functools.partial(place_grads_body, len(one_parts)),
        out_shape=[jax.ShapeDtypeStruct(s, f32) for s in shapes],
        grid=(1,),
        in_specs=[fixed(*v.shape) for v in inputs],
        out_specs=[fixed(*s) for s in shapes],
        compiler_params=pltpu.CompilerParams(vmem_limit_bytes=60 * MiB),
        name="place_grads",
    )(*inputs)


def halve_first_body(scal, *refs):
    me = scal[3]
    parts, (mine_ref, theirs_ref, table_ref) = refs[:-3], refs[-3:]
    total = summed_refs(parts, 0, parts[0].shape[1])
    rows = total.shape[0] // 2
    mine_ref[...] = jnp.where(me == 0, total[:rows], total[rows:])
    theirs_ref[...] = jnp.where(me == 0, total[rows:], total[:rows])
    table_ref[...] = total[:, -LANES:]


def halve_first(scal, parts):
    rows, wide = parts[0].shape
    shapes = [(rows // 2, wide), (rows // 2, wide), (rows, LANES)]
    return pl.pallas_call(
        halve_first_body,
        out_shape=[jax.ShapeDtypeStruct(s, f32) for s in shapes],
        grid_spec=pltpu.PrefetchScalarGridSpec(
            num_scalar_prefetch=1,
            grid=(1,),
            in_specs=[fixed(*v.shape) for v in parts],
            out_specs=[fixed(*s) for s in shapes],
        ),
        compiler_params=pltpu.CompilerParams(vmem_limit_bytes=60 * MiB),
        name="halve_first",
    )(scal, *parts)


def place_first_body(scal, mine_ref, theirs_ref, *out_refs):
    me = scal[3]
    width = out_refs[0].shape[1] // 2
    for i, ref in enumerate(out_refs[:3]):
        mine = mine_ref[:, i * width : (i + 1) * width]
        theirs = theirs_ref[:, i * width : (i + 1) * width]
        ref[:, :width] = jnp.where(me == 0, mine, theirs)
        ref[:, width:] = jnp.where(me == 0, theirs, mine)
    out_refs[3][...] = mine_ref[:, 3 * width :] + theirs_ref[:, 3 * width :]


def place_first(scal, mine, theirs):
    rows, wide = mine.shape
    depth = (wide - LANES) // 3 * 2
    shapes = [(rows, depth)] * 3 + [(rows, LANES)]
    return pl.pallas_call(
        place_first_body,
        out_shape=[jax.ShapeDtypeStruct(s, f32) for s in shapes],
        grid_spec=pltpu.PrefetchScalarGridSpec(
            num_scalar_prefetch=1,
            grid=(1,),
            in_specs=[fixed(*mine.shape)] * 2,
            out_specs=[fixed(*s) for s in shapes],
        ),
        compiler_params=pltpu.CompilerParams(vmem_limit_bytes=60 * MiB),
        name="place_first",
    )(scal, mine, theirs)


def hop(value, mask):
    size = lax.axis_size("dp") * 2
    return lax.ppermute(value, ("dp", "seq"), [(i, i ^ mask) for i in range(size)])


def tied(*values):
    return lax.optimization_barrier(values)


LEVELS = (8, 16, 24)
PLANES = (1, 4, 5)
CORE = 2


def spread(value, masks):
    return [hop(value, mask) for mask in masks]


def total_of(parts, kind):
    total = parts[0].astype(f32)
    for part in parts[1:]:
        total = total + part.astype(f32)
    return total.astype(kind)


def scatter_sums(parts, masks):
    sums = [total_of([p[i] for p in parts], bf16) for i in range(len(masks) + 1)]
    return sums[0], [hop(s, m) for s, m in zip(sums[1:], masks)]


def whole_gather(shard):
    return lax.all_gather(shard, "dp", axis=0, tiled=True)


def join_grid(keep, send, axes):
    both = jnp.stack([keep, send])
    both = both.reshape((2,) * (len(axes) + 1) + both.shape[-2:])
    axes = ("c",) + axes
    order = ("z2", "z1", "y", "c") + (("x",) if "x" in axes else ())
    both = both.transpose([axes.index(n) for n in order] + [both.ndim - 2, both.ndim - 1])
    if "x" in axes:
        both = jnp.where(lax.axis_index("seq") == 1, jnp.flip(both, 4), both)
    return both.astype(f32)


def chunk_columns(weight, chunk):
    rows, hidden = weight.shape
    grid = weight.reshape(rows, BLOCKS * 2, 2, hidden // (4 * BLOCKS))
    return grid[:, :, chunk].reshape(rows, hidden // 2)


def chunk_rows(weight, chunk, shards):
    rows, depth = weight.shape
    grid = weight.reshape(shards, 2, 2, rows // (4 * shards), depth)[:, :, chunk]
    return [grid[:, side].reshape(-1, depth) for side in range(2)]


def halves(sums, depth):
    low, high = sums[..., 2 * depth : 3 * depth], sums[..., 3 * depth : 4 * depth]
    return sums[..., : 2 * depth], jnp.stack([low, high], -3)


def local(
    tokens,
    cotangent,
    lengths,
    rel_bucket,
    gain_attn,
    w_query,
    w_key,
    w_value,
    w_out,
    gain_ff,
    w_in,
    w_back,
    bias_table,
):
    place, me = lax.axis_index("dp"), lax.axis_index("seq")
    own, cot = tokens[0], cotangent[0]
    rows, depth = own.shape
    seq_len = rows * 2
    width = depth // 2
    near = lax.axis_size("dp") == BLOCKS
    length = lengths[0]
    part = place if near else jnp.int32(0)
    info = jnp.stack([me * rows, length, part, me]).astype(jnp.int32)
    far_info = jnp.stack([(1 - me) * rows, length, part, me]).astype(jnp.int32)

    if near:
        first = ready_first(info, w_query, w_key, w_value, gain_attn, gain_ff)
        come = spread(first, LEVELS)
    peer = hop(own, 1)

    padded = jnp.pad(rel_bucket, (0, 1), constant_values=-1)[::-1]
    padded = jnp.concatenate([padded[LANES:], padded[:LANES]])
    choice = jnp.arange(bias_table.shape[0], dtype=jnp.int32)[:, None] == padded[None, :]
    choice = choice.astype(f32)
    offsets = lax.dot_general(bias_table, choice, TN, precision=precise)
    offsets = offsets.reshape(-1, 2, 2 * seq_len)

    if near:
        one, two = ready_rest(info, w_out, w_in, w_back)
        first, come, one, two = tied(first, come, one, two)
        first = jnp.stack([first] + come)
        come = hop(first, 4)
        one_come = spread(one, LEVELS)
        first, come, peer, one, one_come, two = tied(first, come, peer, one, one_come, two)
        first = jnp.stack([first, come], axis=1)
        first = first.reshape((BLOCKS // 2,) + first.shape[2:])
        first = [first, hop(first, CORE)]
        one = jnp.stack([one] + one_come)
        one_come = spread(one, PLANES)
        two_come = hop(two, LEVELS[1])
    else:
        columns = [w_query, w_key, w_value]
        columns = [lax.dynamic_slice_in_dim(w, me * width, width, 1) for w in columns]
        gains = jnp.pad(jnp.stack([gain_attn, gain_ff], axis=1), ((0, 0), (0, LANES - 2)))
        first = whole_gather(jnp.concatenate(columns + [gains], axis=1))
        first = first.reshape(BLOCKS // 2, 2, -1, first.shape[1])
        first = [first[:, 0], first[:, 1]]
        in_all, back_all = whole_gather(w_in), whole_gather(w_back)
        one = [whole_gather(w_out), chunk_columns(in_all, 0)] + chunk_rows(back_all, 0, BLOCKS)
        one = jnp.concatenate(one, axis=1)
        two = jnp.concatenate([chunk_columns(in_all, 1)] + chunk_rows(back_all, 1, BLOCKS), axis=1)

    normed, query, keys, values, weights, gain_cols = project(info, own, peer, first, width)
    keys, values = keys.reshape(seq_len, width), values.reshape(seq_len, width)
    if near:
        query, two, two_come = tied(query, two, two_come)
        two = jnp.stack([two, two_come])
        two_come = hop(two, LEVELS[0])
        query, two = tied(query, two)
    far_out, far_lse = attend(far_info, 1, query, keys, values, offsets)
    theirs = hop(far_out, 1)
    query, far_lse = tied(query, far_lse)
    if near:
        query, two, two_come = tied(query, two, two_come)
        two = jnp.stack([two, two_come], axis=1)
        two = two.reshape((4,) + two.shape[2:])
        two_come = hop(two, 1)
        query, two = tied(query, two)
    near_out, near_lse = attend(info, 0, query, keys, values, offsets)
    if near:
        near_out, one, one_come, theirs, two, two_come = tied(
            near_out, one, one_come, theirs, two, two_come
        )
        one = jnp.stack([one] + one_come)
        one_come = hop(one, CORE)
        two, one = tied(two, one)
        two = jnp.stack([two, two_come])
        two_come = hop(two, 4)
        one, two = tied(one, two)
        one = [one, one_come]
    made = feed_first(info, own, cot, near_out, theirs, gain_cols, one, not near)
    state, keep_one, send_one = made[:7], made[7], made[8]
    if near:
        come = hop(send_one, CORE)
        keep_one, two, two_come = tied(keep_one, two, two_come)
        two = jnp.stack([two, two_come])
        two = two.reshape((4,) + two.shape[2:])
        two_come = hop(two, CORE)
        keep_one, two = tied(keep_one, two)
        keep_one, come_one = scatter_sums([keep_one, come], PLANES)
        state, keep_one = tied(state, keep_one)
        two = [two, two_come]
    made = feed_second(info, state, gain_cols, two, not near)
    result, mid_grad, mix_own, mix_peer, ff_gain, keep_two, send_two = made
    if near:
        keep_one, come_one, mix_peer, send_two = tied(keep_one, come_one, mix_peer, send_two)
        sums = [total_of([p[i] for p in [keep_one] + come_one], bf16) for i in range(4)]
        keep_one, away = jnp.stack([sums[0], sums[2]]), jnp.stack([sums[1], sums[3]])
        come_one = hop(away, LEVELS[0])
    far_grads = hop(mix_peer, 1)
    if near:
        come_two = hop(send_two, CORE)
        keep_one, keep_two, come_two = tied(keep_one, keep_two, come_two)
        keep_two, come_two = scatter_sums([keep_two, come_two], PLANES)
        mix_own, keep_one, keep_two = tied(mix_own, keep_one, keep_two)
    dq_own, dk, dv, diag_own = attend_back(
        info, 0, query, keys, values, mix_own, near_out, near_lse, offsets, ()
    )
    if near:
        dk, keep_one, come_one, far_grads = tied(dk, keep_one, come_one, far_grads)
        keep_one, come_one = scatter_sums([keep_one, come_one], LEVELS[1:2])
        dk, keep_one = tied(dk, keep_one)
    dq_peer, dk, dv, diag_peer = attend_back(
        far_info, 1, query, keys, values, far_grads, far_out, far_lse, offsets, (dk, dv)
    )
    if near:
        dk, keep_one, come_one, keep_two, come_two = tied(dk, keep_one, come_one, keep_two, come_two)
        keep_two, come_two = scatter_sums([keep_two] + come_two, LEVELS)
        dk, keep_two = tied(dk, keep_two)
    diag = (diag_own + diag_peer).reshape(-1, 2 * seq_len)
    table = lax.dot_general(choice, diag, NT, precision=precise)
    buckets, heads = table.shape
    shard = depth // BLOCKS
    table = jnp.pad(table, ((0, shard - buckets), (2, LANES - 2 - heads)))
    stay, leave, w_keep, w_send = project_back(
        info, own, peer, normed, dq_own, dq_peer, dk, dv, weights, gain_cols, ff_gain, table
    )
    come = hop(leave, 1)
    if near:
        w_come = hop(w_send, CORE)
        w_keep, w_come, keep_two, come_two = tied(w_keep, w_come, keep_two, come_two)
        w_keep, w_come = scatter_sums([w_keep, w_come], (4,))
        stay, come, w_keep = tied(stay, come, w_keep)
    grad_tokens = last(own, mid_grad, stay, come, gain_cols)
    if near:
        w_keep, w_come, grad_tokens = tied(w_keep, w_come, grad_tokens)
        w_keep, w_come = scatter_sums([w_keep] + w_come, LEVELS)
        keep_two, come_two, w_keep = tied(keep_two, come_two, w_keep)
        grad_in, grad_back, grad_out = place_grads([keep_one] + come_one, [keep_two] + come_two, depth)
        mine, theirs, table = halve_first(info, [w_keep] + w_come)
    else:
        scatter = functools.partial(lax.psum_scatter, scatter_dimension=0, tiled=True)
        both = ("dp", "seq")
        axes = ("y", "x", "z2", "z1")
        one_sum, two_sum = join_grid(keep_one, send_one, axes), join_grid(keep_two, send_two, axes)
        grad_first = join_grid(w_keep, w_send, ("y", "z2", "z1")).reshape(depth, -1)
        table = lax.psum(grad_first[:shard], "dp")
        table = table[:, -LANES:]
        grad_first = scatter(grad_first, "dp")
        in_one, back_one = halves(one_sum, depth)
        in_two, back_two = halves(two_sum, depth)
        grad_in = jnp.stack([in_one, in_two], axis=-2)
        grad_in = grad_in.reshape(-1, 2, 2 * BLOCKS, depth // BLOCKS).transpose(0, 2, 1, 3)
        grad_in = scatter(grad_in.reshape(-1, 4 * depth), both)
        grad_back = jnp.stack([back_one, back_two], axis=-4).reshape(-1, depth)
        grad_back = scatter(grad_back, both)
        grad_out = scatter(two_sum[..., 4 * depth :].reshape(-1, depth), both)
        count = grad_first.shape[0] // 2
        mine = lax.dynamic_slice_in_dim(grad_first, me * count, count, 0)
        theirs = lax.dynamic_slice_in_dim(grad_first, (1 - me) * count, count, 0)

    *full, gain_sums = place_first(info, mine, hop(theirs, 1))
    return (
        result[None],
        grad_tokens[None],
        gain_sums[:, 0],
        full[0],
        full[1],
        full[2],
        grad_out,
        gain_sums[:, 1],
        grad_in,
        grad_back,
        table[:buckets, 2 : 2 + heads],
    )


def solution(mesh):
    return jax.shard_map(
        local,
        mesh=mesh,
        in_specs=(
            P("dp", "seq", None),
            P("dp", "seq", None),
            P("dp"),
            P(),
            P("dp"),
            P("dp", None),
            P("dp", None),
            P("dp", None),
            P("dp", None),
            P("dp"),
            P("dp", None),
            P("dp", None),
            P(None, "seq"),
        ),
        out_specs=(
            P("dp", "seq", None),
            P("dp", "seq", None),
            P(("dp", "seq")),
            P(("dp", "seq"), None),
            P(("dp", "seq"), None),
            P(("dp", "seq"), None),
            P(("dp", "seq"), None),
            P(("dp", "seq")),
            P(("dp", "seq"), None),
            P(("dp", "seq"), None),
            P(None, "seq"),
        ),
        check_vma=False,
    )
```

```python
import functools

import jax
import jax.numpy as jnp
from jax import lax
from jax.experimental import pallas as pl
from jax.experimental.pallas import tpu as pltpu
from jax.sharding import PartitionSpec as P

DH = 64
PAIR = 2 * DH
LANES = 128
BLOCKS = 16
NT = (((1,), (1,)), ((), ()))
TN = (((0,), (0,)), ((), ()))
epsilon = 1e-06
masked_score = -1e30
precise = lax.Precision.HIGHEST
f32 = jnp.float32
bf16 = jnp.bfloat16
MiB = 2**20


def dot(a, b):
    return jnp.dot(a, b, preferred_element_type=f32)


def dot_nt(a, b):
    return lax.dot_general(a, b, NT, preferred_element_type=f32)


def dot_tn(a, b):
    return lax.dot_general(a, b, TN, preferred_element_type=f32)


def aligned(value, unit):
    return pl.multiple_of(value, unit)


def head_lanes(shape, dim, head):
    index = lax.broadcasted_iota(jnp.int32, shape, dim)
    return (index < DH) if head == 0 else (index >= DH)


def flag_lane(head):
    return DH if head == 0 else 0


def fill_bias(offsets_ref, head, bias_tile):
    row = jnp.broadcast_to(offsets_ref[0, head : head + 1, :], bias_tile.shape)
    bias_tile[...] = pltpu.roll(row, 0, 1, stride=1, stride_axis=0)


def masked_keys(keys, head, length):
    lane = lax.broadcasted_iota(jnp.int32, keys.shape, 1)
    position = lax.broadcasted_iota(jnp.int32, keys.shape, 0)
    other = jnp.where((lane == flag_lane(head)) & (position >= length), masked_score, 0.0)
    return jnp.where(head_lanes(keys.shape, 1, head), keys.astype(f32), other).astype(bf16)


def only_head(rows, head):
    return jnp.where(head_lanes(rows.shape, 1, head), rows.astype(f32), 0.0).astype(bf16)


def flagged(rows, head):
    lane = lax.broadcasted_iota(jnp.int32, rows.shape, 1)
    flag = jnp.where(lane == flag_lane(head), 1.0, 0.0)
    return jnp.where(head_lanes(rows.shape, 1, head), rows.astype(f32), flag).astype(bf16)


def bias_columns(bias_tile, first, count, key_tiles):
    parts = []
    for tile in range(key_tiles):
        start = aligned((key_tiles - 1 - tile) * LANES + first, LANES)
        parts.append(bias_tile[:, pl.ds(start, count)])
    return jnp.concatenate(parts, axis=0)


def attend_body(block, scal, q_ref, k_ref, v_ref, offsets_ref, out_ref, lse_ref, bias_tile):
    row0, length = scal[0], scal[1]
    rows, key_tiles = q_ref.shape[0], k_ref.shape[0] // LANES
    values_t = jnp.transpose(v_ref[...].astype(f32))
    outs = [[] for _ in range(rows // block)]
    for head in range(2):
        fill_bias(offsets_ref, head, bias_tile)
        keys = masked_keys(k_ref[...], head, length)
        values_h = jnp.where(head_lanes(values_t.shape, 0, head), values_t, 1.0).astype(bf16)
        for b in range(rows // block):
            rs = slice(b * block, (b + 1) * block)
            scores = dot_nt(keys, flagged(q_ref[rs, :], head))
            scores = scores + bias_columns(bias_tile, row0 + b * block, block, key_tiles)
            top = jnp.max(scores, axis=0, keepdims=True)
            weights = jnp.exp(scores - top).astype(bf16)
            mixed_t = dot(values_h, weights)
            total = mixed_t[flag_lane(head) : flag_lane(head) + 1]
            mine = mixed_t[:DH] if head == 0 else mixed_t[DH:]
            outs[b].append(mine / total)
            lse_ref[0, head : head + 1, rs] = top + jnp.log(total)
    for b in range(rows // block):
        joined = jnp.transpose(jnp.concatenate(outs[b], axis=0))
        out_ref[b * block : (b + 1) * block, :] = joined.astype(bf16)


def attend(scal, half, queries, keys, values, offsets):
    rows, width = queries.shape[1:]
    seq_len, pairs, span = keys.shape[0], width // PAIR, offsets.shape[2]
    block = min(256, rows)
    tokens_spec = pl.BlockSpec((rows, PAIR), lambda g, s: (0, g))
    keys_spec = pl.BlockSpec((seq_len, PAIR), lambda g, s: (0, g))
    work = rows * seq_len * width
    return pl.pallas_call(
        functools.partial(attend_body, block),
        out_shape=(
            jax.ShapeDtypeStruct((rows, width), bf16),
            jax.ShapeDtypeStruct((pairs, 2, rows), f32),
        ),
        grid_spec=pltpu.PrefetchScalarGridSpec(
            num_scalar_prefetch=1,
            grid=(pairs,),
            in_specs=[
                pl.BlockSpec((pl.Squeezed(), rows, PAIR), lambda g, s: (half, 0, g)),
                keys_spec,
                keys_spec,
                pl.BlockSpec((1, 2, span), lambda g, s: (g, 0, 0)),
            ],
            out_specs=[tokens_spec, pl.BlockSpec((1, 2, rows), lambda g, s: (g, 0, 0))],
            scratch_shapes=[pltpu.VMEM((LANES, span), f32)],
        ),
        compiler_params=pltpu.CompilerParams(vmem_limit_bytes=60 * MiB),
        cost_estimate=pl.CostEstimate(
            flops=16 * work, transcendentals=work // DH, bytes_accessed=4 * seq_len * width
        ),
        name="attend",
    )(scal, queries, keys, values, offsets)


def diagonal_sums(tile):
    span = tile.shape[1]
    size = tile.shape[0] // 2
    while size >= 8:
        tile = tile[:size] + pltpu.roll(tile[size:], span - size, 1)
        size //= 2
    row = lax.broadcasted_iota(jnp.int32, tile.shape, 0)
    for bit in (1, 2, 4):
        tile = jnp.where((row & bit) != 0, pltpu.roll(tile, span - bit, 1), tile)
    return jnp.sum(tile, axis=0, keepdims=True)


def attend_back_body(block, carry, scal, *refs):
    q_ref, k_ref, v_ref, g_ref, o_ref, lse_ref, offsets_ref = refs[:7]
    dq_ref, dk_ref, dv_ref, diag_ref, bias_tile, diag_tile, dk_sum, dv_sum = refs[-8:]
    row0, length = scal[0], scal[1]
    rows, key_tiles = q_ref.shape[0], k_ref.shape[0] // LANES
    if carry:
        dk_sum[...] = refs[7][...]
        dv_sum[...] = refs[8][...]
    else:
        dk_sum[...] = jnp.zeros_like(dk_sum)
        dv_sum[...] = jnp.zeros_like(dv_sum)
    keys_t = jnp.transpose(k_ref[...].astype(f32)).astype(bf16)
    count = rows // block
    dqs = [[] for _ in range(count)]
    deltas = []
    for b in range(count):
        rs = slice(b * block, (b + 1) * block)
        product = jnp.transpose(g_ref[rs, :].astype(f32) * o_ref[rs, :].astype(f32))
        deltas.append(
            (
                jnp.sum(product[:DH], axis=0, keepdims=True),
                jnp.sum(product[DH:], axis=0, keepdims=True),
            )
        )
    for head in range(2):
        fill_bias(offsets_ref, head, bias_tile)
        diag_tile[...] = jnp.zeros_like(diag_tile)
        keys = masked_keys(k_ref[...], head, length)
        for b in range(count):
            rs = slice(b * block, (b + 1) * block)
            queries = q_ref[rs, :]
            grads = only_head(g_ref[rs, :], head)
            scores = dot_nt(keys, flagged(queries, head))
            scores = scores + bias_columns(bias_tile, row0 + b * block, block, key_tiles)
            probs = jnp.exp(scores - lse_ref[0, head : head + 1, rs])
            grad_probs = dot_nt(v_ref[...], grads)
            grad_scores = probs * (grad_probs - deltas[b][head])
            for tile in range(key_tiles):
                start = aligned((key_tiles - 1 - tile) * LANES + row0 + b * block, LANES)
                diag_tile[:, pl.ds(start, block)] += grad_scores[tile * LANES : (tile + 1) * LANES]
            grad_scores = grad_scores.astype(bf16)
            dv_sum[...] += dot(probs.astype(bf16), grads)
            dk_sum[...] += dot(grad_scores, only_head(queries, head))
            dq_t = dot(keys_t, grad_scores)
            dqs[b].append(dq_t[:DH] if head == 0 else dq_t[DH:])
        diag_ref[0, head : head + 1, :] = diagonal_sums(diag_tile[...])
    for b in range(count):
        joined = jnp.transpose(jnp.concatenate(dqs[b], axis=0))
        dq_ref[b * block : (b + 1) * block, :] = joined.astype(bf16)
    dk_ref[...] = dk_sum[...].astype(dk_ref.dtype)
    dv_ref[...] = dv_sum[...].astype(dv_ref.dtype)


def attend_back(scal, half, queries, keys, values, grads, outs, lse, offsets, carry):
    rows, width = queries.shape[1:]
    seq_len, pairs, span = keys.shape[0], width // PAIR, offsets.shape[2]
    block = min(256, rows)
    rows_spec = pl.BlockSpec((rows, PAIR), lambda g, s: (0, g))
    keys_spec = pl.BlockSpec((seq_len, PAIR), lambda g, s: (0, g))
    offsets_spec = pl.BlockSpec((1, 2, span), lambda g, s: (g, 0, 0))
    specs = [
        pl.BlockSpec((pl.Squeezed(), rows, PAIR), lambda g, s: (half, 0, g)),
        keys_spec,
        keys_spec,
        rows_spec,
        rows_spec,
        pl.BlockSpec((1, 2, rows), lambda g, s: (g, 0, 0)),
        offsets_spec,
    ]
    kind = f32
    if carry:
        specs += [keys_spec, keys_spec]
        kind = bf16
    work = rows * seq_len * width
    return pl.pallas_call(
        functools.partial(attend_back_body, block, bool(carry)),
        out_shape=(
            jax.ShapeDtypeStruct((rows, width), bf16),
            jax.ShapeDtypeStruct((seq_len, width), kind),
            jax.ShapeDtypeStruct((seq_len, width), kind),
            jax.ShapeDtypeStruct(offsets.shape, f32),
        ),
        grid_spec=pltpu.PrefetchScalarGridSpec(
            num_scalar_prefetch=1,
            grid=(pairs,),
            in_specs=specs,
            out_specs=[rows_spec, keys_spec, keys_spec, offsets_spec],
            scratch_shapes=[
                pltpu.VMEM((LANES, span), f32),
                pltpu.VMEM((LANES, span), f32),
                pltpu.VMEM((seq_len, PAIR), f32),
                pltpu.VMEM((seq_len, PAIR), f32),
            ],
        ),
        compiler_params=pltpu.CompilerParams(vmem_limit_bytes=60 * MiB),
        cost_estimate=pl.CostEstimate(
            flops=40 * work, transcendentals=work // DH, bytes_accessed=12 * seq_len * width
        ),
        name="attend_back",
    )(scal, queries, keys, values, grads, outs, lse, offsets, *carry)


def normed_rows(values, gain_row):
    inverse = lax.rsqrt(jnp.mean(values * values, axis=-1, keepdims=True) + epsilon)
    return values * inverse * gain_row, inverse


def project_body(
    scal, own_ref, peer_ref, w0_ref, w1_ref, normed_ref, q_ref, k_ref, v_ref, w_ref, gain_ref, gain_row
):
    own_p = scal[2]
    side, step = pl.program_id(0), pl.program_id(1)
    rows, width = w0_ref.shape[1], q_ref.shape[1]

    @pl.when((side == 0) & (step == 0))
    def gather_weights():
        for core, piece in enumerate((w0_ref, w1_ref)):
            for index in range(BLOCKS // 2):
                part = ((index << 1) | core) ^ own_p
                start = aligned(part * rows, 16)
                w_ref[pl.ds(start, rows), :] = piece[index, :, : 3 * width]
                gain_ref[pl.ds(start, rows), :] = piece[index, :, 3 * width :].astype(f32)
        gain_row[...] = jnp.transpose(gain_ref[...])[0:8, :]

    values = jnp.where(side == 0, own_ref[...].astype(f32), peer_ref[...].astype(f32))
    normed = normed_rows(values, gain_row[0:1, :])[0].astype(bf16)
    normed_ref[...] = normed
    made = dot(normed, w_ref[...]).astype(bf16)
    q_ref[...] = made[:, :width]
    k_ref[...] = made[:, width : 2 * width]
    v_ref[...] = made[:, 2 * width :]


def project(scal, own, peer, pieces, width):
    rows, depth = own.shape
    block = min(256, rows)
    steps = rows // block
    whole = pl.BlockSpec(pieces[0].shape, lambda h, b, s: (0, 0, 0))
    by_half = pl.BlockSpec((pl.Squeezed(), block, width), lambda h, b, s: (h, b, 0))
    by_place = pl.BlockSpec((pl.Squeezed(), block, width), lambda h, b, s: (h ^ s[3], b, 0))
    stacked = jax.ShapeDtypeStruct((2, rows, width), bf16)
    return pl.pallas_call(
        project_body,
        out_shape=(
            jax.ShapeDtypeStruct((2, rows, depth), bf16),
            stacked,
            stacked,
            stacked,
            jax.ShapeDtypeStruct((depth, 3 * width), bf16),
            jax.ShapeDtypeStruct((depth, LANES), f32),
        ),
        grid_spec=pltpu.PrefetchScalarGridSpec(
            num_scalar_prefetch=1,
            grid=(2, steps),
            in_specs=[
                pl.BlockSpec((block, depth), lambda h, b, s: (b * (1 - h) + (steps - 1) * h, 0)),
                pl.BlockSpec((block, depth), lambda h, b, s: (b * h, 0)),
                whole,
                whole,
            ],
            out_specs=[
                pl.BlockSpec((pl.Squeezed(), block, depth), lambda h, b, s: (h, b, 0)),
                by_half,
                by_place,
                by_place,
                pl.BlockSpec((depth, 3 * width), lambda h, b, s: (0, 0)),
                pl.BlockSpec((depth, LANES), lambda h, b, s: (0, 0)),
            ],
            scratch_shapes=[pltpu.VMEM((8, depth), f32)],
        ),
        compiler_params=pltpu.CompilerParams(vmem_limit_bytes=60 * MiB),
        cost_estimate=pl.CostEstimate(
            flops=12 * rows * depth * width, transcendentals=0, bytes_accessed=10 * rows * depth
        ),
        name="project",
    )(scal, own, peer, *pieces)


def gelu_parts(values):
    scale = 0.7978845608028654
    square = values * values
    bend = jnp.tanh(scale * (values + 0.044715 * (values * square)))
    half = 0.5 * (1.0 + bend)
    slope = half + (0.5 * scale) * values * (1.0 - bend * bend) * (1.0 + 0.134145 * square)
    return values * half, slope


def bits_of(rel):
    return rel & 1, (rel >> 1) & 1, (rel >> 2) & 1, (rel >> 3) & 1, rel >> 4


def place_of(rel, leading):
    side, _, mid, low, high = bits_of(rel)
    if leading:
        return (mid << 1) | side, (high << 1) | low
    return (mid << 1) | low, (side << 1) | high


def zone_of(rel, zone, leading):
    side, _, mid, low, _ = bits_of(rel)
    if leading:
        return (mid << 1) | side, (zone << 1) + low
    return (mid << 1) | low, (side << 1) + zone


def assemble_rows(pieces, first_column, target, own_p, me):
    half = target.shape[1] // 2
    shard = pieces[0].shape[2]
    for rel in range(2 * BLOCKS):
        side, core = rel & 1, (rel >> 1) & 1
        plane, level = place_of(rel, True)
        row = aligned(((rel >> 1) ^ own_p) * shard, 16)
        column = aligned((side ^ me) * half, LANES)
        source = pieces[core][plane, level, :, pl.ds(first_column, half)]
        target[pl.ds(row, shard), pl.ds(column, half)] = source


def feed_body(leading, direct, scal, *refs):
    refs = list(refs)
    take = lambda count: [refs.pop(0) for _ in range(count)]
    if leading:
        tok_ref, cot_ref, mine_ref, theirs_ref, gain_ref = take(5)
    else:
        rows_in, mid_in, nff_in, out_in, grad_in, mix_in, wo_in, gain_ref = take(8)
    if direct:
        wo_ref = take(1)[0] if leading else None
        wi_ref, *wb_refs = take(3)
    else:
        pieces = take(2)
    if leading:
        rows_s, mid_s, nff_s, out_s, nff_grad, mix_s, wo_s = take(7)
    else:
        out_ref, mid_grad_ref, mix_own_ref, mix_peer_ref, gain_grad_ref = take(5)
    keep_ref, send_ref = take(2)
    if not leading:
        rows_s, mid_s, nff_s, mix_s, wo_s = rows_in, mid_in, nff_in, mix_in, wo_in
        out_s, nff_grad = take(2)
    nff_t, wi_s, wb_s, total = take(4)
    row0, length, own_p, me = scal[0], scal[1], scal[2], scal[3]
    own_r = own_p * 2 + me
    step = pl.program_id(0)
    rows, depth = rows_s.shape
    half = depth // 2
    steps, skip = 2, 1 if leading else 0
    count = depth // (2 * BLOCKS)
    gain_row = jnp.transpose(gain_ref[...])[1:2, :]

    def store_rows(column):
        for rel in range(2 * BLOCKS):
            start = aligned((rel ^ own_r) * count, 8)
            plane, level = place_of(rel, leading)
            target = send_ref if (rel >> 1) & 1 else keep_ref
            piece = total[pl.ds(start, count), :].astype(bf16)
            target[plane, level, :, pl.ds(column, depth)] = piece

    @pl.when(step == 0)
    def start():
        if leading:
            if direct:
                wo_s[...] = wo_ref[...]
            else:
                assemble_rows(pieces, 0, wo_s, own_p, me)
            mix_s[:, pl.ds(aligned(me * half, LANES), half)] = mine_ref[...]
            mix_s[:, pl.ds(aligned((1 - me) * half, LANES), half)] = theirs_ref[...]
            middle = tok_ref[...].astype(f32) + dot(mix_s[...], wo_s[...])
            mid_s[...] = middle
            nff_s[...] = normed_rows(middle, gain_row)[0].astype(bf16)
            position = row0 + lax.broadcasted_iota(jnp.int32, (rows, depth), 0)
            rows_s[...] = jnp.where(position < length, cot_ref[...].astype(f32), 0.0).astype(bf16)
            out_s[...] = middle
            nff_grad[...] = jnp.zeros_like(nff_grad)
        else:
            out_s[...] = out_in[...]
            nff_grad[...] = grad_in[...]
        nff_t[...] = jnp.transpose(nff_s[...].astype(f32)).astype(bf16)

    def hidden_block():
        shard = depth // BLOCKS
        if direct:
            wi_s[...] = wi_ref[...]
            for part in range(BLOCKS // 2):
                for side in range(2):
                    row = (2 * part + side) * shard
                    wb_s[row : row + shard, :] = wb_refs[side][part * shard : (part + 1) * shard, :]
        else:
            assemble_rows(pieces, aligned((skip + step) * half, LANES), wi_s, own_p, me)
            zone = step ^ (own_p >> 3)
            for rel in range(BLOCKS):
                plane, level = zone_of(rel, zone, True)
                column = aligned(((rel & 1) ^ me) * half, LANES)
                for side in range(2):
                    column_in = (skip + 2 + side) * half
                    source = pieces[(rel >> 1) & 1][plane, level, :, column_in : column_in + half]
                    row = aligned((2 * ((rel >> 1) ^ (own_p & 7)) + side) * shard, 16)
                    wb_s[pl.ds(row, shard), pl.ds(column, half)] = source
        pre = dot(nff_s[...], wi_s[...])
        hidden, slope = gelu_parts(pre)
        hidden = hidden.astype(bf16)
        out_s[...] += dot(hidden, wb_s[...])
        pre_grad = (dot_nt(rows_s[...], wb_s[...]) * slope).astype(bf16)
        total[...] = dot_tn(hidden, rows_s[...])
        zone = step ^ (own_p >> 3)
        for rel in range(BLOCKS):
            plane, level = zone_of(rel, zone, leading)
            target = send_ref if (rel >> 1) & 1 else keep_ref
            for side in range(2):
                row = aligned((rel ^ (own_r & 15)) * (2 * count) + side * count, 8)
                piece = total[pl.ds(row, count), :].astype(bf16)
                column = (steps + side) * depth
                target[plane, level, :, column : column + depth] = piece
        nff_grad[...] += dot_nt(pre_grad, wi_s[...])
        total[...] = dot(nff_t[...], pre_grad)
        store_rows(aligned(step * depth, LANES))

    if leading:
        hidden_block()
        return
    pl.when(step < steps)(hidden_block)

    @pl.when(step == steps)
    def finish():
        out_ref[...] = out_s[...].astype(bf16)
        middle = mid_s[...]
        inverse = lax.rsqrt(jnp.mean(middle * middle, axis=-1, keepdims=True) + epsilon)
        grads = nff_grad[...]
        gain_sum = jnp.sum(grads * middle * inverse, axis=0, keepdims=True)
        gain_grad_ref[...] = jnp.broadcast_to(gain_sum, gain_grad_ref.shape)
        scaled = grads * gain_row
        inner = jnp.sum(scaled * middle, axis=-1, keepdims=True)
        mid_grad = (
            rows_s[...].astype(f32)
            + inverse * scaled
            - middle * (inverse * inverse * inverse) * (inner / depth)
        )
        mid_grad_ref[...] = mid_grad
        attn_grad = mid_grad.astype(bf16)
        total[...] = dot_tn(mix_s[...], attn_grad)
        store_rows((steps + 2) * depth)
        turned = dot_nt(attn_grad, wo_s[...])
        first, second = turned[:, :half], turned[:, half:]
        mix_own_ref[...] = jnp.where(me == 0, first, second).astype(bf16)
        mix_peer_ref[...] = jnp.where(me == 0, second, first).astype(bf16)


def fixed(*shape):
    return pl.BlockSpec(shape, lambda *_: (0,) * len(shape))


def direct_specs(depth, skip):
    by_step = lambda f: jnp.minimum(f, 1)
    in_spec = pl.BlockSpec((depth, depth), lambda f, s: (0, by_step(f) + skip))
    low_spec = pl.BlockSpec((depth // 2, depth), lambda f, s: (by_step(f), 2 + skip))
    high_spec = pl.BlockSpec((depth // 2, depth), lambda f, s: (by_step(f), 3 + skip))
    return [fixed(depth, depth)] * skip + [in_spec, low_spec, high_spec]


def feed_call(leading, direct, scal, inputs, in_specs, outputs, chunk, scratch, name):
    rows, depth = outputs[0][0]
    count = depth // (2 * BLOCKS)
    sums = jax.ShapeDtypeStruct((4, 4, count, chunk * depth), bf16)
    return pl.pallas_call(
        functools.partial(feed_body, leading, direct),
        out_shape=[jax.ShapeDtypeStruct(*o) for o in outputs] + [sums] * 2,
        grid_spec=pltpu.PrefetchScalarGridSpec(
            num_scalar_prefetch=1,
            grid=(2 if leading else 3,),
            in_specs=in_specs,
            out_specs=[fixed(*o[0]) for o in outputs] + [fixed(*sums.shape)] * 2,
            scratch_shapes=scratch
            + [
                pltpu.VMEM((depth, rows), bf16),
                pltpu.VMEM((depth, depth), bf16),
                pltpu.VMEM((depth, depth), bf16),
                pltpu.VMEM((depth, depth), f32),
            ],
        ),
        compiler_params=pltpu.CompilerParams(vmem_limit_bytes=60 * MiB),
        cost_estimate=pl.CostEstimate(
            flops=24 * rows * depth * depth,
            transcendentals=2 * rows * depth,
            bytes_accessed=20 * MiB,
        ),
        name=name,
    )(scal, *inputs)


def feed_first(scal, tokens, cotangent, mine, theirs, gains, weights, direct):
    rows, depth = tokens.shape
    inputs = [tokens, cotangent, mine, theirs, gains]
    specs = [fixed(*v.shape) for v in inputs]
    if direct:
        inputs += [weights] * 4
        specs += direct_specs(depth, 1)
    else:
        inputs += weights
        specs += [fixed(*w.shape) for w in weights]
    whole = [(rows, depth)] * 6 + [(depth, depth)]
    outputs = list(zip(whole, [bf16, f32, bf16, f32, f32, bf16, bf16]))
    return feed_call(True, direct, scal, inputs, specs, outputs, 4, [], "feed_first")


def feed_second(scal, state, gains, weights, direct):
    rows, depth = state[0].shape
    half = depth // 2
    inputs = list(state) + [gains]
    specs = [fixed(*v.shape) for v in inputs]
    if direct:
        inputs += [weights] * 3
        specs += direct_specs(depth, 0)
    else:
        inputs += weights
        specs += [fixed(*w.shape) for w in weights]
    whole = [(rows, depth), (rows, depth), (rows, half), (rows, half), (8, depth)]
    outputs = list(zip(whole, [bf16, f32, bf16, bf16, f32]))
    scratch = [pltpu.VMEM((rows, depth), f32)] * 2
    return feed_call(False, direct, scal, inputs, specs, outputs, 5, scratch, "feed_second")


def weight_back_body(
    scal, normed_ref, dq0_ref, dq1_ref, dk_ref, dv_ref, w_ref, gain_ref, ff_ref, table_ref,
    keep_ref, away_ref, total
):
    own_p, me = scal[2], scal[3]
    rows, width = dq0_ref.shape
    depth = w_ref.shape[0]
    near, far = aligned(me * rows, 16), aligned((1 - me) * rows, 16)
    for i, ref in enumerate((None, dk_ref, dv_ref)):
        own = dq0_ref[...] if ref is None else ref[pl.ds(near, rows), :]
        peer = dq1_ref[...] if ref is None else ref[pl.ds(far, rows), :]
        total[:, i * width : (i + 1) * width] = dot_tn(normed_ref[0], own) + dot_tn(normed_ref[1], peer)
    weighted = jnp.sum(total[:, : 3 * width] * w_ref[...].astype(f32), axis=1, keepdims=True)
    lane = lax.broadcasted_iota(jnp.int32, (depth, LANES), 1)
    gains = jnp.where(lane == 0, weighted / gain_ref[:, 0:1], 0.0)
    ff_gain = jnp.transpose(jnp.broadcast_to(ff_ref[0:1, :], (LANES, depth)))
    total[:, 3 * width :] = jnp.where(lane == 1, ff_gain, gains)
    shard = depth // BLOCKS
    for rel in range(BLOCKS):
        start = aligned((rel ^ own_p) * shard, 16)
        whole = jnp.concatenate(
            [
                total[pl.ds(start, shard), : 3 * width],
                total[pl.ds(start, shard), 3 * width :] + table_ref[...],
            ],
            axis=1,
        )
        target = away_ref if rel & 1 else keep_ref
        mid, low, high = (rel >> 1) & 1, (rel >> 2) & 1, rel >> 3
        target[(mid << 1) | low, high] = whole.astype(bf16)


def weight_back(scal, normed, dq_own, dq_peer, dk, dv, weights, gains, ff_gain, table):
    rows, width = dq_own.shape
    depth = weights.shape[0]
    shard = depth // BLOCKS
    inputs = [normed, dq_own, dq_peer, dk, dv, weights, gains, ff_gain, table]
    shape = (4, 2, shard, 3 * width + LANES)
    return pl.pallas_call(
        weight_back_body,
        out_shape=[jax.ShapeDtypeStruct(shape, bf16)] * 2,
        grid_spec=pltpu.PrefetchScalarGridSpec(
            num_scalar_prefetch=1,
            grid=(1,),
            in_specs=[fixed(*v.shape) for v in inputs],
            out_specs=[fixed(*shape)] * 2,
            scratch_shapes=[pltpu.VMEM((depth, 3 * width + LANES), f32)],
        ),
        compiler_params=pltpu.CompilerParams(vmem_limit_bytes=60 * MiB),
        cost_estimate=pl.CostEstimate(
            flops=12 * rows * depth * width, transcendentals=0, bytes_accessed=16 * MiB
        ),
        name="weight_back",
    )(scal, *inputs)


def project_back_body(scal, dq0_ref, dq1_ref, dk_ref, dv_ref, w_ref, own_ref, send_ref, joined):
    side = pl.program_id(0)
    width = dq0_ref.shape[1]
    joined[:, :width] = jnp.where(side == 0, dq1_ref[...].astype(f32), dq0_ref[...].astype(f32)).astype(bf16)
    joined[:, width : 2 * width] = dk_ref[...]
    joined[:, 2 * width :] = dv_ref[...]
    grads = dot_nt(joined[...], w_ref[...])

    @pl.when(side == 0)
    def outgoing():
        send_ref[...] = grads.astype(bf16)

    @pl.when(side == 1)
    def staying():
        own_ref[...] = grads


def project_back(scal, dq_own, dq_peer, dk, dv, weights):
    rows, width = dq_own.shape
    depth = weights.shape[0]
    place = pl.BlockSpec((rows, width), lambda h, s: (1 - h ^ s[3], 0))
    return pl.pallas_call(
        project_back_body,
        out_shape=(
            jax.ShapeDtypeStruct((rows, depth), f32),
            jax.ShapeDtypeStruct((rows, depth), bf16),
        ),
        grid_spec=pltpu.PrefetchScalarGridSpec(
            num_scalar_prefetch=1,
            grid=(2,),
            in_specs=[
                fixed(rows, width),
                fixed(rows, width),
                place,
                place,
                fixed(depth, 3 * width),
            ],
            out_specs=[fixed(rows, depth), fixed(rows, depth)],
            scratch_shapes=[pltpu.VMEM((rows, 3 * width), bf16)],
        ),
        compiler_params=pltpu.CompilerParams(vmem_limit_bytes=60 * MiB),
        cost_estimate=pl.CostEstimate(
            flops=12 * rows * depth * width, transcendentals=0, bytes_accessed=8 * MiB
        ),
        name="project_back",
    )(scal, dq_own, dq_peer, dk, dv, weights)


def last_body(tok_ref, mid_ref, own_ref, come_ref, gain_ref, out_ref):
    depth = tok_ref.shape[1]
    gain_row = jnp.transpose(gain_ref[...])[0:1, :]
    values = tok_ref[...].astype(f32)
    inverse = lax.rsqrt(jnp.mean(values * values, axis=-1, keepdims=True) + epsilon)
    scaled = (own_ref[...] + come_ref[...].astype(f32)) * gain_row
    inner = jnp.sum(scaled * values, axis=-1, keepdims=True)
    grads = inverse * scaled - values * (inverse * inverse * inverse) * (inner / depth)
    out_ref[...] = (mid_ref[...] + grads).astype(bf16)


def last(tokens, mid_grad, own, come, gains):
    rows, depth = tokens.shape
    block = min(256, rows)
    spec = pl.BlockSpec((block, depth), lambda b: (b, 0))
    return pl.pallas_call(
        last_body,
        out_shape=jax.ShapeDtypeStruct((rows, depth), bf16),
        grid=(rows // block,),
        in_specs=[spec, spec, spec, spec, pl.BlockSpec((depth, LANES), lambda b: (0, 0))],
        out_specs=spec,
        compiler_params=pltpu.CompilerParams(vmem_limit_bytes=60 * MiB),
        cost_estimate=pl.CostEstimate(
            flops=16 * rows * depth, transcendentals=0, bytes_accessed=12 * rows * depth
        ),
        name="last",
    )(tokens, mid_grad, own, come, gains)


def chosen(me, low, high):
    return jnp.where(me == 0, low.astype(f32), high.astype(f32)).astype(low.dtype)


def column_of(row):
    count = row.shape[1]
    square = lax.broadcasted_iota(jnp.int32, (count, count), 0)
    other = lax.broadcasted_iota(jnp.int32, (count, count), 1)
    return jnp.sum(jnp.where(square == other, row.astype(f32), 0.0), axis=1, keepdims=True)


def ready_first_body(scal, q_ref, k_ref, v_ref, attn_ref, ff_ref, out_ref):
    me = scal[3]
    width = q_ref.shape[1] // 2
    for i, ref in enumerate((q_ref, k_ref, v_ref)):
        half = chosen(me, ref[:, :width], ref[:, width:])
        out_ref[:, i * width : (i + 1) * width] = half
    lane = lax.broadcasted_iota(jnp.int32, (q_ref.shape[0], LANES), 1)
    gains = jnp.where(lane == 0, column_of(attn_ref[...]), 0.0)
    gains = jnp.where(lane == 1, column_of(ff_ref[...]), gains)
    out_ref[:, 3 * width :] = gains.astype(bf16)


def ready_first(scal, w_query, w_key, w_value, gain_attn, gain_ff):
    rows, depth = w_query.shape
    inputs = [w_query, w_key, w_value, gain_attn[None], gain_ff[None]]
    shape = (rows, 3 * (depth // 2) + LANES)
    return pl.pallas_call(
        ready_first_body,
        out_shape=jax.ShapeDtypeStruct(shape, bf16),
        grid_spec=pltpu.PrefetchScalarGridSpec(
            num_scalar_prefetch=1,
            grid=(1,),
            in_specs=[fixed(*v.shape) for v in inputs],
            out_specs=fixed(*shape),
        ),
        compiler_params=pltpu.CompilerParams(vmem_limit_bytes=60 * MiB),
        name="ready_first",
    )(scal, *inputs)


def ready_rest_body(scal, out_ref, in_ref, back_ref, one_ref, two_ref):
    me = scal[3]
    depth = out_ref.shape[1]
    half = depth // 2
    shard = back_ref.shape[0] // 4
    columns = in_ref[...].astype(f32)
    step = columns.shape[1] // (4 * BLOCKS)
    chunks = []
    for chunk in range(2):
        pieces = [columns[:, (2 * r + chunk) * step : (2 * r + chunk + 1) * step] for r in range(2 * BLOCKS)]
        chunks.append(jnp.concatenate(pieces, axis=1).astype(bf16))
    one_ref[:, :half] = chosen(me, out_ref[:, :half], out_ref[:, half:])
    for f in range(2):
        block = chunks[0][:, f * depth : (f + 1) * depth]
        one_ref[:, (f + 1) * half : (f + 2) * half] = chosen(me, block[:, :half], block[:, half:])
        block = chunks[1][:, f * depth : (f + 1) * depth]
        two_ref[:, f * half : (f + 1) * half] = chosen(me, block[:, :half], block[:, half:])
    for side in range(2):
        rows = back_ref[2 * side * shard : (2 * side + 1) * shard, :]
        one_ref[:, (side + 3) * half : (side + 4) * half] = chosen(me, rows[:, :half], rows[:, half:])
        rows = back_ref[(2 * side + 1) * shard : (2 * side + 2) * shard, :]
        two_ref[:, (side + 2) * half : (side + 3) * half] = chosen(me, rows[:, :half], rows[:, half:])


def ready_rest(scal, w_out, w_in, w_back):
    rows, depth = w_out.shape
    inputs = [w_out, w_in, w_back]
    shapes = [(rows, 5 * depth // 2), (rows, 2 * depth)]
    return pl.pallas_call(
        ready_rest_body,
        out_shape=[jax.ShapeDtypeStruct(s, bf16) for s in shapes],
        grid_spec=pltpu.PrefetchScalarGridSpec(
            num_scalar_prefetch=1,
            grid=(1,),
            in_specs=[fixed(*v.shape) for v in inputs],
            out_specs=[fixed(*s) for s in shapes],
        ),
        compiler_params=pltpu.CompilerParams(vmem_limit_bytes=60 * MiB),
        name="ready_rest",
    )(scal, *inputs)


def summed_refs(refs, start, stop):
    total = refs[0][:, start:stop].astype(f32)
    for ref in refs[1:]:
        total = total + ref[:, start:stop].astype(f32)
    return total


def place_grads_body(count_one, *refs):
    one_refs, two_refs = refs[:count_one], refs[count_one:-3]
    in_ref, back_ref, out_ref = refs[-3:]
    rows, depth = out_ref.shape
    parts = [summed_refs(r, 0, 2 * depth) for r in (one_refs, two_refs)]
    step = 2 * depth // (2 * BLOCKS)
    pieces = []
    for r in range(2 * BLOCKS):
        for part in parts:
            pieces.append(part[:, r * step : (r + 1) * step])
    in_ref[...] = jnp.concatenate(pieces, axis=1)
    for chunk, r in enumerate((one_refs, two_refs)):
        for side in range(2):
            row = (2 * chunk + side) * rows
            back_ref[row : row + rows, :] = summed_refs(r, (2 + side) * depth, (3 + side) * depth)
    out_ref[...] = summed_refs(two_refs, 4 * depth, 5 * depth)


def place_grads(one_parts, two_parts, depth):
    rows = one_parts[0].shape[0]
    inputs = one_parts + two_parts
    shapes = [(rows, 4 * depth), (4 * rows, depth), (rows, depth)]
    return pl.pallas_call(
        functools.partial(place_grads_body, len(one_parts)),
        out_shape=[jax.ShapeDtypeStruct(s, f32) for s in shapes],
        grid=(1,),
        in_specs=[fixed(*v.shape) for v in inputs],
        out_specs=[fixed(*s) for s in shapes],
        compiler_params=pltpu.CompilerParams(vmem_limit_bytes=60 * MiB),
        name="place_grads",
    )(*inputs)


def halve_first_body(column, scal, *refs):
    me = scal[3]
    parts, (mine_ref, theirs_ref, table_ref) = refs[:-3], refs[-3:]
    total = summed_refs(parts, 0, parts[0].shape[1])
    rows = total.shape[0] // 2
    mine_ref[...] = jnp.where(me == 0, total[:rows], total[rows:])
    theirs_ref[...] = jnp.where(me == 0, total[rows:], total[:rows])
    table_ref[...] = total[: table_ref.shape[0], column : column + table_ref.shape[1]]


def halve_first(scal, parts, buckets, heads):
    rows, wide = parts[0].shape
    shapes = [(rows // 2, wide), (rows // 2, wide), (buckets, heads)]
    return pl.pallas_call(
        functools.partial(halve_first_body, wide - LANES + 2),
        out_shape=[jax.ShapeDtypeStruct(s, f32) for s in shapes],
        grid_spec=pltpu.PrefetchScalarGridSpec(
            num_scalar_prefetch=1,
            grid=(1,),
            in_specs=[fixed(*v.shape) for v in parts],
            out_specs=[fixed(*s) for s in shapes],
        ),
        compiler_params=pltpu.CompilerParams(vmem_limit_bytes=60 * MiB),
        name="halve_first",
    )(scal, *parts)


def place_first_body(scal, mine_ref, theirs_ref, *out_refs):
    me = scal[3]
    width = out_refs[0].shape[1] // 2
    for i, ref in enumerate(out_refs[:3]):
        mine = mine_ref[:, i * width : (i + 1) * width]
        theirs = theirs_ref[:, i * width : (i + 1) * width]
        ref[:, :width] = jnp.where(me == 0, mine, theirs)
        ref[:, width:] = jnp.where(me == 0, theirs, mine)
    gains = mine_ref[:, 3 * width :] + theirs_ref[:, 3 * width :]
    rows = gains.shape[0]
    square = lax.broadcasted_iota(jnp.int32, (rows, rows), 0)
    other = lax.broadcasted_iota(jnp.int32, (rows, rows), 1)
    for i in range(2):
        spread_out = jnp.where(square == other, gains[:, i : i + 1], 0.0)
        out_refs[3 + i][...] = jnp.sum(spread_out, axis=0, keepdims=True)


def place_first(scal, mine, theirs):
    rows, wide = mine.shape
    depth = (wide - LANES) // 3 * 2
    shapes = [(rows, depth)] * 3 + [(1, rows)] * 2
    return pl.pallas_call(
        place_first_body,
        out_shape=[jax.ShapeDtypeStruct(s, f32) for s in shapes],
        grid_spec=pltpu.PrefetchScalarGridSpec(
            num_scalar_prefetch=1,
            grid=(1,),
            in_specs=[fixed(*mine.shape)] * 2,
            out_specs=[fixed(*s) for s in shapes],
        ),
        compiler_params=pltpu.CompilerParams(vmem_limit_bytes=60 * MiB),
        name="place_first",
    )(scal, mine, theirs)


def hop(value, mask):
    size = lax.axis_size("dp") * 2
    return lax.ppermute(value, ("dp", "seq"), [(i, i ^ mask) for i in range(size)])


def tied(*values):
    return lax.optimization_barrier(values)


LEVELS = (8, 16, 24)
PLANES = (1, 4, 5)
HEIGHTS = (8, 4, 12)
ENDS = (16, 1, 17)
CORE = 2


def spread(value, masks):
    return [hop(value, mask) for mask in masks]


def total_of(parts, kind):
    total = parts[0].astype(f32)
    for part in parts[1:]:
        total = total + part.astype(f32)
    return total.astype(kind)


def scatter_sums(parts, masks):
    sums = [total_of([p[i] for p in parts], bf16) for i in range(len(masks) + 1)]
    return sums[0], [hop(s, m) for s, m in zip(sums[1:], masks)]


def whole_gather(shard):
    return lax.all_gather(shard, "dp", axis=0, tiled=True)


def join_grid(keep, send, axes):
    both = jnp.stack([keep, send])
    both = both.reshape((2,) * (len(axes) + 1) + both.shape[-2:])
    axes = ("c",) + axes
    order = ("z2", "z1", "y", "c") + (("x",) if "x" in axes else ())
    both = both.transpose([axes.index(n) for n in order] + [both.ndim - 2, both.ndim - 1])
    if "x" in axes:
        both = jnp.where(lax.axis_index("seq") == 1, jnp.flip(both, 4), both)
    return both.astype(f32)


def chunk_columns(weight, chunk):
    rows, hidden = weight.shape
    grid = weight.reshape(rows, BLOCKS * 2, 2, hidden // (4 * BLOCKS))
    return grid[:, :, chunk].reshape(rows, hidden // 2)


def chunk_rows(weight, chunk, shards):
    rows, depth = weight.shape
    grid = weight.reshape(shards, 2, 2, rows // (4 * shards), depth)[:, :, chunk]
    return [grid[:, side].reshape(-1, depth) for side in range(2)]


def halves(sums, depth):
    low, high = sums[..., 2 * depth : 3 * depth], sums[..., 3 * depth : 4 * depth]
    return sums[..., : 2 * depth], jnp.stack([low, high], -3)


def local(
    tokens,
    cotangent,
    lengths,
    rel_bucket,
    gain_attn,
    w_query,
    w_key,
    w_value,
    w_out,
    gain_ff,
    w_in,
    w_back,
    bias_table,
):
    place, me = lax.axis_index("dp"), lax.axis_index("seq")
    own, cot = tokens[0], cotangent[0]
    rows, depth = own.shape
    seq_len = rows * 2
    width = depth // 2
    near = lax.axis_size("dp") == BLOCKS
    length = lengths[0]
    part = place if near else jnp.int32(0)
    info = jnp.stack([me * rows, length, part, me]).astype(jnp.int32)
    far_info = jnp.stack([(1 - me) * rows, length, part, me]).astype(jnp.int32)

    if near:
        first = ready_first(info, w_query, w_key, w_value, gain_attn, gain_ff)
        come = spread(first, LEVELS)
    peer = hop(own, 1)

    padded = jnp.pad(rel_bucket, (0, 1), constant_values=-1)[::-1]
    padded = jnp.concatenate([padded[LANES:], padded[:LANES]])
    choice = jnp.arange(bias_table.shape[0], dtype=jnp.int32)[:, None] == padded[None, :]
    choice = choice.astype(f32)
    offsets = lax.dot_general(bias_table, choice, TN, precision=precise)
    offsets = offsets.reshape(-1, 2, 2 * seq_len)

    if near:
        one, two = ready_rest(info, w_out, w_in, w_back)
        first, come, one, two = tied(first, come, one, two)
        first = jnp.stack([first] + come)
        come = hop(first, 4)
        one_come = spread(one, LEVELS)
        first, come, peer, one, one_come, two = tied(first, come, peer, one, one_come, two)
        first = jnp.stack([first, come], axis=1)
        first = first.reshape((BLOCKS // 2,) + first.shape[2:])
        first = [first, hop(first, CORE)]
        one = jnp.stack([one] + one_come)
        one_come = spread(one, PLANES)
        two_come = hop(two, 16)
    else:
        columns = [w_query, w_key, w_value]
        columns = [lax.dynamic_slice_in_dim(w, me * width, width, 1) for w in columns]
        gains = jnp.pad(jnp.stack([gain_attn, gain_ff], axis=1), ((0, 0), (0, LANES - 2)))
        first = whole_gather(jnp.concatenate(columns + [gains], axis=1))
        first = first.reshape(BLOCKS // 2, 2, -1, first.shape[1])
        first = [first[:, 0], first[:, 1]]
        in_all, back_all = whole_gather(w_in), whole_gather(w_back)
        one = [whole_gather(w_out), chunk_columns(in_all, 0)] + chunk_rows(back_all, 0, BLOCKS)
        one = jnp.concatenate(one, axis=1)
        two = jnp.concatenate([chunk_columns(in_all, 1)] + chunk_rows(back_all, 1, BLOCKS), axis=1)

    normed, query, keys, values, weights, gain_cols = project(info, own, peer, first, width)
    keys, values = keys.reshape(seq_len, width), values.reshape(seq_len, width)
    if near:
        query, two, two_come = tied(query, two, two_come)
        two = jnp.stack([two, two_come])
        two_come = hop(two, 8)
        query, two = tied(query, two)
    far_out, far_lse = attend(far_info, 1, query, keys, values, offsets)
    theirs = hop(far_out, 1)
    query, far_lse = tied(query, far_lse)
    near_out, near_lse = attend(info, 0, query, keys, values, offsets)
    if near:
        near_out, one, one_come, theirs, two, two_come = tied(
            near_out, one, one_come, theirs, two, two_come
        )
        one = jnp.stack([one] + one_come)
        one_come = hop(one, CORE)
        two = jnp.stack([two, two_come], axis=1)
        two = two.reshape((4,) + two.shape[2:])
        two_come = spread(two, PLANES)
        one, two = tied(one, two)
        one = [one, one_come]
    made = feed_first(info, own, cot, near_out, theirs, gain_cols, one, not near)
    state, keep_one, send_one = made[:7], made[7], made[8]
    if near:
        come = hop(send_one, CORE)
        keep_one, two, two_come = tied(keep_one, two, two_come)
        two = jnp.stack([two] + two_come)
        two_come = hop(two, CORE)
        keep_one, two = tied(keep_one, two)
        keep_one, come_one = scatter_sums([keep_one, come], PLANES)
        state, keep_one = tied(state, keep_one)
        two = [two, two_come]
    made = feed_second(info, state, gain_cols, two, not near)
    result, mid_grad, mix_own, mix_peer, ff_gain, keep_two, send_two = made
    if near:
        keep_one, come_one, mix_peer, send_two = tied(keep_one, come_one, mix_peer, send_two)
        sums = [total_of([p[i] for p in [keep_one] + come_one], bf16) for i in range(4)]
        keep_one, away = jnp.stack([sums[0], sums[2]]), jnp.stack([sums[1], sums[3]])
        come_one = hop(away, LEVELS[0])
    far_grads = hop(mix_peer, 1)
    if near:
        come_two = hop(send_two, CORE)
        keep_one, keep_two, come_two = tied(keep_one, keep_two, come_two)
        keep_two, come_two = scatter_sums([keep_two, come_two], HEIGHTS)
        mix_own, keep_one, keep_two = tied(mix_own, keep_one, keep_two)
    dq_own, dk, dv, diag_own = attend_back(
        info, 0, query, keys, values, mix_own, near_out, near_lse, offsets, ()
    )
    if near:
        dk, keep_one, come_one, far_grads = tied(dk, keep_one, come_one, far_grads)
        keep_one, come_one = scatter_sums([keep_one, come_one], LEVELS[1:2])
        dk, keep_one = tied(dk, keep_one)
    dq_peer, dk, dv, diag_peer = attend_back(
        far_info, 1, query, keys, values, far_grads, far_out, far_lse, offsets, (dk, dv)
    )
    if near:
        dk, keep_one, come_one, keep_two, come_two = tied(dk, keep_one, come_one, keep_two, come_two)
        keep_two, come_two = scatter_sums([keep_two] + come_two, ENDS)
        dk, keep_two = tied(dk, keep_two)
    diag = (diag_own + diag_peer).reshape(-1, 2 * seq_len)
    table = lax.dot_general(choice, diag, NT, precision=precise)
    buckets, heads = table.shape
    shard = depth // BLOCKS
    table = jnp.pad(table, ((0, shard - buckets), (2, LANES - 2 - heads)))
    w_keep, w_send = weight_back(
        info, normed, dq_own, dq_peer, dk, dv, weights, gain_cols, ff_gain, table
    )
    if near:
        w_come = hop(w_send, CORE)
        dk, w_keep = tied(dk, w_keep)
    stay, leave = project_back(info, dq_own, dq_peer, dk, dv, weights)
    if near:
        w_keep, w_come, leave = tied(w_keep, w_come, leave)
        w_keep, w_come = scatter_sums([w_keep, w_come], HEIGHTS)
        leave, w_keep = tied(leave, w_keep)
    come = hop(leave, 1)
    if near:
        keep_two, come_two, w_keep = tied(keep_two, come_two, w_keep)
        grad_in, grad_back, grad_out = place_grads([keep_one] + come_one, [keep_two] + come_two, depth)
        w_keep, w_come, grad_in = tied(w_keep, w_come, grad_in)
        w_keep, w_come = scatter_sums([w_keep] + w_come, (16,))
        stay, come, w_keep = tied(stay, come, w_keep)
    grad_tokens = last(own, mid_grad, stay, come, gain_cols)
    if near:
        w_keep, w_come, grad_tokens = tied(w_keep, w_come, grad_tokens)
        mine, theirs, table = halve_first(info, [w_keep] + w_come, buckets, heads)
    else:
        scatter = functools.partial(lax.psum_scatter, scatter_dimension=0, tiled=True)
        both = ("dp", "seq")
        one_sum = join_grid(keep_one, send_one, ("y", "x", "z2", "z1"))
        two_sum = join_grid(keep_two, send_two, ("y", "z1", "x", "z2"))
        grad_first = join_grid(w_keep, w_send, ("y", "z1", "z2")).reshape(depth, -1)
        table = lax.psum(grad_first[:shard], "dp")
        table = table[:buckets, 3 * width + 2 : 3 * width + 2 + heads]
        grad_first = scatter(grad_first, "dp")
        in_one, back_one = halves(one_sum, depth)
        in_two, back_two = halves(two_sum, depth)
        grad_in = jnp.stack([in_one, in_two], axis=-2)
        grad_in = grad_in.reshape(-1, 2, 2 * BLOCKS, depth // BLOCKS).transpose(0, 2, 1, 3)
        grad_in = scatter(grad_in.reshape(-1, 4 * depth), both)
        grad_back = jnp.stack([back_one, back_two], axis=-4).reshape(-1, depth)
        grad_back = scatter(grad_back, both)
        grad_out = scatter(two_sum[..., 4 * depth :].reshape(-1, depth), both)
        count = grad_first.shape[0] // 2
        mine = lax.dynamic_slice_in_dim(grad_first, me * count, count, 0)
        theirs = lax.dynamic_slice_in_dim(grad_first, (1 - me) * count, count, 0)

    *full, attn_gain, ff_gain = place_first(info, mine, hop(theirs, 1))
    return (
        result[None],
        grad_tokens[None],
        attn_gain[0],
        full[0],
        full[1],
        full[2],
        grad_out,
        ff_gain[0],
        grad_in,
        grad_back,
        table,
    )


def solution(mesh):
    return jax.shard_map(
        local,
        mesh=mesh,
        in_specs=(
            P("dp", "seq", None),
            P("dp", "seq", None),
            P("dp"),
            P(),
            P("dp"),
            P("dp", None),
            P("dp", None),
            P("dp", None),
            P("dp", None),
            P("dp"),
            P("dp", None),
            P("dp", None),
            P(None, "seq"),
        ),
        out_specs=(
            P("dp", "seq", None),
            P("dp", "seq", None),
            P(("dp", "seq")),
            P(("dp", "seq"), None),
            P(("dp", "seq"), None),
            P(("dp", "seq"), None),
            P(("dp", "seq"), None),
            P(("dp", "seq")),
            P(("dp", "seq"), None),
            P(("dp", "seq"), None),
            P(None, "seq"),
        ),
        check_vma=False,
    )
```

```python
import functools

import jax
import jax.numpy as jnp
from jax import lax
from jax.experimental import pallas as pl
from jax.experimental.pallas import tpu as pltpu
from jax.sharding import PartitionSpec as P

DH = 64
PAIR = 2 * DH
LANES = 128
BLOCKS = 16
NT = (((1,), (1,)), ((), ()))
TN = (((0,), (0,)), ((), ()))
epsilon = 1e-06
masked_score = -1e30
precise = lax.Precision.HIGHEST
f32 = jnp.float32
bf16 = jnp.bfloat16
MiB = 2**20


def dot(a, b):
    return jnp.dot(a, b, preferred_element_type=f32)


def dot_nt(a, b):
    return lax.dot_general(a, b, NT, preferred_element_type=f32)


def dot_tn(a, b):
    return lax.dot_general(a, b, TN, preferred_element_type=f32)


def aligned(value, unit):
    return pl.multiple_of(value, unit)


def head_lanes(shape, dim, head):
    index = lax.broadcasted_iota(jnp.int32, shape, dim)
    return (index < DH) if head == 0 else (index >= DH)


def flag_lane(head):
    return DH if head == 0 else 0


def fill_bias(offsets_ref, head, bias_tile):
    row = jnp.broadcast_to(offsets_ref[0, head : head + 1, :], bias_tile.shape)
    bias_tile[...] = pltpu.roll(row, 0, 1, stride=1, stride_axis=0)


def masked_keys(keys, head, length):
    lane = lax.broadcasted_iota(jnp.int32, keys.shape, 1)
    position = lax.broadcasted_iota(jnp.int32, keys.shape, 0)
    other = jnp.where((lane == flag_lane(head)) & (position >= length), masked_score, 0.0)
    return jnp.where(head_lanes(keys.shape, 1, head), keys.astype(f32), other).astype(bf16)


def only_head(rows, head):
    return jnp.where(head_lanes(rows.shape, 1, head), rows.astype(f32), 0.0).astype(bf16)


def flagged(rows, head):
    lane = lax.broadcasted_iota(jnp.int32, rows.shape, 1)
    flag = jnp.where(lane == flag_lane(head), 1.0, 0.0)
    return jnp.where(head_lanes(rows.shape, 1, head), rows.astype(f32), flag).astype(bf16)


def bias_columns(bias_tile, first, count, key_tiles):
    parts = []
    for tile in range(key_tiles):
        start = aligned((key_tiles - 1 - tile) * LANES + first, LANES)
        parts.append(bias_tile[:, pl.ds(start, count)])
    return jnp.concatenate(parts, axis=0)


def attend_body(block, scal, q_ref, k_ref, v_ref, offsets_ref, out_ref, lse_ref, bias_tile):
    row0, length = scal[0], scal[1]
    rows, key_tiles = q_ref.shape[0], k_ref.shape[0] // LANES
    values_t = jnp.transpose(v_ref[...].astype(f32))
    outs = [[] for _ in range(rows // block)]
    for head in range(2):
        fill_bias(offsets_ref, head, bias_tile)
        keys = masked_keys(k_ref[...], head, length)
        values_h = jnp.where(head_lanes(values_t.shape, 0, head), values_t, 1.0).astype(bf16)
        for b in range(rows // block):
            rs = slice(b * block, (b + 1) * block)
            scores = dot_nt(keys, flagged(q_ref[rs, :], head))
            scores = scores + bias_columns(bias_tile, row0 + b * block, block, key_tiles)
            top = jnp.max(scores, axis=0, keepdims=True)
            weights = jnp.exp(scores - top).astype(bf16)
            mixed_t = dot(values_h, weights)
            total = mixed_t[flag_lane(head) : flag_lane(head) + 1]
            mine = mixed_t[:DH] if head == 0 else mixed_t[DH:]
            outs[b].append(mine / total)
            lse_ref[0, head : head + 1, rs] = top + jnp.log(total)
    for b in range(rows // block):
        joined = jnp.transpose(jnp.concatenate(outs[b], axis=0))
        out_ref[b * block : (b + 1) * block, :] = joined.astype(bf16)


def attend(scal, half, queries, keys, values, offsets):
    rows, width = queries.shape[1:]
    seq_len, pairs, span = keys.shape[0], width // PAIR, offsets.shape[2]
    block = min(256, rows)
    tokens_spec = pl.BlockSpec((rows, PAIR), lambda g, s: (0, g))
    keys_spec = pl.BlockSpec((seq_len, PAIR), lambda g, s: (0, g))
    work = rows * seq_len * width
    return pl.pallas_call(
        functools.partial(attend_body, block),
        out_shape=(
            jax.ShapeDtypeStruct((rows, width), bf16),
            jax.ShapeDtypeStruct((pairs, 2, rows), f32),
        ),
        grid_spec=pltpu.PrefetchScalarGridSpec(
            num_scalar_prefetch=1,
            grid=(pairs,),
            in_specs=[
                pl.BlockSpec((pl.Squeezed(), rows, PAIR), lambda g, s: (half, 0, g)),
                keys_spec,
                keys_spec,
                pl.BlockSpec((1, 2, span), lambda g, s: (g, 0, 0)),
            ],
            out_specs=[tokens_spec, pl.BlockSpec((1, 2, rows), lambda g, s: (g, 0, 0))],
            scratch_shapes=[pltpu.VMEM((LANES, span), f32)],
        ),
        compiler_params=pltpu.CompilerParams(vmem_limit_bytes=24 * MiB),
        cost_estimate=pl.CostEstimate(
            flops=16 * work, transcendentals=work // DH, bytes_accessed=4 * seq_len * width
        ),
        name="attend",
    )(scal, queries, keys, values, offsets)


def diagonal_sums(tile):
    span = tile.shape[1]
    size = tile.shape[0] // 2
    while size >= 8:
        tile = tile[:size] + pltpu.roll(tile[size:], span - size, 1)
        size //= 2
    row = lax.broadcasted_iota(jnp.int32, tile.shape, 0)
    for bit in (1, 2, 4):
        tile = jnp.where((row & bit) != 0, pltpu.roll(tile, span - bit, 1), tile)
    return jnp.sum(tile, axis=0, keepdims=True)


def attend_back_body(block, carry, scal, *refs):
    q_ref, k_ref, v_ref, g_ref, o_ref, lse_ref, offsets_ref = refs[:7]
    dq_ref, dk_ref, dv_ref, diag_ref, bias_tile, diag_tile, dk_sum, dv_sum = refs[-8:]
    row0, length = scal[0], scal[1]
    rows, key_tiles = q_ref.shape[0], k_ref.shape[0] // LANES
    if carry:
        dk_sum[...] = refs[7][...]
        dv_sum[...] = refs[8][...]
    else:
        dk_sum[...] = jnp.zeros_like(dk_sum)
        dv_sum[...] = jnp.zeros_like(dv_sum)
    keys_t = jnp.transpose(k_ref[...].astype(f32)).astype(bf16)
    count = rows // block
    dqs = [[] for _ in range(count)]
    deltas = []
    for b in range(count):
        rs = slice(b * block, (b + 1) * block)
        product = jnp.transpose(g_ref[rs, :].astype(f32) * o_ref[rs, :].astype(f32))
        deltas.append(
            (
                jnp.sum(product[:DH], axis=0, keepdims=True),
                jnp.sum(product[DH:], axis=0, keepdims=True),
            )
        )
    for head in range(2):
        fill_bias(offsets_ref, head, bias_tile)
        diag_tile[...] = jnp.zeros_like(diag_tile)
        keys = masked_keys(k_ref[...], head, length)
        for b in range(count):
            rs = slice(b * block, (b + 1) * block)
            queries = q_ref[rs, :]
            grads = only_head(g_ref[rs, :], head)
            scores = dot_nt(keys, flagged(queries, head))
            scores = scores + bias_columns(bias_tile, row0 + b * block, block, key_tiles)
            probs = jnp.exp(scores - lse_ref[0, head : head + 1, rs])
            grad_probs = dot_nt(v_ref[...], grads)
            grad_scores = probs * (grad_probs - deltas[b][head])
            for tile in range(key_tiles):
                start = aligned((key_tiles - 1 - tile) * LANES + row0 + b * block, LANES)
                diag_tile[:, pl.ds(start, block)] += grad_scores[tile * LANES : (tile + 1) * LANES]
            grad_scores = grad_scores.astype(bf16)
            dv_sum[...] += dot(probs.astype(bf16), grads)
            dk_sum[...] += dot(grad_scores, only_head(queries, head))
            dq_t = dot(keys_t, grad_scores)
            dqs[b].append(dq_t[:DH] if head == 0 else dq_t[DH:])
        diag_ref[0, head : head + 1, :] = diagonal_sums(diag_tile[...])
    for b in range(count):
        joined = jnp.transpose(jnp.concatenate(dqs[b], axis=0))
        dq_ref[b * block : (b + 1) * block, :] = joined.astype(bf16)
    dk_ref[...] = dk_sum[...].astype(dk_ref.dtype)
    dv_ref[...] = dv_sum[...].astype(dv_ref.dtype)


def attend_back(scal, half, queries, keys, values, grads, outs, lse, offsets, carry):
    rows, width = queries.shape[1:]
    seq_len, pairs, span = keys.shape[0], width // PAIR, offsets.shape[2]
    block = min(256, rows)
    rows_spec = pl.BlockSpec((rows, PAIR), lambda g, s: (0, g))
    keys_spec = pl.BlockSpec((seq_len, PAIR), lambda g, s: (0, g))
    offsets_spec = pl.BlockSpec((1, 2, span), lambda g, s: (g, 0, 0))
    specs = [
        pl.BlockSpec((pl.Squeezed(), rows, PAIR), lambda g, s: (half, 0, g)),
        keys_spec,
        keys_spec,
        rows_spec,
        rows_spec,
        pl.BlockSpec((1, 2, rows), lambda g, s: (g, 0, 0)),
        offsets_spec,
    ]
    kind = f32
    if carry:
        specs += [keys_spec, keys_spec]
        kind = bf16
    work = rows * seq_len * width
    return pl.pallas_call(
        functools.partial(attend_back_body, block, bool(carry)),
        out_shape=(
            jax.ShapeDtypeStruct((rows, width), bf16),
            jax.ShapeDtypeStruct((seq_len, width), kind),
            jax.ShapeDtypeStruct((seq_len, width), kind),
            jax.ShapeDtypeStruct(offsets.shape, f32),
        ),
        grid_spec=pltpu.PrefetchScalarGridSpec(
            num_scalar_prefetch=1,
            grid=(pairs,),
            in_specs=specs,
            out_specs=[rows_spec, keys_spec, keys_spec, offsets_spec],
            scratch_shapes=[
                pltpu.VMEM((LANES, span), f32),
                pltpu.VMEM((LANES, span), f32),
                pltpu.VMEM((seq_len, PAIR), f32),
                pltpu.VMEM((seq_len, PAIR), f32),
            ],
        ),
        compiler_params=pltpu.CompilerParams(vmem_limit_bytes=32 * MiB),
        cost_estimate=pl.CostEstimate(
            flops=40 * work, transcendentals=work // DH, bytes_accessed=12 * seq_len * width
        ),
        name="attend_back",
    )(scal, queries, keys, values, grads, outs, lse, offsets, *carry)


def normed_rows(values, gain_row):
    inverse = lax.rsqrt(jnp.mean(values * values, axis=-1, keepdims=True) + epsilon)
    return values * inverse * gain_row, inverse


def project_body(
    scal, own_ref, peer_ref, w0_ref, w1_ref, normed_ref, q_ref, k_ref, v_ref, w_ref, gain_ref, gain_row
):
    own_p = scal[2]
    side, step = pl.program_id(0), pl.program_id(1)
    rows, width = w0_ref.shape[1], q_ref.shape[1]

    @pl.when((side == 0) & (step == 0))
    def gather_weights():
        for core, piece in enumerate((w0_ref, w1_ref)):
            for index in range(BLOCKS // 2):
                part = ((index << 1) | core) ^ own_p
                start = aligned(part * rows, 16)
                w_ref[pl.ds(start, rows), :] = piece[index, :, : 3 * width]
                gain_ref[pl.ds(start, rows), :] = piece[index, :, 3 * width :].astype(f32)
        gain_row[...] = jnp.transpose(gain_ref[...])[0:8, :]

    values = jnp.where(side == 0, own_ref[...].astype(f32), peer_ref[...].astype(f32))
    normed = normed_rows(values, gain_row[0:1, :])[0].astype(bf16)
    normed_ref[...] = normed
    made = dot(normed, w_ref[...]).astype(bf16)
    q_ref[...] = made[:, :width]
    k_ref[...] = made[:, width : 2 * width]
    v_ref[...] = made[:, 2 * width :]


def project(scal, own, peer, pieces, width):
    rows, depth = own.shape
    block = min(256, rows)
    steps = rows // block
    whole = pl.BlockSpec(pieces[0].shape, lambda h, b, s: (0, 0, 0))
    by_half = pl.BlockSpec((pl.Squeezed(), block, width), lambda h, b, s: (h, b, 0))
    by_place = pl.BlockSpec((pl.Squeezed(), block, width), lambda h, b, s: (h ^ s[3], b, 0))
    stacked = jax.ShapeDtypeStruct((2, rows, width), bf16)
    return pl.pallas_call(
        project_body,
        out_shape=(
            jax.ShapeDtypeStruct((2, rows, depth), bf16),
            stacked,
            stacked,
            stacked,
            jax.ShapeDtypeStruct((depth, 3 * width), bf16),
            jax.ShapeDtypeStruct((depth, LANES), f32),
        ),
        grid_spec=pltpu.PrefetchScalarGridSpec(
            num_scalar_prefetch=1,
            grid=(2, steps),
            in_specs=[
                pl.BlockSpec((block, depth), lambda h, b, s: (b * (1 - h) + (steps - 1) * h, 0)),
                pl.BlockSpec((block, depth), lambda h, b, s: (b * h, 0)),
                whole,
                whole,
            ],
            out_specs=[
                pl.BlockSpec((pl.Squeezed(), block, depth), lambda h, b, s: (h, b, 0)),
                by_half,
                by_place,
                by_place,
                pl.BlockSpec((depth, 3 * width), lambda h, b, s: (0, 0)),
                pl.BlockSpec((depth, LANES), lambda h, b, s: (0, 0)),
            ],
            scratch_shapes=[pltpu.VMEM((8, depth), f32)],
        ),
        compiler_params=pltpu.CompilerParams(vmem_limit_bytes=16 * MiB),
        cost_estimate=pl.CostEstimate(
            flops=12 * rows * depth * width, transcendentals=0, bytes_accessed=10 * rows * depth
        ),
        name="project",
    )(scal, own, peer, *pieces)


def gelu_parts(values):
    scale = 0.7978845608028654
    square = values * values
    bend = jnp.tanh(scale * (values + 0.044715 * (values * square)))
    half = 0.5 * (1.0 + bend)
    slope = half + (0.5 * scale) * values * (1.0 - bend * bend) * (1.0 + 0.134145 * square)
    return values * half, slope


def bits_of(rel):
    return rel & 1, (rel >> 1) & 1, (rel >> 2) & 1, (rel >> 3) & 1, rel >> 4


def place_of(rel, leading):
    side, _, mid, low, high = bits_of(rel)
    if leading:
        return (mid << 1) | side, (high << 1) | low
    return (mid << 1) | low, (side << 1) | high


def zone_of(rel, zone, leading):
    side, _, mid, low, _ = bits_of(rel)
    if leading:
        return (mid << 1) | side, (zone << 1) + low
    return (mid << 1) | low, (side << 1) + zone


def assemble_rows(pieces, first_column, target, own_p, me):
    half = target.shape[1] // 2
    shard = pieces[0].shape[2]
    for rel in range(2 * BLOCKS):
        side, core = rel & 1, (rel >> 1) & 1
        plane, level = place_of(rel, True)
        row = aligned(((rel >> 1) ^ own_p) * shard, 16)
        column = aligned((side ^ me) * half, LANES)
        source = pieces[core][plane, level, :, pl.ds(first_column, half)]
        target[pl.ds(row, shard), pl.ds(column, half)] = source


def feed_body(leading, direct, scal, *refs):
    refs = list(refs)
    take = lambda count: [refs.pop(0) for _ in range(count)]
    if leading:
        tok_ref, cot_ref, mine_ref, theirs_ref, gain_ref = take(5)
    else:
        rows_in, mid_in, nff_in, out_in, grad_in, mix_in, wo_in, gain_ref = take(8)
    if direct:
        wo_ref = take(1)[0] if leading else None
        wi_ref, *wb_refs = take(3)
    else:
        pieces = take(2)
    if leading:
        rows_s, mid_s, nff_s, out_s, nff_grad, mix_s, wo_s = take(7)
    else:
        out_ref, mid_grad_ref, mix_own_ref, mix_peer_ref, gain_grad_ref = take(5)
    keep_ref, send_ref = take(2)
    if not leading:
        rows_s, mid_s, nff_s, mix_s, wo_s = rows_in, mid_in, nff_in, mix_in, wo_in
        out_s, nff_grad = take(2)
    nff_t, wi_s, wb_s, total = take(4)
    row0, length, own_p, me = scal[0], scal[1], scal[2], scal[3]
    own_r = own_p * 2 + me
    step = pl.program_id(0)
    rows, depth = rows_s.shape
    half = depth // 2
    steps, skip = 2, 1 if leading else 0
    count = depth // (2 * BLOCKS)
    gain_row = jnp.transpose(gain_ref[...])[1:2, :]

    def store_rows(column):
        for rel in range(2 * BLOCKS):
            start = aligned((rel ^ own_r) * count, 8)
            plane, level = place_of(rel, leading)
            target = send_ref if (rel >> 1) & 1 else keep_ref
            piece = total[pl.ds(start, count), :].astype(bf16)
            target[plane, level, :, pl.ds(column, depth)] = piece

    @pl.when(step == 0)
    def start():
        if leading:
            if direct:
                wo_s[...] = wo_ref[...]
            else:
                assemble_rows(pieces, 0, wo_s, own_p, me)
            mix_s[:, pl.ds(aligned(me * half, LANES), half)] = mine_ref[...]
            mix_s[:, pl.ds(aligned((1 - me) * half, LANES), half)] = theirs_ref[...]
            middle = tok_ref[...].astype(f32) + dot(mix_s[...], wo_s[...])
            mid_s[...] = middle
            nff_s[...] = normed_rows(middle, gain_row)[0].astype(bf16)
            position = row0 + lax.broadcasted_iota(jnp.int32, (rows, depth), 0)
            rows_s[...] = jnp.where(position < length, cot_ref[...].astype(f32), 0.0).astype(bf16)
            out_s[...] = middle
            nff_grad[...] = jnp.zeros_like(nff_grad)
        else:
            out_s[...] = out_in[...]
            nff_grad[...] = grad_in[...]
        nff_t[...] = jnp.transpose(nff_s[...].astype(f32)).astype(bf16)

    def hidden_block():
        shard = depth // BLOCKS
        if direct:
            wi_s[...] = wi_ref[...]
            for part in range(BLOCKS // 2):
                for side in range(2):
                    row = (2 * part + side) * shard
                    wb_s[row : row + shard, :] = wb_refs[side][part * shard : (part + 1) * shard, :]
        else:
            assemble_rows(pieces, aligned((skip + step) * half, LANES), wi_s, own_p, me)
            zone = step ^ (own_p >> 3)
            for rel in range(BLOCKS):
                plane, level = zone_of(rel, zone, True)
                column = aligned(((rel & 1) ^ me) * half, LANES)
                for side in range(2):
                    column_in = (skip + 2 + side) * half
                    source = pieces[(rel >> 1) & 1][plane, level, :, column_in : column_in + half]
                    row = aligned((2 * ((rel >> 1) ^ (own_p & 7)) + side) * shard, 16)
                    wb_s[pl.ds(row, shard), pl.ds(column, half)] = source
        pre = dot(nff_s[...], wi_s[...])
        hidden, slope = gelu_parts(pre)
        hidden = hidden.astype(bf16)
        out_s[...] += dot(hidden, wb_s[...])
        pre_grad = (dot_nt(rows_s[...], wb_s[...]) * slope).astype(bf16)
        total[...] = dot_tn(hidden, rows_s[...])
        zone = step ^ (own_p >> 3)
        for rel in range(BLOCKS):
            plane, level = zone_of(rel, zone, leading)
            target = send_ref if (rel >> 1) & 1 else keep_ref
            for side in range(2):
                row = aligned((rel ^ (own_r & 15)) * (2 * count) + side * count, 8)
                piece = total[pl.ds(row, count), :].astype(bf16)
                column = (steps + side) * depth
                target[plane, level, :, column : column + depth] = piece
        nff_grad[...] += dot_nt(pre_grad, wi_s[...])
        total[...] = dot(nff_t[...], pre_grad)
        store_rows(aligned(step * depth, LANES))

    if leading:
        hidden_block()
        return
    pl.when(step < steps)(hidden_block)

    @pl.when(step == steps)
    def finish():
        out_ref[...] = out_s[...].astype(bf16)
        middle = mid_s[...]
        inverse = lax.rsqrt(jnp.mean(middle * middle, axis=-1, keepdims=True) + epsilon)
        grads = nff_grad[...]
        gain_sum = jnp.sum(grads * middle * inverse, axis=0, keepdims=True)
        gain_grad_ref[...] = jnp.broadcast_to(gain_sum, gain_grad_ref.shape)
        scaled = grads * gain_row
        inner = jnp.sum(scaled * middle, axis=-1, keepdims=True)
        mid_grad = (
            rows_s[...].astype(f32)
            + inverse * scaled
            - middle * (inverse * inverse * inverse) * (inner / depth)
        )
        mid_grad_ref[...] = mid_grad
        attn_grad = mid_grad.astype(bf16)
        total[...] = dot_tn(mix_s[...], attn_grad)
        store_rows((steps + 2) * depth)
        turned = dot_nt(attn_grad, wo_s[...])
        first, second = turned[:, :half], turned[:, half:]
        mix_own_ref[...] = jnp.where(me == 0, first, second).astype(bf16)
        mix_peer_ref[...] = jnp.where(me == 0, second, first).astype(bf16)


def fixed(*shape):
    return pl.BlockSpec(shape, lambda *_: (0,) * len(shape), pipeline_mode=pl.Buffered(1))


def direct_specs(depth, skip):
    by_step = lambda f: jnp.minimum(f, 1)
    in_spec = pl.BlockSpec((depth, depth), lambda f, s: (0, by_step(f) + skip))
    low_spec = pl.BlockSpec((depth // 2, depth), lambda f, s: (by_step(f), 2 + skip))
    high_spec = pl.BlockSpec((depth // 2, depth), lambda f, s: (by_step(f), 3 + skip))
    return [fixed(depth, depth)] * skip + [in_spec, low_spec, high_spec]


def feed_call(leading, direct, scal, inputs, in_specs, outputs, chunk, scratch, name):
    rows, depth = outputs[0][0]
    count = depth // (2 * BLOCKS)
    sums = jax.ShapeDtypeStruct((4, 4, count, chunk * depth), bf16)
    return pl.pallas_call(
        functools.partial(feed_body, leading, direct),
        out_shape=[jax.ShapeDtypeStruct(*o) for o in outputs] + [sums] * 2,
        grid_spec=pltpu.PrefetchScalarGridSpec(
            num_scalar_prefetch=1,
            grid=(2 if leading else 3,),
            in_specs=in_specs,
            out_specs=[fixed(*o[0]) for o in outputs] + [fixed(*sums.shape)] * 2,
            scratch_shapes=scratch
            + [
                pltpu.VMEM((depth, rows), bf16),
                pltpu.VMEM((depth, depth), bf16),
                pltpu.VMEM((depth, depth), bf16),
                pltpu.VMEM((depth, depth), f32),
            ],
        ),
        compiler_params=pltpu.CompilerParams(vmem_limit_bytes=40 * MiB),
        cost_estimate=pl.CostEstimate(
            flops=24 * rows * depth * depth,
            transcendentals=2 * rows * depth,
            bytes_accessed=20 * MiB,
        ),
        name=name,
    )(scal, *inputs)


def feed_first(scal, tokens, cotangent, mine, theirs, gains, weights, direct):
    rows, depth = tokens.shape
    inputs = [tokens, cotangent, mine, theirs, gains]
    specs = [fixed(*v.shape) for v in inputs]
    if direct:
        inputs += [weights] * 4
        specs += direct_specs(depth, 1)
    else:
        inputs += weights
        specs += [fixed(*w.shape) for w in weights]
    whole = [(rows, depth)] * 6 + [(depth, depth)]
    outputs = list(zip(whole, [bf16, f32, bf16, f32, f32, bf16, bf16]))
    return feed_call(True, direct, scal, inputs, specs, outputs, 4, [], "feed_first")


def feed_second(scal, state, gains, weights, direct):
    rows, depth = state[0].shape
    half = depth // 2
    inputs = list(state) + [gains]
    specs = [fixed(*v.shape) for v in inputs]
    if direct:
        inputs += [weights] * 3
        specs += direct_specs(depth, 0)
    else:
        inputs += weights
        specs += [fixed(*w.shape) for w in weights]
    whole = [(rows, depth), (rows, depth), (rows, half), (rows, half), (8, depth)]
    outputs = list(zip(whole, [bf16, f32, bf16, bf16, f32]))
    scratch = [pltpu.VMEM((rows, depth), f32)] * 2
    return feed_call(False, direct, scal, inputs, specs, outputs, 5, scratch, "feed_second")


def weight_back_body(
    scal, normed_ref, dq0_ref, dq1_ref, dk_ref, dv_ref, w_ref, gain_ref, ff_ref, table_ref,
    keep_ref, away_ref, total
):
    own_p, me = scal[2], scal[3]
    rows, width = dq0_ref.shape
    depth = w_ref.shape[0]
    near, far = aligned(me * rows, 16), aligned((1 - me) * rows, 16)
    for i, ref in enumerate((None, dk_ref, dv_ref)):
        own = dq0_ref[...] if ref is None else ref[pl.ds(near, rows), :]
        peer = dq1_ref[...] if ref is None else ref[pl.ds(far, rows), :]
        total[:, i * width : (i + 1) * width] = dot_tn(normed_ref[0], own) + dot_tn(normed_ref[1], peer)
    weighted = jnp.sum(total[:, : 3 * width] * w_ref[...].astype(f32), axis=1, keepdims=True)
    lane = lax.broadcasted_iota(jnp.int32, (depth, LANES), 1)
    gains = jnp.where(lane == 0, weighted / gain_ref[:, 0:1], 0.0)
    ff_gain = jnp.transpose(jnp.broadcast_to(ff_ref[0:1, :], (LANES, depth)))
    total[:, 3 * width :] = jnp.where(lane == 1, ff_gain, gains)
    shard = depth // BLOCKS
    for rel in range(BLOCKS):
        start = aligned((rel ^ own_p) * shard, 16)
        whole = jnp.concatenate(
            [
                total[pl.ds(start, shard), : 3 * width],
                total[pl.ds(start, shard), 3 * width :] + table_ref[...],
            ],
            axis=1,
        )
        target = away_ref if rel & 1 else keep_ref
        mid, low, high = (rel >> 1) & 1, (rel >> 2) & 1, rel >> 3
        target[(mid << 1) | low, high] = whole.astype(bf16)


def weight_back(scal, normed, dq_own, dq_peer, dk, dv, weights, gains, ff_gain, table):
    rows, width = dq_own.shape
    depth = weights.shape[0]
    shard = depth // BLOCKS
    inputs = [normed, dq_own, dq_peer, dk, dv, weights, gains, ff_gain, table]
    shape = (4, 2, shard, 3 * width + LANES)
    return pl.pallas_call(
        weight_back_body,
        out_shape=[jax.ShapeDtypeStruct(shape, bf16)] * 2,
        grid_spec=pltpu.PrefetchScalarGridSpec(
            num_scalar_prefetch=1,
            grid=(1,),
            in_specs=[fixed(*v.shape) for v in inputs],
            out_specs=[fixed(*shape)] * 2,
            scratch_shapes=[pltpu.VMEM((depth, 3 * width + LANES), f32)],
        ),
        compiler_params=pltpu.CompilerParams(vmem_limit_bytes=60 * MiB),
        cost_estimate=pl.CostEstimate(
            flops=12 * rows * depth * width, transcendentals=0, bytes_accessed=16 * MiB
        ),
        name="weight_back",
    )(scal, *inputs)


def project_back_body(scal, dq0_ref, dq1_ref, dk_ref, dv_ref, w_ref, own_ref, send_ref, joined):
    side = pl.program_id(0)
    width = dq0_ref.shape[1]
    joined[:, :width] = jnp.where(side == 0, dq1_ref[...].astype(f32), dq0_ref[...].astype(f32)).astype(bf16)
    joined[:, width : 2 * width] = dk_ref[...]
    joined[:, 2 * width :] = dv_ref[...]
    grads = dot_nt(joined[...], w_ref[...])

    @pl.when(side == 0)
    def outgoing():
        send_ref[...] = grads.astype(bf16)

    @pl.when(side == 1)
    def staying():
        own_ref[...] = grads


def project_back(scal, dq_own, dq_peer, dk, dv, weights):
    rows, width = dq_own.shape
    depth = weights.shape[0]
    place = pl.BlockSpec((rows, width), lambda h, s: (1 - h ^ s[3], 0))
    return pl.pallas_call(
        project_back_body,
        out_shape=(
            jax.ShapeDtypeStruct((rows, depth), f32),
            jax.ShapeDtypeStruct((rows, depth), bf16),
        ),
        grid_spec=pltpu.PrefetchScalarGridSpec(
            num_scalar_prefetch=1,
            grid=(2,),
            in_specs=[
                fixed(rows, width),
                fixed(rows, width),
                place,
                place,
                fixed(depth, 3 * width),
            ],
            out_specs=[fixed(rows, depth), fixed(rows, depth)],
            scratch_shapes=[pltpu.VMEM((rows, 3 * width), bf16)],
        ),
        compiler_params=pltpu.CompilerParams(vmem_limit_bytes=60 * MiB),
        cost_estimate=pl.CostEstimate(
            flops=12 * rows * depth * width, transcendentals=0, bytes_accessed=8 * MiB
        ),
        name="project_back",
    )(scal, dq_own, dq_peer, dk, dv, weights)


def last_body(tok_ref, mid_ref, own_ref, come_ref, gain_ref, out_ref):
    depth = tok_ref.shape[1]
    gain_row = jnp.transpose(gain_ref[...])[0:1, :]
    values = tok_ref[...].astype(f32)
    inverse = lax.rsqrt(jnp.mean(values * values, axis=-1, keepdims=True) + epsilon)
    scaled = (own_ref[...] + come_ref[...].astype(f32)) * gain_row
    inner = jnp.sum(scaled * values, axis=-1, keepdims=True)
    grads = inverse * scaled - values * (inverse * inverse * inverse) * (inner / depth)
    out_ref[...] = (mid_ref[...] + grads).astype(bf16)


def last(tokens, mid_grad, own, come, gains):
    rows, depth = tokens.shape
    block = min(256, rows)
    spec = pl.BlockSpec((block, depth), lambda b: (b, 0))
    return pl.pallas_call(
        last_body,
        out_shape=jax.ShapeDtypeStruct((rows, depth), bf16),
        grid=(rows // block,),
        in_specs=[spec, spec, spec, spec, pl.BlockSpec((depth, LANES), lambda b: (0, 0))],
        out_specs=spec,
        compiler_params=pltpu.CompilerParams(vmem_limit_bytes=60 * MiB),
        cost_estimate=pl.CostEstimate(
            flops=16 * rows * depth, transcendentals=0, bytes_accessed=12 * rows * depth
        ),
        name="last",
    )(tokens, mid_grad, own, come, gains)


def chosen(me, low, high):
    return jnp.where(me == 0, low.astype(f32), high.astype(f32)).astype(low.dtype)


def column_of(row):
    count = row.shape[1]
    square = lax.broadcasted_iota(jnp.int32, (count, count), 0)
    other = lax.broadcasted_iota(jnp.int32, (count, count), 1)
    return jnp.sum(jnp.where(square == other, row.astype(f32), 0.0), axis=1, keepdims=True)


def ready_first_body(scal, q_ref, k_ref, v_ref, attn_ref, ff_ref, out_ref):
    me = scal[3]
    width = q_ref.shape[1] // 2
    for i, ref in enumerate((q_ref, k_ref, v_ref)):
        half = chosen(me, ref[:, :width], ref[:, width:])
        out_ref[:, i * width : (i + 1) * width] = half
    lane = lax.broadcasted_iota(jnp.int32, (q_ref.shape[0], LANES), 1)
    gains = jnp.where(lane == 0, column_of(attn_ref[...]), 0.0)
    gains = jnp.where(lane == 1, column_of(ff_ref[...]), gains)
    out_ref[:, 3 * width :] = gains.astype(bf16)


def ready_first(scal, w_query, w_key, w_value, gain_attn, gain_ff):
    rows, depth = w_query.shape
    inputs = [w_query, w_key, w_value, gain_attn[None], gain_ff[None]]
    shape = (rows, 3 * (depth // 2) + LANES)
    return pl.pallas_call(
        ready_first_body,
        out_shape=jax.ShapeDtypeStruct(shape, bf16),
        grid_spec=pltpu.PrefetchScalarGridSpec(
            num_scalar_prefetch=1,
            grid=(1,),
            in_specs=[fixed(*v.shape) for v in inputs],
            out_specs=fixed(*shape),
        ),
        compiler_params=pltpu.CompilerParams(vmem_limit_bytes=60 * MiB),
        name="ready_first",
    )(scal, *inputs)


def ready_rest_body(scal, out_ref, in_ref, back_ref, one_ref, two_ref):
    me = scal[3]
    depth = out_ref.shape[1]
    half = depth // 2
    shard = back_ref.shape[0] // 4
    columns = in_ref[...].astype(f32)
    step = columns.shape[1] // (4 * BLOCKS)
    chunks = []
    for chunk in range(2):
        pieces = [columns[:, (2 * r + chunk) * step : (2 * r + chunk + 1) * step] for r in range(2 * BLOCKS)]
        chunks.append(jnp.concatenate(pieces, axis=1).astype(bf16))
    one_ref[:, :half] = chosen(me, out_ref[:, :half], out_ref[:, half:])
    for f in range(2):
        block = chunks[0][:, f * depth : (f + 1) * depth]
        one_ref[:, (f + 1) * half : (f + 2) * half] = chosen(me, block[:, :half], block[:, half:])
        block = chunks[1][:, f * depth : (f + 1) * depth]
        two_ref[:, f * half : (f + 1) * half] = chosen(me, block[:, :half], block[:, half:])
    for side in range(2):
        rows = back_ref[2 * side * shard : (2 * side + 1) * shard, :]
        one_ref[:, (side + 3) * half : (side + 4) * half] = chosen(me, rows[:, :half], rows[:, half:])
        rows = back_ref[(2 * side + 1) * shard : (2 * side + 2) * shard, :]
        two_ref[:, (side + 2) * half : (side + 3) * half] = chosen(me, rows[:, :half], rows[:, half:])


def ready_rest(scal, w_out, w_in, w_back):
    rows, depth = w_out.shape
    inputs = [w_out, w_in, w_back]
    shapes = [(rows, 5 * depth // 2), (rows, 2 * depth)]
    return pl.pallas_call(
        ready_rest_body,
        out_shape=[jax.ShapeDtypeStruct(s, bf16) for s in shapes],
        grid_spec=pltpu.PrefetchScalarGridSpec(
            num_scalar_prefetch=1,
            grid=(1,),
            in_specs=[fixed(*v.shape) for v in inputs],
            out_specs=[fixed(*s) for s in shapes],
        ),
        compiler_params=pltpu.CompilerParams(vmem_limit_bytes=60 * MiB),
        name="ready_rest",
    )(scal, *inputs)


def summed_refs(refs, start, stop):
    total = refs[0][:, start:stop].astype(f32)
    for ref in refs[1:]:
        total = total + ref[:, start:stop].astype(f32)
    return total


def place_grads_body(count_one, *refs):
    one_refs, two_refs = refs[:count_one], refs[count_one:-3]
    in_ref, back_ref, out_ref = refs[-3:]
    rows, depth = out_ref.shape
    parts = [summed_refs(r, 0, 2 * depth) for r in (one_refs, two_refs)]
    step = 2 * depth // (2 * BLOCKS)
    pieces = []
    for r in range(2 * BLOCKS):
        for part in parts:
            pieces.append(part[:, r * step : (r + 1) * step])
    in_ref[...] = jnp.concatenate(pieces, axis=1)
    for chunk, r in enumerate((one_refs, two_refs)):
        for side in range(2):
            row = (2 * chunk + side) * rows
            back_ref[row : row + rows, :] = summed_refs(r, (2 + side) * depth, (3 + side) * depth)
    out_ref[...] = summed_refs(two_refs, 4 * depth, 5 * depth)


def place_grads(one_parts, two_parts, depth):
    rows = one_parts[0].shape[0]
    inputs = one_parts + two_parts
    shapes = [(rows, 4 * depth), (4 * rows, depth), (rows, depth)]
    return pl.pallas_call(
        functools.partial(place_grads_body, len(one_parts)),
        out_shape=[jax.ShapeDtypeStruct(s, f32) for s in shapes],
        grid=(1,),
        in_specs=[fixed(*v.shape) for v in inputs],
        out_specs=[fixed(*s) for s in shapes],
        compiler_params=pltpu.CompilerParams(vmem_limit_bytes=16 * MiB),
        name="place_grads",
    )(*inputs)


def halve_first_body(column, scal, *refs):
    me = scal[3]
    parts, (mine_ref, theirs_ref, table_ref) = refs[:-3], refs[-3:]
    total = summed_refs(parts, 0, parts[0].shape[1])
    rows = total.shape[0] // 2
    mine_ref[...] = jnp.where(me == 0, total[:rows], total[rows:])
    theirs_ref[...] = jnp.where(me == 0, total[rows:], total[:rows])
    table_ref[...] = total[: table_ref.shape[0], column : column + table_ref.shape[1]]


def halve_first(scal, parts, buckets, heads):
    rows, wide = parts[0].shape
    shapes = [(rows // 2, wide), (rows // 2, wide), (buckets, heads)]
    return pl.pallas_call(
        functools.partial(halve_first_body, wide - LANES + 2),
        out_shape=[jax.ShapeDtypeStruct(s, f32) for s in shapes],
        grid_spec=pltpu.PrefetchScalarGridSpec(
            num_scalar_prefetch=1,
            grid=(1,),
            in_specs=[fixed(*v.shape) for v in parts],
            out_specs=[fixed(*s) for s in shapes],
        ),
        compiler_params=pltpu.CompilerParams(vmem_limit_bytes=16 * MiB),
        name="halve_first",
    )(scal, *parts)


def place_first_body(scal, mine_ref, theirs_ref, *out_refs):
    me = scal[3]
    width = out_refs[0].shape[1] // 2
    for i, ref in enumerate(out_refs[:3]):
        mine = mine_ref[:, i * width : (i + 1) * width]
        theirs = theirs_ref[:, i * width : (i + 1) * width]
        ref[:, :width] = jnp.where(me == 0, mine, theirs)
        ref[:, width:] = jnp.where(me == 0, theirs, mine)
    gains = mine_ref[:, 3 * width :] + theirs_ref[:, 3 * width :]
    rows = gains.shape[0]
    square = lax.broadcasted_iota(jnp.int32, (rows, rows), 0)
    other = lax.broadcasted_iota(jnp.int32, (rows, rows), 1)
    for i in range(2):
        spread_out = jnp.where(square == other, gains[:, i : i + 1], 0.0)
        out_refs[3 + i][...] = jnp.sum(spread_out, axis=0, keepdims=True)


def place_first(scal, mine, theirs):
    rows, wide = mine.shape
    depth = (wide - LANES) // 3 * 2
    shapes = [(rows, depth)] * 3 + [(1, rows)] * 2
    return pl.pallas_call(
        place_first_body,
        out_shape=[jax.ShapeDtypeStruct(s, f32) for s in shapes],
        grid_spec=pltpu.PrefetchScalarGridSpec(
            num_scalar_prefetch=1,
            grid=(1,),
            in_specs=[fixed(*mine.shape)] * 2,
            out_specs=[fixed(*s) for s in shapes],
        ),
        compiler_params=pltpu.CompilerParams(vmem_limit_bytes=16 * MiB),
        name="place_first",
    )(scal, mine, theirs)


def hop(value, mask):
    size = lax.axis_size("dp") * 2
    return lax.ppermute(value, ("dp", "seq"), [(i, i ^ mask) for i in range(size)])


def tied(*values):
    return lax.optimization_barrier(values)


LEVELS = (8, 16, 24)
PLANES = (1, 4, 5)
HEIGHTS = (8, 4, 12)
ENDS = (16, 1, 17)
CORE = 2


def spread(value, masks):
    return [hop(value, mask) for mask in masks]


def total_of(parts, kind):
    total = parts[0].astype(f32)
    for part in parts[1:]:
        total = total + part.astype(f32)
    return total.astype(kind)


def scatter_sums(parts, masks):
    sums = [total_of([p[i] for p in parts], bf16) for i in range(len(masks) + 1)]
    return sums[0], [hop(s, m) for s, m in zip(sums[1:], masks)]


def whole_gather(shard):
    return lax.all_gather(shard, "dp", axis=0, tiled=True)


def join_grid(keep, send, axes):
    both = jnp.stack([keep, send])
    both = both.reshape((2,) * (len(axes) + 1) + both.shape[-2:])
    axes = ("c",) + axes
    order = ("z2", "z1", "y", "c") + (("x",) if "x" in axes else ())
    both = both.transpose([axes.index(n) for n in order] + [both.ndim - 2, both.ndim - 1])
    if "x" in axes:
        both = jnp.where(lax.axis_index("seq") == 1, jnp.flip(both, 4), both)
    return both.astype(f32)


def chunk_columns(weight, chunk):
    rows, hidden = weight.shape
    grid = weight.reshape(rows, BLOCKS * 2, 2, hidden // (4 * BLOCKS))
    return grid[:, :, chunk].reshape(rows, hidden // 2)


def chunk_rows(weight, chunk, shards):
    rows, depth = weight.shape
    grid = weight.reshape(shards, 2, 2, rows // (4 * shards), depth)[:, :, chunk]
    return [grid[:, side].reshape(-1, depth) for side in range(2)]


def halves(sums, depth):
    low, high = sums[..., 2 * depth : 3 * depth], sums[..., 3 * depth : 4 * depth]
    return sums[..., : 2 * depth], jnp.stack([low, high], -3)


def local(
    tokens,
    cotangent,
    lengths,
    rel_bucket,
    gain_attn,
    w_query,
    w_key,
    w_value,
    w_out,
    gain_ff,
    w_in,
    w_back,
    bias_table,
):
    place, me = lax.axis_index("dp"), lax.axis_index("seq")
    own, cot = tokens[0], cotangent[0]
    rows, depth = own.shape
    seq_len = rows * 2
    width = depth // 2
    near = lax.axis_size("dp") == BLOCKS
    length = lengths[0]
    part = place if near else jnp.int32(0)
    info = jnp.stack([me * rows, length, part, me]).astype(jnp.int32)
    far_info = jnp.stack([(1 - me) * rows, length, part, me]).astype(jnp.int32)

    if near:
        first = ready_first(info, w_query, w_key, w_value, gain_attn, gain_ff)
        come = spread(first, LEVELS)
    peer = hop(own, 1)

    padded = jnp.pad(rel_bucket, (0, 1), constant_values=-1)[::-1]
    padded = jnp.concatenate([padded[LANES:], padded[:LANES]])
    choice = jnp.arange(bias_table.shape[0], dtype=jnp.int32)[:, None] == padded[None, :]
    choice = choice.astype(f32)
    offsets = lax.dot_general(bias_table, choice, TN, precision=precise)
    offsets = offsets.reshape(-1, 2, 2 * seq_len)

    if near:
        one, two = ready_rest(info, w_out, w_in, w_back)
        first, come, one, two = tied(first, come, one, two)
        first = jnp.stack([first] + come)
        come = hop(first, 4)
        one_come = spread(one, LEVELS)
        first, come, peer, one, one_come, two = tied(first, come, peer, one, one_come, two)
        first = jnp.stack([first, come], axis=1)
        first = first.reshape((BLOCKS // 2,) + first.shape[2:])
        first = [first, hop(first, CORE)]
        one = jnp.stack([one] + one_come)
        one_come = spread(one, PLANES)
        two_come = hop(two, 16)
    else:
        columns = [w_query, w_key, w_value]
        columns = [lax.dynamic_slice_in_dim(w, me * width, width, 1) for w in columns]
        gains = jnp.pad(jnp.stack([gain_attn, gain_ff], axis=1), ((0, 0), (0, LANES - 2)))
        first = whole_gather(jnp.concatenate(columns + [gains], axis=1))
        first = first.reshape(BLOCKS // 2, 2, -1, first.shape[1])
        first = [first[:, 0], first[:, 1]]
        in_all, back_all = whole_gather(w_in), whole_gather(w_back)
        one = [whole_gather(w_out), chunk_columns(in_all, 0)] + chunk_rows(back_all, 0, BLOCKS)
        one = jnp.concatenate(one, axis=1)
        two = jnp.concatenate([chunk_columns(in_all, 1)] + chunk_rows(back_all, 1, BLOCKS), axis=1)

    normed, query, keys, values, weights, gain_cols = project(info, own, peer, first, width)
    keys, values = keys.reshape(seq_len, width), values.reshape(seq_len, width)
    if near:
        query, two, two_come = tied(query, two, two_come)
        two = jnp.stack([two, two_come])
        two_come = hop(two, 8)
        query, two = tied(query, two)
    far_out, far_lse = attend(far_info, 1, query, keys, values, offsets)
    theirs = hop(far_out, 1)
    query, far_lse = tied(query, far_lse)
    near_out, near_lse = attend(info, 0, query, keys, values, offsets)
    if near:
        near_out, one, one_come, theirs, two, two_come = tied(
            near_out, one, one_come, theirs, two, two_come
        )
        one = jnp.stack([one] + one_come)
        one_come = hop(one, CORE)
        two = jnp.stack([two, two_come], axis=1)
        two = two.reshape((4,) + two.shape[2:])
        two_come = spread(two, PLANES)
        one, two = tied(one, two)
        one = [one, one_come]
    made = feed_first(info, own, cot, near_out, theirs, gain_cols, one, not near)
    state, keep_one, send_one = made[:7], made[7], made[8]
    if near:
        come = hop(send_one, CORE)
        keep_one, two, two_come = tied(keep_one, two, two_come)
        two = jnp.stack([two] + two_come)
        two_come = hop(two, CORE)
        keep_one, two = tied(keep_one, two)
        keep_one, come_one = scatter_sums([keep_one, come], PLANES)
        state, keep_one = tied(state, keep_one)
        two = [two, two_come]
    made = feed_second(info, state, gain_cols, two, not near)
    result, mid_grad, mix_own, mix_peer, ff_gain, keep_two, send_two = made
    if near:
        keep_one, come_one, mix_peer, send_two = tied(keep_one, come_one, mix_peer, send_two)
        sums = [total_of([p[i] for p in [keep_one] + come_one], bf16) for i in range(4)]
        keep_one, away = jnp.stack([sums[0], sums[2]]), jnp.stack([sums[1], sums[3]])
        come_one = hop(away, LEVELS[0])
    far_grads = hop(mix_peer, 1)
    if near:
        come_two = hop(send_two, CORE)
        keep_one, keep_two, come_two = tied(keep_one, keep_two, come_two)
        keep_two, come_two = scatter_sums([keep_two, come_two], HEIGHTS)
        mix_own, keep_one, keep_two = tied(mix_own, keep_one, keep_two)
    dq_own, dk, dv, diag_own = attend_back(
        info, 0, query, keys, values, mix_own, near_out, near_lse, offsets, ()
    )
    if near:
        dk, keep_one, come_one, far_grads = tied(dk, keep_one, come_one, far_grads)
        keep_one, come_one = scatter_sums([keep_one, come_one], LEVELS[1:2])
        dk, keep_one = tied(dk, keep_one)
    dq_peer, dk, dv, diag_peer = attend_back(
        far_info, 1, query, keys, values, far_grads, far_out, far_lse, offsets, (dk, dv)
    )
    diag = (diag_own + diag_peer).reshape(-1, 2 * seq_len)
    table = lax.dot_general(choice, diag, NT, precision=precise)
    buckets, heads = table.shape
    shard = depth // BLOCKS
    table = jnp.pad(table, ((0, shard - buckets), (2, LANES - 2 - heads)))
    w_keep, w_send = weight_back(
        info, normed, dq_own, dq_peer, dk, dv, weights, gain_cols, ff_gain, table
    )
    if near:
        w_come = hop(w_send, CORE)
        keep_two, come_two, w_keep = tied(keep_two, come_two, w_keep)
        parts = [keep_two] + come_two
        away = total_of([p[2:] for p in parts], bf16)
        keep_two = total_of([p[:2] for p in parts], bf16)
        come_two = hop(away, 1)
        w_keep, w_come, keep_two = tied(w_keep, w_come, keep_two)
        w_keep, w_come = scatter_sums([w_keep, w_come], HEIGHTS)
        dk, w_keep = tied(dk, w_keep)
    stay, leave = project_back(info, dq_own, dq_peer, dk, dv, weights)
    come = hop(leave, 1)
    if near:
        keep_two, come_two, stay = tied(keep_two, come_two, stay)
        keep_two, come_two = scatter_sums([keep_two, come_two], (16,))
        w_keep, w_come, keep_two = tied(w_keep, w_come, keep_two)
        w_keep, w_come = scatter_sums([w_keep] + w_come, (16,))
        keep_two, come_two, w_keep = tied(keep_two, come_two, w_keep)
        grad_in, grad_back, grad_out = place_grads([keep_one] + come_one, [keep_two] + come_two, depth)
        w_keep, w_come, grad_in = tied(w_keep, w_come, grad_in)
        mine, theirs, table = halve_first(info, [w_keep] + w_come, buckets, heads)
        stay, come, mine = tied(stay, come, mine)
    grad_tokens = last(own, mid_grad, stay, come, gain_cols)
    if near:
        mine, grad_tokens = tied(mine, grad_tokens)
    else:
        scatter = functools.partial(lax.psum_scatter, scatter_dimension=0, tiled=True)
        both = ("dp", "seq")
        one_sum = join_grid(keep_one, send_one, ("y", "x", "z2", "z1"))
        two_sum = join_grid(keep_two, send_two, ("y", "z1", "x", "z2"))
        grad_first = join_grid(w_keep, w_send, ("y", "z1", "z2")).reshape(depth, -1)
        table = lax.psum(grad_first[:shard], "dp")
        table = table[:buckets, 3 * width + 2 : 3 * width + 2 + heads]
        grad_first = scatter(grad_first, "dp")
        in_one, back_one = halves(one_sum, depth)
        in_two, back_two = halves(two_sum, depth)
        grad_in = jnp.stack([in_one, in_two], axis=-2)
        grad_in = grad_in.reshape(-1, 2, 2 * BLOCKS, depth // BLOCKS).transpose(0, 2, 1, 3)
        grad_in = scatter(grad_in.reshape(-1, 4 * depth), both)
        grad_back = jnp.stack([back_one, back_two], axis=-4).reshape(-1, depth)
        grad_back = scatter(grad_back, both)
        grad_out = scatter(two_sum[..., 4 * depth :].reshape(-1, depth), both)
        count = grad_first.shape[0] // 2
        mine = lax.dynamic_slice_in_dim(grad_first, me * count, count, 0)
        theirs = lax.dynamic_slice_in_dim(grad_first, (1 - me) * count, count, 0)

    *full, attn_gain, ff_gain = place_first(info, mine, hop(theirs, 1))
    return (
        result[None],
        grad_tokens[None],
        attn_gain[0],
        full[0],
        full[1],
        full[2],
        grad_out,
        ff_gain[0],
        grad_in,
        grad_back,
        table,
    )


def solution(mesh):
    return jax.shard_map(
        local,
        mesh=mesh,
        in_specs=(
            P("dp", "seq", None),
            P("dp", "seq", None),
            P("dp"),
            P(),
            P("dp"),
            P("dp", None),
            P("dp", None),
            P("dp", None),
            P("dp", None),
            P("dp"),
            P("dp", None),
            P("dp", None),
            P(None, "seq"),
        ),
        out_specs=(
            P("dp", "seq", None),
            P("dp", "seq", None),
            P(("dp", "seq")),
            P(("dp", "seq"), None),
            P(("dp", "seq"), None),
            P(("dp", "seq"), None),
            P(("dp", "seq"), None),
            P(("dp", "seq")),
            P(("dp", "seq"), None),
            P(("dp", "seq"), None),
            P(None, "seq"),
        ),
        check_vma=False,
    )
```

```python
import functools

import jax
import jax.numpy as jnp
from jax import lax
from jax.experimental import pallas as pl
from jax.experimental.pallas import tpu as pltpu
from jax.sharding import PartitionSpec as P

DH = 64
PAIR = 2 * DH
LANES = 128
BLOCKS = 16
NT = (((1,), (1,)), ((), ()))
TN = (((0,), (0,)), ((), ()))
epsilon = 1e-06
masked_score = -1e30
precise = lax.Precision.HIGHEST
f32 = jnp.float32
bf16 = jnp.bfloat16
MiB = 2**20


def dot(a, b):
    return jnp.dot(a, b, preferred_element_type=f32)


def dot_nt(a, b):
    return lax.dot_general(a, b, NT, preferred_element_type=f32)


def dot_tn(a, b):
    return lax.dot_general(a, b, TN, preferred_element_type=f32)


def aligned(value, unit):
    return pl.multiple_of(value, unit)


def head_lanes(shape, dim, head):
    index = lax.broadcasted_iota(jnp.int32, shape, dim)
    return (index < DH) if head == 0 else (index >= DH)


def flag_lane(head):
    return DH if head == 0 else 0


def fill_bias(offsets_ref, head, bias_tile):
    row = jnp.broadcast_to(offsets_ref[0, head : head + 1, :], bias_tile.shape)
    bias_tile[...] = pltpu.roll(row, 0, 1, stride=1, stride_axis=0)


def masked_keys(keys, head, length):
    lane = lax.broadcasted_iota(jnp.int32, keys.shape, 1)
    position = lax.broadcasted_iota(jnp.int32, keys.shape, 0)
    other = jnp.where((lane == flag_lane(head)) & (position >= length), masked_score, 0.0)
    return jnp.where(head_lanes(keys.shape, 1, head), keys.astype(f32), other).astype(bf16)


def only_head(rows, head):
    return jnp.where(head_lanes(rows.shape, 1, head), rows.astype(f32), 0.0).astype(bf16)


def flagged(rows, head):
    lane = lax.broadcasted_iota(jnp.int32, rows.shape, 1)
    flag = jnp.where(lane == flag_lane(head), 1.0, 0.0)
    return jnp.where(head_lanes(rows.shape, 1, head), rows.astype(f32), flag).astype(bf16)


def bias_columns(bias_tile, first, count, key_tiles):
    parts = []
    for tile in range(key_tiles):
        start = aligned((key_tiles - 1 - tile) * LANES + first, LANES)
        parts.append(bias_tile[:, pl.ds(start, count)])
    return jnp.concatenate(parts, axis=0)


def attend_body(block, scal, q_ref, k_ref, v_ref, offsets_ref, out_ref, lse_ref, bias_tile):
    row0, length = scal[0], scal[1]
    rows, key_tiles = q_ref.shape[0], k_ref.shape[0] // LANES
    values_t = jnp.transpose(v_ref[...].astype(f32))
    outs = [[] for _ in range(rows // block)]
    for head in range(2):
        fill_bias(offsets_ref, head, bias_tile)
        keys = masked_keys(k_ref[...], head, length)
        values_h = jnp.where(head_lanes(values_t.shape, 0, head), values_t, 1.0).astype(bf16)
        for b in range(rows // block):
            rs = slice(b * block, (b + 1) * block)
            scores = dot_nt(keys, flagged(q_ref[rs, :], head))
            scores = scores + bias_columns(bias_tile, row0 + b * block, block, key_tiles)
            top = jnp.max(scores, axis=0, keepdims=True)
            weights = jnp.exp(scores - top).astype(bf16)
            mixed_t = dot(values_h, weights)
            total = mixed_t[flag_lane(head) : flag_lane(head) + 1]
            mine = mixed_t[:DH] if head == 0 else mixed_t[DH:]
            outs[b].append(mine / total)
            lse_ref[0, head : head + 1, rs] = top + jnp.log(total)
    for b in range(rows // block):
        joined = jnp.transpose(jnp.concatenate(outs[b], axis=0))
        out_ref[b * block : (b + 1) * block, :] = joined.astype(bf16)


def attend(scal, half, queries, keys, values, offsets):
    rows, width = queries.shape[1:]
    seq_len, pairs, span = keys.shape[0], width // PAIR, offsets.shape[2]
    block = min(512, rows)
    tokens_spec = pl.BlockSpec((rows, PAIR), lambda g, s: (0, g))
    keys_spec = pl.BlockSpec((seq_len, PAIR), lambda g, s: (0, g))
    work = rows * seq_len * width
    return pl.pallas_call(
        functools.partial(attend_body, block),
        out_shape=(
            jax.ShapeDtypeStruct((rows, width), bf16),
            jax.ShapeDtypeStruct((pairs, 2, rows), f32),
        ),
        grid_spec=pltpu.PrefetchScalarGridSpec(
            num_scalar_prefetch=1,
            grid=(pairs,),
            in_specs=[
                pl.BlockSpec((pl.Squeezed(), rows, PAIR), lambda g, s: (half, 0, g)),
                keys_spec,
                keys_spec,
                pl.BlockSpec((1, 2, span), lambda g, s: (g, 0, 0)),
            ],
            out_specs=[tokens_spec, pl.BlockSpec((1, 2, rows), lambda g, s: (g, 0, 0))],
            scratch_shapes=[pltpu.VMEM((LANES, span), f32)],
        ),
        compiler_params=pltpu.CompilerParams(vmem_limit_bytes=32 * MiB),
        cost_estimate=pl.CostEstimate(
            flops=16 * work, transcendentals=work // DH, bytes_accessed=4 * seq_len * width
        ),
        name="attend",
    )(scal, queries, keys, values, offsets)


def diagonal_sums(tile):
    span = tile.shape[1]
    size = tile.shape[0] // 2
    while size >= 8:
        tile = tile[:size] + pltpu.roll(tile[size:], span - size, 1)
        size //= 2
    row = lax.broadcasted_iota(jnp.int32, tile.shape, 0)
    for bit in (1, 2, 4):
        tile = jnp.where((row & bit) != 0, pltpu.roll(tile, span - bit, 1), tile)
    return jnp.sum(tile, axis=0, keepdims=True)


def attend_back_body(block, carry, scal, *refs):
    q_ref, k_ref, v_ref, g_ref, o_ref, lse_ref, offsets_ref = refs[:7]
    dq_ref, dk_ref, dv_ref, diag_ref, bias_tile, diag_tile, dk_sum, dv_sum = refs[-8:]
    row0, length = scal[0], scal[1]
    rows, key_tiles = q_ref.shape[0], k_ref.shape[0] // LANES
    if carry:
        dk_sum[...] = refs[7][...]
        dv_sum[...] = refs[8][...]
    else:
        dk_sum[...] = jnp.zeros_like(dk_sum)
        dv_sum[...] = jnp.zeros_like(dv_sum)
    keys_t = jnp.transpose(k_ref[...].astype(f32)).astype(bf16)
    count = rows // block
    dqs = [[] for _ in range(count)]
    deltas = []
    for b in range(count):
        rs = slice(b * block, (b + 1) * block)
        product = jnp.transpose(g_ref[rs, :].astype(f32) * o_ref[rs, :].astype(f32))
        deltas.append(
            (
                jnp.sum(product[:DH], axis=0, keepdims=True),
                jnp.sum(product[DH:], axis=0, keepdims=True),
            )
        )
    for head in range(2):
        fill_bias(offsets_ref, head, bias_tile)
        diag_tile[...] = jnp.zeros_like(diag_tile)
        keys = masked_keys(k_ref[...], head, length)
        for b in range(count):
            rs = slice(b * block, (b + 1) * block)
            queries = q_ref[rs, :]
            grads = only_head(g_ref[rs, :], head)
            scores = dot_nt(keys, flagged(queries, head))
            scores = scores + bias_columns(bias_tile, row0 + b * block, block, key_tiles)
            probs = jnp.exp(scores - lse_ref[0, head : head + 1, rs])
            grad_probs = dot_nt(v_ref[...], grads)
            grad_scores = probs * (grad_probs - deltas[b][head])
            for tile in range(key_tiles):
                start = aligned((key_tiles - 1 - tile) * LANES + row0 + b * block, LANES)
                diag_tile[:, pl.ds(start, block)] += grad_scores[tile * LANES : (tile + 1) * LANES]
            grad_scores = grad_scores.astype(bf16)
            dv_sum[...] += dot(probs.astype(bf16), grads)
            dk_sum[...] += dot(grad_scores, only_head(queries, head))
            dq_t = dot(keys_t, grad_scores)
            dqs[b].append(dq_t[:DH] if head == 0 else dq_t[DH:])
        diag_ref[0, head : head + 1, :] = diagonal_sums(diag_tile[...])
    for b in range(count):
        joined = jnp.transpose(jnp.concatenate(dqs[b], axis=0))
        dq_ref[b * block : (b + 1) * block, :] = joined.astype(bf16)
    dk_ref[...] = dk_sum[...].astype(dk_ref.dtype)
    dv_ref[...] = dv_sum[...].astype(dv_ref.dtype)


def attend_back(scal, half, queries, keys, values, grads, outs, lse, offsets, carry):
    rows, width = queries.shape[1:]
    seq_len, pairs, span = keys.shape[0], width // PAIR, offsets.shape[2]
    block = min(256, rows)
    rows_spec = pl.BlockSpec((rows, PAIR), lambda g, s: (0, g))
    keys_spec = pl.BlockSpec((seq_len, PAIR), lambda g, s: (0, g))
    offsets_spec = pl.BlockSpec((1, 2, span), lambda g, s: (g, 0, 0))
    specs = [
        pl.BlockSpec((pl.Squeezed(), rows, PAIR), lambda g, s: (half, 0, g)),
        keys_spec,
        keys_spec,
        rows_spec,
        rows_spec,
        pl.BlockSpec((1, 2, rows), lambda g, s: (g, 0, 0)),
        offsets_spec,
    ]
    kind = f32
    if carry:
        specs += [keys_spec, keys_spec]
        kind = bf16
    work = rows * seq_len * width
    return pl.pallas_call(
        functools.partial(attend_back_body, block, bool(carry)),
        out_shape=(
            jax.ShapeDtypeStruct((rows, width), bf16),
            jax.ShapeDtypeStruct((seq_len, width), kind),
            jax.ShapeDtypeStruct((seq_len, width), kind),
            jax.ShapeDtypeStruct(offsets.shape, f32),
        ),
        grid_spec=pltpu.PrefetchScalarGridSpec(
            num_scalar_prefetch=1,
            grid=(pairs,),
            in_specs=specs,
            out_specs=[rows_spec, keys_spec, keys_spec, offsets_spec],
            scratch_shapes=[
                pltpu.VMEM((LANES, span), f32),
                pltpu.VMEM((LANES, span), f32),
                pltpu.VMEM((seq_len, PAIR), f32),
                pltpu.VMEM((seq_len, PAIR), f32),
            ],
        ),
        compiler_params=pltpu.CompilerParams(vmem_limit_bytes=32 * MiB),
        cost_estimate=pl.CostEstimate(
            flops=40 * work, transcendentals=work // DH, bytes_accessed=12 * seq_len * width
        ),
        name="attend_back",
    )(scal, queries, keys, values, grads, outs, lse, offsets, *carry)


def normed_rows(values, gain_row):
    inverse = lax.rsqrt(jnp.mean(values * values, axis=-1, keepdims=True) + epsilon)
    return values * inverse * gain_row, inverse


def project_body(
    scal, own_ref, peer_ref, w0_ref, w1_ref, normed_ref, q_ref, k_ref, v_ref, w_ref, gain_ref, gain_row
):
    own_p = scal[2]
    side, step = pl.program_id(0), pl.program_id(1)
    rows, width = w0_ref.shape[1], q_ref.shape[1]

    @pl.when((side == 0) & (step == 0))
    def gather_weights():
        for core, piece in enumerate((w0_ref, w1_ref)):
            for index in range(BLOCKS // 2):
                part = ((index << 1) | core) ^ own_p
                start = aligned(part * rows, 16)
                w_ref[pl.ds(start, rows), :] = piece[index, :, : 3 * width]
                gain_ref[pl.ds(start, rows), :] = piece[index, :, 3 * width :].astype(f32)
        gain_row[...] = jnp.transpose(gain_ref[...])[0:8, :]

    values = jnp.where(side == 0, own_ref[...].astype(f32), peer_ref[...].astype(f32))
    normed = normed_rows(values, gain_row[0:1, :])[0].astype(bf16)
    normed_ref[...] = normed
    made = dot(normed, w_ref[...]).astype(bf16)
    q_ref[...] = made[:, :width]
    k_ref[...] = made[:, width : 2 * width]
    v_ref[...] = made[:, 2 * width :]


def project(scal, own, peer, pieces, width):
    rows, depth = own.shape
    block = min(256, rows)
    steps = rows // block
    whole = pl.BlockSpec(pieces[0].shape, lambda h, b, s: (0, 0, 0))
    by_half = pl.BlockSpec((pl.Squeezed(), block, width), lambda h, b, s: (h, b, 0))
    by_place = pl.BlockSpec((pl.Squeezed(), block, width), lambda h, b, s: (h ^ s[3], b, 0))
    stacked = jax.ShapeDtypeStruct((2, rows, width), bf16)
    return pl.pallas_call(
        project_body,
        out_shape=(
            jax.ShapeDtypeStruct((2, rows, depth), bf16),
            stacked,
            stacked,
            stacked,
            jax.ShapeDtypeStruct((depth, 3 * width), bf16),
            jax.ShapeDtypeStruct((depth, LANES), f32),
        ),
        grid_spec=pltpu.PrefetchScalarGridSpec(
            num_scalar_prefetch=1,
            grid=(2, steps),
            in_specs=[
                pl.BlockSpec((block, depth), lambda h, b, s: (b * (1 - h) + (steps - 1) * h, 0)),
                pl.BlockSpec((block, depth), lambda h, b, s: (b * h, 0)),
                whole,
                whole,
            ],
            out_specs=[
                pl.BlockSpec((pl.Squeezed(), block, depth), lambda h, b, s: (h, b, 0)),
                by_half,
                by_place,
                by_place,
                pl.BlockSpec((depth, 3 * width), lambda h, b, s: (0, 0)),
                pl.BlockSpec((depth, LANES), lambda h, b, s: (0, 0)),
            ],
            scratch_shapes=[pltpu.VMEM((8, depth), f32)],
        ),
        compiler_params=pltpu.CompilerParams(vmem_limit_bytes=60 * MiB),
        cost_estimate=pl.CostEstimate(
            flops=12 * rows * depth * width, transcendentals=0, bytes_accessed=10 * rows * depth
        ),
        name="project",
    )(scal, own, peer, *pieces)


def gelu_parts(values):
    scale = 0.7978845608028654
    square = values * values
    bend = jnp.tanh(scale * (values + 0.044715 * (values * square)))
    half = 0.5 * (1.0 + bend)
    slope = half + (0.5 * scale) * values * (1.0 - bend * bend) * (1.0 + 0.134145 * square)
    return values * half, slope


def bits_of(rel):
    return rel & 1, (rel >> 1) & 1, (rel >> 2) & 1, (rel >> 3) & 1, rel >> 4


def place_of(rel, leading):
    side, _, mid, low, high = bits_of(rel)
    if leading:
        return (mid << 1) | side, (high << 1) | low
    return (mid << 1) | low, (side << 1) | high


def zone_of(rel, zone, leading):
    side, _, mid, low, _ = bits_of(rel)
    if leading:
        return (mid << 1) | side, (zone << 1) + low
    return (mid << 1) | low, (side << 1) + zone


def assemble_rows(pieces, first_column, target, own_p, me):
    half = target.shape[1] // 2
    shard = pieces[0].shape[2]
    for rel in range(2 * BLOCKS):
        side, core = rel & 1, (rel >> 1) & 1
        plane, level = place_of(rel, True)
        row = aligned(((rel >> 1) ^ own_p) * shard, 16)
        column = aligned((side ^ me) * half, LANES)
        source = pieces[core][plane, level, :, pl.ds(first_column, half)]
        target[pl.ds(row, shard), pl.ds(column, half)] = source


def feed_body(leading, direct, scal, *refs):
    refs = list(refs)
    take = lambda count: [refs.pop(0) for _ in range(count)]
    if leading:
        tok_ref, cot_ref, mine_ref, theirs_ref, gain_ref = take(5)
    else:
        rows_in, mid_in, nff_in, out_in, grad_in, mix_in, wo_in, gain_ref = take(8)
    if direct:
        wo_ref = take(1)[0] if leading else None
        wi_ref, *wb_refs = take(3)
    else:
        pieces = take(2)
    if leading:
        rows_s, mid_s, nff_s, out_s, nff_grad, mix_s, wo_s = take(7)
    else:
        out_ref, mid_grad_ref, mix_own_ref, mix_peer_ref, gain_grad_ref = take(5)
    keep_ref, send_ref = take(2)
    if not leading:
        rows_s, mid_s, nff_s, mix_s, wo_s = rows_in, mid_in, nff_in, mix_in, wo_in
        out_s, nff_grad = take(2)
    nff_t, wi_s, wb_s, total = take(4)
    row0, length, own_p, me = scal[0], scal[1], scal[2], scal[3]
    own_r = own_p * 2 + me
    step = pl.program_id(0)
    rows, depth = rows_s.shape
    half = depth // 2
    steps, skip = 2, 1 if leading else 0
    count = depth // (2 * BLOCKS)
    gain_row = jnp.transpose(gain_ref[...])[1:2, :]

    def store_rows(column):
        for rel in range(2 * BLOCKS):
            start = aligned((rel ^ own_r) * count, 8)
            plane, level = place_of(rel, leading)
            target = send_ref if (rel >> 1) & 1 else keep_ref
            piece = total[pl.ds(start, count), :].astype(bf16)
            target[plane, level, :, pl.ds(column, depth)] = piece

    @pl.when(step == 0)
    def start():
        if leading:
            if direct:
                wo_s[...] = wo_ref[...]
            else:
                assemble_rows(pieces, 0, wo_s, own_p, me)
            mix_s[:, pl.ds(aligned(me * half, LANES), half)] = mine_ref[...]
            mix_s[:, pl.ds(aligned((1 - me) * half, LANES), half)] = theirs_ref[...]
            middle = tok_ref[...].astype(f32) + dot(mix_s[...], wo_s[...])
            mid_s[...] = middle
            nff_s[...] = normed_rows(middle, gain_row)[0].astype(bf16)
            position = row0 + lax.broadcasted_iota(jnp.int32, (rows, depth), 0)
            rows_s[...] = jnp.where(position < length, cot_ref[...].astype(f32), 0.0).astype(bf16)
            out_s[...] = middle
            nff_grad[...] = jnp.zeros_like(nff_grad)
        else:
            out_s[...] = out_in[...]
            nff_grad[...] = grad_in[...]
        nff_t[...] = jnp.transpose(nff_s[...].astype(f32)).astype(bf16)

    def hidden_block():
        shard = depth // BLOCKS
        if direct:
            wi_s[...] = wi_ref[...]
            for part in range(BLOCKS // 2):
                for side in range(2):
                    row = (2 * part + side) * shard
                    wb_s[row : row + shard, :] = wb_refs[side][part * shard : (part + 1) * shard, :]
        else:
            assemble_rows(pieces, aligned((skip + step) * half, LANES), wi_s, own_p, me)
            zone = step ^ (own_p >> 3)
            for rel in range(BLOCKS):
                plane, level = zone_of(rel, zone, True)
                column = aligned(((rel & 1) ^ me) * half, LANES)
                for side in range(2):
                    column_in = (skip + 2 + side) * half
                    source = pieces[(rel >> 1) & 1][plane, level, :, column_in : column_in + half]
                    row = aligned((2 * ((rel >> 1) ^ (own_p & 7)) + side) * shard, 16)
                    wb_s[pl.ds(row, shard), pl.ds(column, half)] = source
        pre = dot(nff_s[...], wi_s[...])
        hidden, slope = gelu_parts(pre)
        hidden = hidden.astype(bf16)
        out_s[...] += dot(hidden, wb_s[...])
        pre_grad = (dot_nt(rows_s[...], wb_s[...]) * slope).astype(bf16)
        total[...] = dot_tn(hidden, rows_s[...])
        zone = step ^ (own_p >> 3)
        for rel in range(BLOCKS):
            plane, level = zone_of(rel, zone, leading)
            target = send_ref if (rel >> 1) & 1 else keep_ref
            for side in range(2):
                row = aligned((rel ^ (own_r & 15)) * (2 * count) + side * count, 8)
                piece = total[pl.ds(row, count), :].astype(bf16)
                column = (steps + side) * depth
                target[plane, level, :, column : column + depth] = piece
        nff_grad[...] += dot_nt(pre_grad, wi_s[...])
        total[...] = dot(nff_t[...], pre_grad)
        store_rows(aligned(step * depth, LANES))

    if leading:
        hidden_block()
        return
    pl.when(step < steps)(hidden_block)

    @pl.when(step == steps)
    def finish():
        out_ref[...] = out_s[...].astype(bf16)
        middle = mid_s[...]
        inverse = lax.rsqrt(jnp.mean(middle * middle, axis=-1, keepdims=True) + epsilon)
        grads = nff_grad[...]
        gain_sum = jnp.sum(grads * middle * inverse, axis=0, keepdims=True)
        gain_grad_ref[...] = jnp.broadcast_to(gain_sum, gain_grad_ref.shape)
        scaled = grads * gain_row
        inner = jnp.sum(scaled * middle, axis=-1, keepdims=True)
        mid_grad = (
            rows_s[...].astype(f32)
            + inverse * scaled
            - middle * (inverse * inverse * inverse) * (inner / depth)
        )
        mid_grad_ref[...] = mid_grad
        attn_grad = mid_grad.astype(bf16)
        total[...] = dot_tn(mix_s[...], attn_grad)
        store_rows((steps + 2) * depth)
        turned = dot_nt(attn_grad, wo_s[...])
        first, second = turned[:, :half], turned[:, half:]
        mix_own_ref[...] = jnp.where(me == 0, first, second).astype(bf16)
        mix_peer_ref[...] = jnp.where(me == 0, second, first).astype(bf16)


def fixed(*shape):
    return pl.BlockSpec(shape, lambda *_: (0,) * len(shape), pipeline_mode=pl.Buffered(1))


def direct_specs(depth, skip):
    by_step = lambda f: jnp.minimum(f, 1)
    in_spec = pl.BlockSpec((depth, depth), lambda f, s: (0, by_step(f) + skip))
    low_spec = pl.BlockSpec((depth // 2, depth), lambda f, s: (by_step(f), 2 + skip))
    high_spec = pl.BlockSpec((depth // 2, depth), lambda f, s: (by_step(f), 3 + skip))
    return [fixed(depth, depth)] * skip + [in_spec, low_spec, high_spec]


def feed_call(leading, direct, scal, inputs, in_specs, outputs, chunk, scratch, name):
    rows, depth = outputs[0][0]
    count = depth // (2 * BLOCKS)
    sums = jax.ShapeDtypeStruct((4, 4, count, chunk * depth), bf16)
    return pl.pallas_call(
        functools.partial(feed_body, leading, direct),
        out_shape=[jax.ShapeDtypeStruct(*o) for o in outputs] + [sums] * 2,
        grid_spec=pltpu.PrefetchScalarGridSpec(
            num_scalar_prefetch=1,
            grid=(2 if leading else 3,),
            in_specs=in_specs,
            out_specs=[fixed(*o[0]) for o in outputs] + [fixed(*sums.shape)] * 2,
            scratch_shapes=scratch
            + [
                pltpu.VMEM((depth, rows), bf16),
                pltpu.VMEM((depth, depth), bf16),
                pltpu.VMEM((depth, depth), bf16),
                pltpu.VMEM((depth, depth), f32),
            ],
        ),
        compiler_params=pltpu.CompilerParams(vmem_limit_bytes=40 * MiB),
        cost_estimate=pl.CostEstimate(
            flops=24 * rows * depth * depth,
            transcendentals=2 * rows * depth,
            bytes_accessed=20 * MiB,
        ),
        name=name,
    )(scal, *inputs)


def feed_first(scal, tokens, cotangent, mine, theirs, gains, weights, direct):
    rows, depth = tokens.shape
    inputs = [tokens, cotangent, mine, theirs, gains]
    specs = [fixed(*v.shape) for v in inputs]
    if direct:
        inputs += [weights] * 4
        specs += direct_specs(depth, 1)
    else:
        inputs += weights
        specs += [fixed(*w.shape) for w in weights]
    whole = [(rows, depth)] * 6 + [(depth, depth)]
    outputs = list(zip(whole, [bf16, f32, bf16, f32, f32, bf16, bf16]))
    return feed_call(True, direct, scal, inputs, specs, outputs, 4, [], "feed_first")


def feed_second(scal, state, gains, weights, direct):
    rows, depth = state[0].shape
    half = depth // 2
    inputs = list(state) + [gains]
    specs = [fixed(*v.shape) for v in inputs]
    if direct:
        inputs += [weights] * 3
        specs += direct_specs(depth, 0)
    else:
        inputs += weights
        specs += [fixed(*w.shape) for w in weights]
    whole = [(rows, depth), (rows, depth), (rows, half), (rows, half), (8, depth)]
    outputs = list(zip(whole, [bf16, f32, bf16, bf16, f32]))
    scratch = [pltpu.VMEM((rows, depth), f32)] * 2
    return feed_call(False, direct, scal, inputs, specs, outputs, 5, scratch, "feed_second")


def weight_back_body(
    scal, normed_ref, dq0_ref, dq1_ref, dk_ref, dv_ref, w_ref, gain_ref, ff_ref, table_ref,
    keep_ref, away_ref, total
):
    own_p, me = scal[2], scal[3]
    rows, width = dq0_ref.shape
    depth = w_ref.shape[0]
    near, far = aligned(me * rows, 16), aligned((1 - me) * rows, 16)
    for i, ref in enumerate((None, dk_ref, dv_ref)):
        own = dq0_ref[...] if ref is None else ref[pl.ds(near, rows), :]
        peer = dq1_ref[...] if ref is None else ref[pl.ds(far, rows), :]
        total[:, i * width : (i + 1) * width] = dot_tn(normed_ref[0], own) + dot_tn(normed_ref[1], peer)
    weighted = jnp.sum(total[:, : 3 * width] * w_ref[...].astype(f32), axis=1, keepdims=True)
    lane = lax.broadcasted_iota(jnp.int32, (depth, LANES), 1)
    gains = jnp.where(lane == 0, weighted / gain_ref[:, 0:1], 0.0)
    ff_gain = jnp.transpose(jnp.broadcast_to(ff_ref[0:1, :], (LANES, depth)))
    total[:, 3 * width :] = jnp.where(lane == 1, ff_gain, gains)
    shard = depth // BLOCKS
    for rel in range(BLOCKS):
        start = aligned((rel ^ own_p) * shard, 16)
        whole = jnp.concatenate(
            [
                total[pl.ds(start, shard), : 3 * width],
                total[pl.ds(start, shard), 3 * width :] + table_ref[...],
            ],
            axis=1,
        )
        target = away_ref if rel & 1 else keep_ref
        mid, low, high = (rel >> 1) & 1, (rel >> 2) & 1, rel >> 3
        target[(mid << 1) | low, high] = whole.astype(bf16)


def weight_back(scal, normed, dq_own, dq_peer, dk, dv, weights, gains, ff_gain, table):
    rows, width = dq_own.shape
    depth = weights.shape[0]
    shard = depth // BLOCKS
    inputs = [normed, dq_own, dq_peer, dk, dv, weights, gains, ff_gain, table]
    shape = (4, 2, shard, 3 * width + LANES)
    return pl.pallas_call(
        weight_back_body,
        out_shape=[jax.ShapeDtypeStruct(shape, bf16)] * 2,
        grid_spec=pltpu.PrefetchScalarGridSpec(
            num_scalar_prefetch=1,
            grid=(1,),
            in_specs=[fixed(*v.shape) for v in inputs],
            out_specs=[fixed(*shape)] * 2,
            scratch_shapes=[pltpu.VMEM((depth, 3 * width + LANES), f32)],
        ),
        compiler_params=pltpu.CompilerParams(vmem_limit_bytes=24 * MiB),
        cost_estimate=pl.CostEstimate(
            flops=12 * rows * depth * width, transcendentals=0, bytes_accessed=16 * MiB
        ),
        name="weight_back",
    )(scal, *inputs)


def project_back_body(scal, dq0_ref, dq1_ref, dk_ref, dv_ref, w_ref, own_ref, send_ref, joined):
    side = pl.program_id(0)
    width = dq0_ref.shape[1]
    joined[:, :width] = jnp.where(side == 0, dq1_ref[...].astype(f32), dq0_ref[...].astype(f32)).astype(bf16)
    joined[:, width : 2 * width] = dk_ref[...]
    joined[:, 2 * width :] = dv_ref[...]
    grads = dot_nt(joined[...], w_ref[...])

    @pl.when(side == 0)
    def outgoing():
        send_ref[...] = grads.astype(bf16)

    @pl.when(side == 1)
    def staying():
        own_ref[...] = grads


def project_back(scal, dq_own, dq_peer, dk, dv, weights):
    rows, width = dq_own.shape
    depth = weights.shape[0]
    place = pl.BlockSpec((rows, width), lambda h, s: (1 - h ^ s[3], 0))
    return pl.pallas_call(
        project_back_body,
        out_shape=(
            jax.ShapeDtypeStruct((rows, depth), f32),
            jax.ShapeDtypeStruct((rows, depth), bf16),
        ),
        grid_spec=pltpu.PrefetchScalarGridSpec(
            num_scalar_prefetch=1,
            grid=(2,),
            in_specs=[
                fixed(rows, width),
                fixed(rows, width),
                place,
                place,
                fixed(depth, 3 * width),
            ],
            out_specs=[fixed(rows, depth), fixed(rows, depth)],
            scratch_shapes=[pltpu.VMEM((rows, 3 * width), bf16)],
        ),
        compiler_params=pltpu.CompilerParams(vmem_limit_bytes=16 * MiB),
        cost_estimate=pl.CostEstimate(
            flops=12 * rows * depth * width, transcendentals=0, bytes_accessed=8 * MiB
        ),
        name="project_back",
    )(scal, dq_own, dq_peer, dk, dv, weights)


def last_body(tok_ref, mid_ref, own_ref, come_ref, gain_ref, out_ref):
    depth = tok_ref.shape[1]
    gain_row = jnp.transpose(gain_ref[...])[0:1, :]
    values = tok_ref[...].astype(f32)
    inverse = lax.rsqrt(jnp.mean(values * values, axis=-1, keepdims=True) + epsilon)
    scaled = (own_ref[...] + come_ref[...].astype(f32)) * gain_row
    inner = jnp.sum(scaled * values, axis=-1, keepdims=True)
    grads = inverse * scaled - values * (inverse * inverse * inverse) * (inner / depth)
    out_ref[...] = (mid_ref[...] + grads).astype(bf16)


def last(tokens, mid_grad, own, come, gains):
    rows, depth = tokens.shape
    block = min(256, rows)
    spec = pl.BlockSpec((block, depth), lambda b: (b, 0))
    return pl.pallas_call(
        last_body,
        out_shape=jax.ShapeDtypeStruct((rows, depth), bf16),
        grid=(rows // block,),
        in_specs=[spec, spec, spec, spec, pl.BlockSpec((depth, LANES), lambda b: (0, 0))],
        out_specs=spec,
        compiler_params=pltpu.CompilerParams(vmem_limit_bytes=60 * MiB),
        cost_estimate=pl.CostEstimate(
            flops=16 * rows * depth, transcendentals=0, bytes_accessed=12 * rows * depth
        ),
        name="last",
    )(tokens, mid_grad, own, come, gains)


def chosen(me, low, high):
    return jnp.where(me == 0, low.astype(f32), high.astype(f32)).astype(low.dtype)


def column_of(row):
    count = row.shape[1]
    square = lax.broadcasted_iota(jnp.int32, (count, count), 0)
    other = lax.broadcasted_iota(jnp.int32, (count, count), 1)
    return jnp.sum(jnp.where(square == other, row.astype(f32), 0.0), axis=1, keepdims=True)


def ready_first_body(scal, q_ref, k_ref, v_ref, attn_ref, ff_ref, out_ref):
    me = scal[3]
    width = q_ref.shape[1] // 2
    for i, ref in enumerate((q_ref, k_ref, v_ref)):
        half = chosen(me, ref[:, :width], ref[:, width:])
        out_ref[:, i * width : (i + 1) * width] = half
    lane = lax.broadcasted_iota(jnp.int32, (q_ref.shape[0], LANES), 1)
    gains = jnp.where(lane == 0, column_of(attn_ref[...]), 0.0)
    gains = jnp.where(lane == 1, column_of(ff_ref[...]), gains)
    out_ref[:, 3 * width :] = gains.astype(bf16)


def ready_first(scal, w_query, w_key, w_value, gain_attn, gain_ff):
    rows, depth = w_query.shape
    inputs = [w_query, w_key, w_value, gain_attn[None], gain_ff[None]]
    shape = (rows, 3 * (depth // 2) + LANES)
    return pl.pallas_call(
        ready_first_body,
        out_shape=jax.ShapeDtypeStruct(shape, bf16),
        grid_spec=pltpu.PrefetchScalarGridSpec(
            num_scalar_prefetch=1,
            grid=(1,),
            in_specs=[fixed(*v.shape) for v in inputs],
            out_specs=fixed(*shape),
        ),
        compiler_params=pltpu.CompilerParams(vmem_limit_bytes=60 * MiB),
        name="ready_first",
    )(scal, *inputs)


def ready_rest_body(scal, out_ref, in_ref, back_ref, one_ref, two_ref):
    me = scal[3]
    depth = out_ref.shape[1]
    half = depth // 2
    shard = back_ref.shape[0] // 4
    columns = in_ref[...].astype(f32)
    step = columns.shape[1] // (4 * BLOCKS)
    chunks = []
    for chunk in range(2):
        pieces = [columns[:, (2 * r + chunk) * step : (2 * r + chunk + 1) * step] for r in range(2 * BLOCKS)]
        chunks.append(jnp.concatenate(pieces, axis=1).astype(bf16))
    one_ref[:, :half] = chosen(me, out_ref[:, :half], out_ref[:, half:])
    for f in range(2):
        block = chunks[0][:, f * depth : (f + 1) * depth]
        one_ref[:, (f + 1) * half : (f + 2) * half] = chosen(me, block[:, :half], block[:, half:])
        block = chunks[1][:, f * depth : (f + 1) * depth]
        two_ref[:, f * half : (f + 1) * half] = chosen(me, block[:, :half], block[:, half:])
    for side in range(2):
        rows = back_ref[2 * side * shard : (2 * side + 1) * shard, :]
        one_ref[:, (side + 3) * half : (side + 4) * half] = chosen(me, rows[:, :half], rows[:, half:])
        rows = back_ref[(2 * side + 1) * shard : (2 * side + 2) * shard, :]
        two_ref[:, (side + 2) * half : (side + 3) * half] = chosen(me, rows[:, :half], rows[:, half:])


def ready_rest(scal, w_out, w_in, w_back):
    rows, depth = w_out.shape
    inputs = [w_out, w_in, w_back]
    shapes = [(rows, 5 * depth // 2), (rows, 2 * depth)]
    return pl.pallas_call(
        ready_rest_body,
        out_shape=[jax.ShapeDtypeStruct(s, bf16) for s in shapes],
        grid_spec=pltpu.PrefetchScalarGridSpec(
            num_scalar_prefetch=1,
            grid=(1,),
            in_specs=[fixed(*v.shape) for v in inputs],
            out_specs=[fixed(*s) for s in shapes],
        ),
        compiler_params=pltpu.CompilerParams(vmem_limit_bytes=60 * MiB),
        name="ready_rest",
    )(scal, *inputs)


def summed_refs(refs, start, stop):
    total = refs[0][:, start:stop].astype(f32)
    for ref in refs[1:]:
        total = total + ref[:, start:stop].astype(f32)
    return total


def place_grads_body(count_one, *refs):
    one_refs, two_refs = refs[:count_one], refs[count_one:-3]
    in_ref, back_ref, out_ref = refs[-3:]
    rows, depth = out_ref.shape
    parts = [summed_refs(r, 0, 2 * depth) for r in (one_refs, two_refs)]
    step = 2 * depth // (2 * BLOCKS)
    pieces = []
    for r in range(2 * BLOCKS):
        for part in parts:
            pieces.append(part[:, r * step : (r + 1) * step])
    in_ref[...] = jnp.concatenate(pieces, axis=1)
    for chunk, r in enumerate((one_refs, two_refs)):
        for side in range(2):
            row = (2 * chunk + side) * rows
            back_ref[row : row + rows, :] = summed_refs(r, (2 + side) * depth, (3 + side) * depth)
    out_ref[...] = summed_refs(two_refs, 4 * depth, 5 * depth)


def place_grads(one_parts, two_parts, depth):
    rows = one_parts[0].shape[0]
    inputs = one_parts + two_parts
    shapes = [(rows, 4 * depth), (4 * rows, depth), (rows, depth)]
    return pl.pallas_call(
        functools.partial(place_grads_body, len(one_parts)),
        out_shape=[jax.ShapeDtypeStruct(s, f32) for s in shapes],
        grid=(1,),
        in_specs=[fixed(*v.shape) for v in inputs],
        out_specs=[fixed(*s) for s in shapes],
        compiler_params=pltpu.CompilerParams(vmem_limit_bytes=16 * MiB),
        name="place_grads",
    )(*inputs)


def halve_first_body(column, scal, *refs):
    me = scal[3]
    parts, (mine_ref, theirs_ref, table_ref) = refs[:-3], refs[-3:]
    total = summed_refs(parts, 0, parts[0].shape[1])
    rows = total.shape[0] // 2
    mine_ref[...] = jnp.where(me == 0, total[:rows], total[rows:])
    theirs_ref[...] = jnp.where(me == 0, total[rows:], total[:rows])
    table_ref[...] = total[: table_ref.shape[0], column : column + table_ref.shape[1]]


def halve_first(scal, parts, buckets, heads):
    rows, wide = parts[0].shape
    shapes = [(rows // 2, wide), (rows // 2, wide), (buckets, heads)]
    return pl.pallas_call(
        functools.partial(halve_first_body, wide - LANES + 2),
        out_shape=[jax.ShapeDtypeStruct(s, f32) for s in shapes],
        grid_spec=pltpu.PrefetchScalarGridSpec(
            num_scalar_prefetch=1,
            grid=(1,),
            in_specs=[fixed(*v.shape) for v in parts],
            out_specs=[fixed(*s) for s in shapes],
        ),
        compiler_params=pltpu.CompilerParams(vmem_limit_bytes=16 * MiB),
        name="halve_first",
    )(scal, *parts)


def place_first_body(scal, mine_ref, theirs_ref, *out_refs):
    me = scal[3]
    width = out_refs[0].shape[1] // 2
    for i, ref in enumerate(out_refs[:3]):
        mine = mine_ref[:, i * width : (i + 1) * width]
        theirs = theirs_ref[:, i * width : (i + 1) * width]
        ref[:, :width] = jnp.where(me == 0, mine, theirs)
        ref[:, width:] = jnp.where(me == 0, theirs, mine)
    gains = mine_ref[:, 3 * width :] + theirs_ref[:, 3 * width :]
    rows = gains.shape[0]
    square = lax.broadcasted_iota(jnp.int32, (rows, rows), 0)
    other = lax.broadcasted_iota(jnp.int32, (rows, rows), 1)
    for i in range(2):
        spread_out = jnp.where(square == other, gains[:, i : i + 1], 0.0)
        out_refs[3 + i][...] = jnp.sum(spread_out, axis=0, keepdims=True)


def place_first(scal, mine, theirs):
    rows, wide = mine.shape
    depth = (wide - LANES) // 3 * 2
    shapes = [(rows, depth)] * 3 + [(1, rows)] * 2
    return pl.pallas_call(
        place_first_body,
        out_shape=[jax.ShapeDtypeStruct(s, f32) for s in shapes],
        grid_spec=pltpu.PrefetchScalarGridSpec(
            num_scalar_prefetch=1,
            grid=(1,),
            in_specs=[fixed(*mine.shape)] * 2,
            out_specs=[fixed(*s) for s in shapes],
        ),
        compiler_params=pltpu.CompilerParams(vmem_limit_bytes=16 * MiB),
        name="place_first",
    )(scal, mine, theirs)


def hop(value, mask):
    size = lax.axis_size("dp") * 2
    return lax.ppermute(value, ("dp", "seq"), [(i, i ^ mask) for i in range(size)])


def tied(*values):
    return lax.optimization_barrier(values)


LEVELS = (8, 16, 24)
PLANES = (1, 4, 5)
HEIGHTS = (8, 4, 12)
ENDS = (16, 1, 17)
CORE = 2


def spread(value, masks):
    return [hop(value, mask) for mask in masks]


def total_of(parts, kind):
    total = parts[0].astype(f32)
    for part in parts[1:]:
        total = total + part.astype(f32)
    return total.astype(kind)


def scatter_sums(parts, masks):
    sums = [total_of([p[i] for p in parts], bf16) for i in range(len(masks) + 1)]
    return sums[0], [hop(s, m) for s, m in zip(sums[1:], masks)]


def planes_of(mine, come):
    first = jnp.stack([mine[0], come[0]], axis=1)
    second = jnp.stack([mine[1], come[1]])
    parts = [v.reshape((4,) + v.shape[2:]) for v in (first, second)]
    return jnp.concatenate(parts, axis=1)


def whole_gather(shard):
    return lax.all_gather(shard, "dp", axis=0, tiled=True)


def join_grid(keep, send, axes):
    both = jnp.stack([keep, send])
    both = both.reshape((2,) * (len(axes) + 1) + both.shape[-2:])
    axes = ("c",) + axes
    order = ("z2", "z1", "y", "c") + (("x",) if "x" in axes else ())
    both = both.transpose([axes.index(n) for n in order] + [both.ndim - 2, both.ndim - 1])
    if "x" in axes:
        both = jnp.where(lax.axis_index("seq") == 1, jnp.flip(both, 4), both)
    return both.astype(f32)


def chunk_columns(weight, chunk):
    rows, hidden = weight.shape
    grid = weight.reshape(rows, BLOCKS * 2, 2, hidden // (4 * BLOCKS))
    return grid[:, :, chunk].reshape(rows, hidden // 2)


def chunk_rows(weight, chunk, shards):
    rows, depth = weight.shape
    grid = weight.reshape(shards, 2, 2, rows // (4 * shards), depth)[:, :, chunk]
    return [grid[:, side].reshape(-1, depth) for side in range(2)]


def halves(sums, depth):
    low, high = sums[..., 2 * depth : 3 * depth], sums[..., 3 * depth : 4 * depth]
    return sums[..., : 2 * depth], jnp.stack([low, high], -3)


def local(
    tokens,
    cotangent,
    lengths,
    rel_bucket,
    gain_attn,
    w_query,
    w_key,
    w_value,
    w_out,
    gain_ff,
    w_in,
    w_back,
    bias_table,
):
    place, me = lax.axis_index("dp"), lax.axis_index("seq")
    own, cot = tokens[0], cotangent[0]
    rows, depth = own.shape
    seq_len = rows * 2
    width = depth // 2
    near = lax.axis_size("dp") == BLOCKS
    length = lengths[0]
    part = place if near else jnp.int32(0)
    info = jnp.stack([me * rows, length, part, me]).astype(jnp.int32)
    far_info = jnp.stack([(1 - me) * rows, length, part, me]).astype(jnp.int32)

    if near:
        first = ready_first(info, w_query, w_key, w_value, gain_attn, gain_ff)
        come = spread(first, LEVELS)
    peer = hop(own, 1)

    padded = jnp.pad(rel_bucket, (0, 1), constant_values=-1)[::-1]
    padded = jnp.concatenate([padded[LANES:], padded[:LANES]])
    choice = jnp.arange(bias_table.shape[0], dtype=jnp.int32)[:, None] == padded[None, :]
    choice = choice.astype(f32)
    offsets = lax.dot_general(bias_table, choice, TN, precision=precise)
    offsets = offsets.reshape(-1, 2, 2 * seq_len)

    if near:
        one, two = ready_rest(info, w_out, w_in, w_back)
        first, come, one, two = tied(first, come, one, two)
        first = jnp.stack([first] + come)
        come = hop(first, 4)
        one_come = spread(one, LEVELS)
        first, come, peer, one, one_come, two = tied(first, come, peer, one, one_come, two)
        first = jnp.stack([first, come], axis=1)
        first = first.reshape((BLOCKS // 2,) + first.shape[2:])
        first = [first, hop(first, CORE)]
        one = [jnp.stack([one, one_come[0]]), jnp.stack(one_come[1:])]
        one_come = [hop(one[0], 4), hop(one[1], 1)]
        two_come = hop(two, 16)
    else:
        columns = [w_query, w_key, w_value]
        columns = [lax.dynamic_slice_in_dim(w, me * width, width, 1) for w in columns]
        gains = jnp.pad(jnp.stack([gain_attn, gain_ff], axis=1), ((0, 0), (0, LANES - 2)))
        first = whole_gather(jnp.concatenate(columns + [gains], axis=1))
        first = first.reshape(BLOCKS // 2, 2, -1, first.shape[1])
        first = [first[:, 0], first[:, 1]]
        in_all, back_all = whole_gather(w_in), whole_gather(w_back)
        one = [whole_gather(w_out), chunk_columns(in_all, 0)] + chunk_rows(back_all, 0, BLOCKS)
        one = jnp.concatenate(one, axis=1)
        two = jnp.concatenate([chunk_columns(in_all, 1)] + chunk_rows(back_all, 1, BLOCKS), axis=1)

    normed, query, keys, values, weights, gain_cols = project(info, own, peer, first, width)
    keys, values = keys.reshape(seq_len, width), values.reshape(seq_len, width)
    if near:
        query, one, one_come, two, two_come = tied(query, one, one_come, two, two_come)
        one = [jnp.stack([mine, come]) for mine, come in zip(one, one_come)]
        one_come = [hop(one[0], 1), hop(one[1], 4)]
        two = jnp.stack([two, two_come])
        two_come = hop(two, 8)
        query, one, two = tied(query, one, two)
    far_out, far_lse = attend(far_info, 1, query, keys, values, offsets)
    theirs = hop(far_out, 1)
    query, far_lse = tied(query, far_lse)
    near_out, near_lse = attend(info, 0, query, keys, values, offsets)
    if near:
        near_out, one, one_come, theirs, two, two_come = tied(
            near_out, one, one_come, theirs, two, two_come
        )
        one = planes_of(one, one_come)
        one_come = hop(one, CORE)
        two = jnp.stack([two, two_come], axis=1)
        two = two.reshape((4,) + two.shape[2:])
        two_come = spread(two, PLANES)
        one, two = tied(one, two)
        one = [one, one_come]
    made = feed_first(info, own, cot, near_out, theirs, gain_cols, one, not near)
    state, keep_one, send_one = made[:7], made[7], made[8]
    if near:
        come = hop(send_one, CORE)
        keep_one, two, two_come = tied(keep_one, two, two_come)
        two = jnp.stack([two] + two_come)
        two_come = hop(two, CORE)
        keep_one, two = tied(keep_one, two)
        keep_one, come_one = scatter_sums([keep_one, come], PLANES)
        state, keep_one = tied(state, keep_one)
        two = [two, two_come]
    made = feed_second(info, state, gain_cols, two, not near)
    result, mid_grad, mix_own, mix_peer, ff_gain, keep_two, send_two = made
    if near:
        keep_one, come_one, mix_peer, send_two = tied(keep_one, come_one, mix_peer, send_two)
        sums = [total_of([p[i] for p in [keep_one] + come_one], bf16) for i in range(4)]
        keep_one, away = jnp.stack([sums[0], sums[2]]), jnp.stack([sums[1], sums[3]])
        come_one = hop(away, LEVELS[0])
    far_grads = hop(mix_peer, 1)
    if near:
        come_two = hop(send_two, CORE)
        keep_one, keep_two, come_two = tied(keep_one, keep_two, come_two)
        keep_two, come_two = scatter_sums([keep_two, come_two], HEIGHTS)
        mix_own, keep_one, keep_two = tied(mix_own, keep_one, keep_two)
    dq_own, dk, dv, diag_own = attend_back(
        info, 0, query, keys, values, mix_own, near_out, near_lse, offsets, ()
    )
    if near:
        dk, keep_one, come_one, far_grads = tied(dk, keep_one, come_one, far_grads)
        keep_one, come_one = scatter_sums([keep_one, come_one], LEVELS[1:2])
        dk, keep_one = tied(dk, keep_one)
    dq_peer, dk, dv, diag_peer = attend_back(
        far_info, 1, query, keys, values, far_grads, far_out, far_lse, offsets, (dk, dv)
    )
    diag = (diag_own + diag_peer).reshape(-1, 2 * seq_len)
    table = lax.dot_general(choice, diag, NT, precision=precise)
    buckets, heads = table.shape
    shard = depth // BLOCKS
    table = jnp.pad(table, ((0, shard - buckets), (2, LANES - 2 - heads)))
    w_keep, w_send = weight_back(
        info, normed, dq_own, dq_peer, dk, dv, weights, gain_cols, ff_gain, table
    )
    if near:
        w_come = hop(w_send, CORE)
        keep_two, come_two, w_keep = tied(keep_two, come_two, w_keep)
        parts = [keep_two] + come_two
        away = total_of([p[2:] for p in parts], bf16)
        keep_two = total_of([p[:2] for p in parts], bf16)
        come_two = hop(away, 1)
        w_keep, w_come, keep_two = tied(w_keep, w_come, keep_two)
        w_keep, w_come = scatter_sums([w_keep, w_come], HEIGHTS)
        dk, w_keep = tied(dk, w_keep)
    stay, leave = project_back(info, dq_own, dq_peer, dk, dv, weights)
    come = hop(leave, 1)
    if near:
        keep_two, come_two, stay = tied(keep_two, come_two, stay)
        keep_two, come_two = scatter_sums([keep_two, come_two], (16,))
        w_keep, w_come, keep_two = tied(w_keep, w_come, keep_two)
        w_keep, w_come = scatter_sums([w_keep] + w_come, (16,))
        keep_two, come_two, w_keep = tied(keep_two, come_two, w_keep)
        grad_in, grad_back, grad_out = place_grads([keep_one] + come_one, [keep_two] + come_two, depth)
        w_keep, w_come, grad_in = tied(w_keep, w_come, grad_in)
        mine, theirs, table = halve_first(info, [w_keep] + w_come, buckets, heads)
        stay, come, mine = tied(stay, come, mine)
    grad_tokens = last(own, mid_grad, stay, come, gain_cols)
    if near:
        mine, grad_tokens = tied(mine, grad_tokens)
    else:
        scatter = functools.partial(lax.psum_scatter, scatter_dimension=0, tiled=True)
        both = ("dp", "seq")
        one_sum = join_grid(keep_one, send_one, ("y", "x", "z2", "z1"))
        two_sum = join_grid(keep_two, send_two, ("y", "z1", "x", "z2"))
        grad_first = join_grid(w_keep, w_send, ("y", "z1", "z2")).reshape(depth, -1)
        table = lax.psum(grad_first[:shard], "dp")
        table = table[:buckets, 3 * width + 2 : 3 * width + 2 + heads]
        grad_first = scatter(grad_first, "dp")
        in_one, back_one = halves(one_sum, depth)
        in_two, back_two = halves(two_sum, depth)
        grad_in = jnp.stack([in_one, in_two], axis=-2)
        grad_in = grad_in.reshape(-1, 2, 2 * BLOCKS, depth // BLOCKS).transpose(0, 2, 1, 3)
        grad_in = scatter(grad_in.reshape(-1, 4 * depth), both)
        grad_back = jnp.stack([back_one, back_two], axis=-4).reshape(-1, depth)
        grad_back = scatter(grad_back, both)
        grad_out = scatter(two_sum[..., 4 * depth :].reshape(-1, depth), both)
        count = grad_first.shape[0] // 2
        mine = lax.dynamic_slice_in_dim(grad_first, me * count, count, 0)
        theirs = lax.dynamic_slice_in_dim(grad_first, (1 - me) * count, count, 0)

    *full, attn_gain, ff_gain = place_first(info, mine, hop(theirs, 1))
    return (
        result[None],
        grad_tokens[None],
        attn_gain[0],
        full[0],
        full[1],
        full[2],
        grad_out,
        ff_gain[0],
        grad_in,
        grad_back,
        table,
    )


def solution(mesh):
    return jax.shard_map(
        local,
        mesh=mesh,
        in_specs=(
            P("dp", "seq", None),
            P("dp", "seq", None),
            P("dp"),
            P(),
            P("dp"),
            P("dp", None),
            P("dp", None),
            P("dp", None),
            P("dp", None),
            P("dp"),
            P("dp", None),
            P("dp", None),
            P(None, "seq"),
        ),
        out_specs=(
            P("dp", "seq", None),
            P("dp", "seq", None),
            P(("dp", "seq")),
            P(("dp", "seq"), None),
            P(("dp", "seq"), None),
            P(("dp", "seq"), None),
            P(("dp", "seq"), None),
            P(("dp", "seq")),
            P(("dp", "seq"), None),
            P(("dp", "seq"), None),
            P(None, "seq"),
        ),
        check_vma=False,
    )
```

```python
import functools

import jax
import jax.numpy as jnp
from jax import lax
from jax.experimental import pallas as pl
from jax.experimental.pallas import tpu as pltpu
from jax.sharding import PartitionSpec as P

DH = 64
PAIR = 2 * DH
LANES = 128
BLOCKS = 16
NT = (((1,), (1,)), ((), ()))
TN = (((0,), (0,)), ((), ()))
epsilon = 1e-06
masked_score = -1e30
precise = lax.Precision.HIGHEST
f32 = jnp.float32
bf16 = jnp.bfloat16
MiB = 2**20


def dot(a, b):
    return jnp.dot(a, b, preferred_element_type=f32)


def dot_nt(a, b):
    return lax.dot_general(a, b, NT, preferred_element_type=f32)


def dot_tn(a, b):
    return lax.dot_general(a, b, TN, preferred_element_type=f32)


def aligned(value, unit):
    return pl.multiple_of(value, unit)


def head_lanes(shape, dim, head):
    index = lax.broadcasted_iota(jnp.int32, shape, dim)
    return (index < DH) if head == 0 else (index >= DH)


def flag_lane(head):
    return DH if head == 0 else 0


def fill_bias(offsets_ref, head, bias_tile):
    row = jnp.broadcast_to(offsets_ref[0, head : head + 1, :], bias_tile.shape)
    bias_tile[...] = pltpu.roll(row, 0, 1, stride=1, stride_axis=0)


def masked_keys(keys, head, length):
    lane = lax.broadcasted_iota(jnp.int32, keys.shape, 1)
    position = lax.broadcasted_iota(jnp.int32, keys.shape, 0)
    other = jnp.where((lane == flag_lane(head)) & (position >= length), masked_score, 0.0)
    return jnp.where(head_lanes(keys.shape, 1, head), keys.astype(f32), other).astype(bf16)


def only_head(rows, head):
    return jnp.where(head_lanes(rows.shape, 1, head), rows.astype(f32), 0.0).astype(bf16)


def flagged(rows, head):
    lane = lax.broadcasted_iota(jnp.int32, rows.shape, 1)
    flag = jnp.where(lane == flag_lane(head), 1.0, 0.0)
    return jnp.where(head_lanes(rows.shape, 1, head), rows.astype(f32), flag).astype(bf16)


def bias_columns(bias_tile, first, count, key_tiles):
    parts = []
    for tile in range(key_tiles):
        start = aligned((key_tiles - 1 - tile) * LANES + first, LANES)
        parts.append(bias_tile[:, pl.ds(start, count)])
    return jnp.concatenate(parts, axis=0)


def attend_body(block, scal, q_ref, k_ref, v_ref, offsets_ref, out_ref, lse_ref, bias_tile):
    row0, length = scal[0], scal[1]
    rows, key_tiles = q_ref.shape[0], k_ref.shape[0] // LANES
    values_t = jnp.transpose(v_ref[...].astype(f32))
    outs = [[] for _ in range(rows // block)]
    for head in range(2):
        fill_bias(offsets_ref, head, bias_tile)
        keys = masked_keys(k_ref[...], head, length)
        values_h = jnp.where(head_lanes(values_t.shape, 0, head), values_t, 1.0).astype(bf16)
        for b in range(rows // block):
            rs = slice(b * block, (b + 1) * block)
            scores = dot_nt(keys, flagged(q_ref[rs, :], head))
            scores = scores + bias_columns(bias_tile, row0 + b * block, block, key_tiles)
            top = jnp.max(scores, axis=0, keepdims=True)
            weights = jnp.exp(scores - top).astype(bf16)
            mixed_t = dot(values_h, weights)
            total = mixed_t[flag_lane(head) : flag_lane(head) + 1]
            mine = mixed_t[:DH] if head == 0 else mixed_t[DH:]
            outs[b].append(mine / total)
            lse_ref[0, head : head + 1, rs] = top + jnp.log(total)
    for b in range(rows // block):
        joined = jnp.transpose(jnp.concatenate(outs[b], axis=0))
        out_ref[b * block : (b + 1) * block, :] = joined.astype(bf16)


def attend(scal, half, queries, keys, values, offsets):
    rows, width = queries.shape[1:]
    seq_len, pairs, span = keys.shape[0], width // PAIR, offsets.shape[2]
    block = min(512, rows)
    tokens_spec = pl.BlockSpec((rows, PAIR), lambda g, s: (0, g))
    keys_spec = pl.BlockSpec((seq_len, PAIR), lambda g, s: (0, g))
    work = rows * seq_len * width
    return pl.pallas_call(
        functools.partial(attend_body, block),
        out_shape=(
            jax.ShapeDtypeStruct((rows, width), bf16),
            jax.ShapeDtypeStruct((pairs, 2, rows), f32),
        ),
        grid_spec=pltpu.PrefetchScalarGridSpec(
            num_scalar_prefetch=1,
            grid=(pairs,),
            in_specs=[
                pl.BlockSpec((pl.Squeezed(), rows, PAIR), lambda g, s: (half, 0, g)),
                keys_spec,
                keys_spec,
                pl.BlockSpec((1, 2, span), lambda g, s: (g, 0, 0)),
            ],
            out_specs=[tokens_spec, pl.BlockSpec((1, 2, rows), lambda g, s: (g, 0, 0))],
            scratch_shapes=[pltpu.VMEM((LANES, span), f32)],
        ),
        compiler_params=pltpu.CompilerParams(vmem_limit_bytes=32 * MiB),
        cost_estimate=pl.CostEstimate(
            flops=16 * work, transcendentals=work // DH, bytes_accessed=4 * seq_len * width
        ),
        name="attend",
    )(scal, queries, keys, values, offsets)


def diagonal_sums(tile):
    span = tile.shape[1]
    size = tile.shape[0] // 2
    while size >= 8:
        tile = tile[:size] + pltpu.roll(tile[size:], span - size, 1)
        size //= 2
    row = lax.broadcasted_iota(jnp.int32, tile.shape, 0)
    for bit in (1, 2, 4):
        tile = jnp.where((row & bit) != 0, pltpu.roll(tile, span - bit, 1), tile)
    return jnp.sum(tile, axis=0, keepdims=True)


def attend_back_body(block, carry, scal, *refs):
    q_ref, k_ref, v_ref, g_ref, o_ref, lse_ref, offsets_ref = refs[:7]
    dq_ref, dk_ref, dv_ref, diag_ref, bias_tile, diag_tile, dk_sum, dv_sum = refs[-8:]
    row0, length = scal[0], scal[1]
    rows, key_tiles = q_ref.shape[0], k_ref.shape[0] // LANES
    if carry:
        dk_sum[...] = refs[7][...]
        dv_sum[...] = refs[8][...]
    else:
        dk_sum[...] = jnp.zeros_like(dk_sum)
        dv_sum[...] = jnp.zeros_like(dv_sum)
    keys_t = jnp.transpose(k_ref[...].astype(f32)).astype(bf16)
    count = rows // block
    dqs = [[] for _ in range(count)]
    deltas = []
    for b in range(count):
        rs = slice(b * block, (b + 1) * block)
        product = jnp.transpose(g_ref[rs, :].astype(f32) * o_ref[rs, :].astype(f32))
        deltas.append(
            (
                jnp.sum(product[:DH], axis=0, keepdims=True),
                jnp.sum(product[DH:], axis=0, keepdims=True),
            )
        )
    for head in range(2):
        fill_bias(offsets_ref, head, bias_tile)
        diag_tile[...] = jnp.zeros_like(diag_tile)
        keys = masked_keys(k_ref[...], head, length)
        for b in range(count):
            rs = slice(b * block, (b + 1) * block)
            queries = q_ref[rs, :]
            grads = only_head(g_ref[rs, :], head)
            scores = dot_nt(keys, flagged(queries, head))
            scores = scores + bias_columns(bias_tile, row0 + b * block, block, key_tiles)
            probs = jnp.exp(scores - lse_ref[0, head : head + 1, rs])
            grad_probs = dot_nt(v_ref[...], grads)
            grad_scores = probs * (grad_probs - deltas[b][head])
            for tile in range(key_tiles):
                start = aligned((key_tiles - 1 - tile) * LANES + row0 + b * block, LANES)
                diag_tile[:, pl.ds(start, block)] += grad_scores[tile * LANES : (tile + 1) * LANES]
            grad_scores = grad_scores.astype(bf16)
            dv_sum[...] += dot(probs.astype(bf16), grads)
            dk_sum[...] += dot(grad_scores, only_head(queries, head))
            dq_t = dot(keys_t, grad_scores)
            dqs[b].append(dq_t[:DH] if head == 0 else dq_t[DH:])
        diag_ref[0, head : head + 1, :] = diagonal_sums(diag_tile[...])
    for b in range(count):
        joined = jnp.transpose(jnp.concatenate(dqs[b], axis=0))
        dq_ref[b * block : (b + 1) * block, :] = joined.astype(bf16)
    dk_ref[...] = dk_sum[...].astype(dk_ref.dtype)
    dv_ref[...] = dv_sum[...].astype(dv_ref.dtype)


def attend_back(scal, half, queries, keys, values, grads, outs, lse, offsets, carry):
    rows, width = queries.shape[1:]
    seq_len, pairs, span = keys.shape[0], width // PAIR, offsets.shape[2]
    block = min(256, rows)
    rows_spec = pl.BlockSpec((rows, PAIR), lambda g, s: (0, g))
    keys_spec = pl.BlockSpec((seq_len, PAIR), lambda g, s: (0, g))
    offsets_spec = pl.BlockSpec((1, 2, span), lambda g, s: (g, 0, 0))
    specs = [
        pl.BlockSpec((pl.Squeezed(), rows, PAIR), lambda g, s: (half, 0, g)),
        keys_spec,
        keys_spec,
        rows_spec,
        rows_spec,
        pl.BlockSpec((1, 2, rows), lambda g, s: (g, 0, 0)),
        offsets_spec,
    ]
    kind = f32
    if carry:
        specs += [keys_spec, keys_spec]
        kind = bf16
    work = rows * seq_len * width
    return pl.pallas_call(
        functools.partial(attend_back_body, block, bool(carry)),
        out_shape=(
            jax.ShapeDtypeStruct((rows, width), bf16),
            jax.ShapeDtypeStruct((seq_len, width), kind),
            jax.ShapeDtypeStruct((seq_len, width), kind),
            jax.ShapeDtypeStruct(offsets.shape, f32),
        ),
        grid_spec=pltpu.PrefetchScalarGridSpec(
            num_scalar_prefetch=1,
            grid=(pairs,),
            in_specs=specs,
            out_specs=[rows_spec, keys_spec, keys_spec, offsets_spec],
            scratch_shapes=[
                pltpu.VMEM((LANES, span), f32),
                pltpu.VMEM((LANES, span), f32),
                pltpu.VMEM((seq_len, PAIR), f32),
                pltpu.VMEM((seq_len, PAIR), f32),
            ],
        ),
        compiler_params=pltpu.CompilerParams(vmem_limit_bytes=32 * MiB),
        cost_estimate=pl.CostEstimate(
            flops=40 * work, transcendentals=work // DH, bytes_accessed=12 * seq_len * width
        ),
        name="attend_back",
    )(scal, queries, keys, values, grads, outs, lse, offsets, *carry)


def normed_rows(values, gain_row):
    inverse = lax.rsqrt(jnp.mean(values * values, axis=-1, keepdims=True) + epsilon)
    return values * inverse * gain_row, inverse


def project_body(
    scal, own_ref, peer_ref, w0_ref, w1_ref, normed_ref, q_ref, k_ref, v_ref, w_ref, gain_ref, gain_row
):
    own_p = scal[2]
    side, step = pl.program_id(0), pl.program_id(1)
    rows, width = w0_ref.shape[1], q_ref.shape[1]

    @pl.when((side == 0) & (step == 0))
    def gather_weights():
        for core, piece in enumerate((w0_ref, w1_ref)):
            for index in range(BLOCKS // 2):
                part = ((index << 1) | core) ^ own_p
                start = aligned(part * rows, 16)
                w_ref[pl.ds(start, rows), :] = piece[index, :, : 3 * width]
                gain_ref[pl.ds(start, rows), :] = piece[index, :, 3 * width :].astype(f32)
        gain_row[...] = jnp.transpose(gain_ref[...])[0:8, :]

    values = jnp.where(side == 0, own_ref[...].astype(f32), peer_ref[...].astype(f32))
    normed = normed_rows(values, gain_row[0:1, :])[0].astype(bf16)
    normed_ref[...] = normed
    made = dot(normed, w_ref[...]).astype(bf16)
    q_ref[...] = made[:, :width]
    k_ref[...] = made[:, width : 2 * width]
    v_ref[...] = made[:, 2 * width :]


def project(scal, own, peer, pieces, width):
    rows, depth = own.shape
    block = min(256, rows)
    steps = rows // block
    whole = pl.BlockSpec(pieces[0].shape, lambda h, b, s: (0, 0, 0))
    by_half = pl.BlockSpec((pl.Squeezed(), block, width), lambda h, b, s: (h, b, 0))
    by_place = pl.BlockSpec((pl.Squeezed(), block, width), lambda h, b, s: (h ^ s[3], b, 0))
    stacked = jax.ShapeDtypeStruct((2, rows, width), bf16)
    return pl.pallas_call(
        project_body,
        out_shape=(
            jax.ShapeDtypeStruct((2, rows, depth), bf16),
            stacked,
            stacked,
            stacked,
            jax.ShapeDtypeStruct((depth, 3 * width), bf16),
            jax.ShapeDtypeStruct((depth, LANES), f32),
        ),
        grid_spec=pltpu.PrefetchScalarGridSpec(
            num_scalar_prefetch=1,
            grid=(2, steps),
            in_specs=[
                pl.BlockSpec((block, depth), lambda h, b, s: (b * (1 - h) + (steps - 1) * h, 0)),
                pl.BlockSpec((block, depth), lambda h, b, s: (b * h, 0)),
                whole,
                whole,
            ],
            out_specs=[
                pl.BlockSpec((pl.Squeezed(), block, depth), lambda h, b, s: (h, b, 0)),
                by_half,
                by_place,
                by_place,
                pl.BlockSpec((depth, 3 * width), lambda h, b, s: (0, 0)),
                pl.BlockSpec((depth, LANES), lambda h, b, s: (0, 0)),
            ],
            scratch_shapes=[pltpu.VMEM((8, depth), f32)],
        ),
        compiler_params=pltpu.CompilerParams(vmem_limit_bytes=60 * MiB),
        cost_estimate=pl.CostEstimate(
            flops=12 * rows * depth * width, transcendentals=0, bytes_accessed=10 * rows * depth
        ),
        name="project",
    )(scal, own, peer, *pieces)


def gelu_parts(values):
    scale = 0.7978845608028654
    square = values * values
    bend = jnp.tanh(scale * (values + 0.044715 * (values * square)))
    half = 0.5 * (1.0 + bend)
    slope = half + (0.5 * scale) * values * (1.0 - bend * bend) * (1.0 + 0.134145 * square)
    return values * half, slope


def bits_of(rel):
    return rel & 1, (rel >> 1) & 1, (rel >> 2) & 1, (rel >> 3) & 1, rel >> 4


def place_of(rel, leading):
    side, _, mid, low, high = bits_of(rel)
    if leading:
        return (mid << 1) | side, (high << 1) | low
    return (mid << 1) | low, (side << 1) | high


def zone_of(rel, zone, leading):
    side, _, mid, low, _ = bits_of(rel)
    if leading:
        return (mid << 1) | side, (zone << 1) + low
    return (mid << 1) | low, (side << 1) + zone


def assemble_rows(pieces, first_column, target, own_p, me):
    half = target.shape[1] // 2
    shard = pieces[0].shape[2]
    for rel in range(2 * BLOCKS):
        side, core = rel & 1, (rel >> 1) & 1
        plane, level = place_of(rel, True)
        row = aligned(((rel >> 1) ^ own_p) * shard, 16)
        column = aligned((side ^ me) * half, LANES)
        source = pieces[core][plane, level, :, pl.ds(first_column, half)]
        target[pl.ds(row, shard), pl.ds(column, half)] = source


def feed_body(leading, direct, scal, *refs):
    refs = list(refs)
    take = lambda count: [refs.pop(0) for _ in range(count)]
    if leading:
        tok_ref, cot_ref, mine_ref, theirs_ref, gain_ref = take(5)
    else:
        rows_in, mid_in, nff_in, out_in, grad_in, mix_in, wo_in, gain_ref = take(8)
    if direct:
        wo_ref = take(1)[0] if leading else None
        wi_ref, *wb_refs = take(3)
    else:
        pieces = take(2)
    if leading:
        rows_s, mid_s, nff_s, out_s, nff_grad, mix_s, wo_s = take(7)
    else:
        out_ref, mid_grad_ref, mix_own_ref, mix_peer_ref, gain_grad_ref = take(5)
    keep_ref, send_ref = take(2)
    if not leading:
        rows_s, mid_s, nff_s, mix_s, wo_s = rows_in, mid_in, nff_in, mix_in, wo_in
        out_s, nff_grad = take(2)
    nff_t, wi_s, wb_s, total = take(4)
    row0, length, own_p, me = scal[0], scal[1], scal[2], scal[3]
    own_r = own_p * 2 + me
    step = pl.program_id(0)
    rows, depth = rows_s.shape
    half = depth // 2
    steps, skip = 2, 1 if leading else 0
    count = depth // (2 * BLOCKS)
    gain_row = jnp.transpose(gain_ref[...])[1:2, :]

    def store_rows(column):
        for rel in range(2 * BLOCKS):
            start = aligned((rel ^ own_r) * count, 8)
            plane, level = place_of(rel, leading)
            target = send_ref if (rel >> 1) & 1 else keep_ref
            piece = total[pl.ds(start, count), :].astype(bf16)
            target[plane, level, :, pl.ds(column, depth)] = piece

    @pl.when(step == 0)
    def start():
        if leading:
            if direct:
                wo_s[...] = wo_ref[...]
            else:
                assemble_rows(pieces, 0, wo_s, own_p, me)
            mix_s[:, pl.ds(aligned(me * half, LANES), half)] = mine_ref[...]
            mix_s[:, pl.ds(aligned((1 - me) * half, LANES), half)] = theirs_ref[...]
            middle = tok_ref[...].astype(f32) + dot(mix_s[...], wo_s[...])
            mid_s[...] = middle
            nff_s[...] = normed_rows(middle, gain_row)[0].astype(bf16)
            position = row0 + lax.broadcasted_iota(jnp.int32, (rows, depth), 0)
            rows_s[...] = jnp.where(position < length, cot_ref[...].astype(f32), 0.0).astype(bf16)
            out_s[...] = middle
            nff_grad[...] = jnp.zeros_like(nff_grad)
        else:
            out_s[...] = out_in[...]
            nff_grad[...] = grad_in[...]
        nff_t[...] = jnp.transpose(nff_s[...].astype(f32)).astype(bf16)

    def hidden_block():
        shard = depth // BLOCKS
        if direct:
            wi_s[...] = wi_ref[...]
            for part in range(BLOCKS // 2):
                for side in range(2):
                    row = (2 * part + side) * shard
                    wb_s[row : row + shard, :] = wb_refs[side][part * shard : (part + 1) * shard, :]
        else:
            assemble_rows(pieces, aligned((skip + step) * half, LANES), wi_s, own_p, me)
            zone = step ^ (own_p >> 3)
            for rel in range(BLOCKS):
                plane, level = zone_of(rel, zone, True)
                column = aligned(((rel & 1) ^ me) * half, LANES)
                for side in range(2):
                    column_in = (skip + 2 + side) * half
                    source = pieces[(rel >> 1) & 1][plane, level, :, column_in : column_in + half]
                    row = aligned((2 * ((rel >> 1) ^ (own_p & 7)) + side) * shard, 16)
                    wb_s[pl.ds(row, shard), pl.ds(column, half)] = source
        pre = dot(nff_s[...], wi_s[...])
        hidden, slope = gelu_parts(pre)
        hidden = hidden.astype(bf16)
        out_s[...] += dot(hidden, wb_s[...])
        pre_grad = (dot_nt(rows_s[...], wb_s[...]) * slope).astype(bf16)
        total[...] = dot_tn(hidden, rows_s[...])
        zone = step ^ (own_p >> 3)
        for rel in range(BLOCKS):
            plane, level = zone_of(rel, zone, leading)
            target = send_ref if (rel >> 1) & 1 else keep_ref
            for side in range(2):
                row = aligned((rel ^ (own_r & 15)) * (2 * count) + side * count, 8)
                piece = total[pl.ds(row, count), :].astype(bf16)
                column = (steps + side) * depth
                target[plane, level, :, column : column + depth] = piece
        nff_grad[...] += dot_nt(pre_grad, wi_s[...])
        total[...] = dot(nff_t[...], pre_grad)
        store_rows(aligned(step * depth, LANES))

    if leading:
        hidden_block()
        return
    pl.when(step < steps)(hidden_block)

    @pl.when(step == steps)
    def finish():
        out_ref[...] = out_s[...].astype(bf16)
        middle = mid_s[...]
        inverse = lax.rsqrt(jnp.mean(middle * middle, axis=-1, keepdims=True) + epsilon)
        grads = nff_grad[...]
        gain_sum = jnp.sum(grads * middle * inverse, axis=0, keepdims=True)
        gain_grad_ref[...] = jnp.broadcast_to(gain_sum, gain_grad_ref.shape)
        scaled = grads * gain_row
        inner = jnp.sum(scaled * middle, axis=-1, keepdims=True)
        mid_grad = (
            rows_s[...].astype(f32)
            + inverse * scaled
            - middle * (inverse * inverse * inverse) * (inner / depth)
        )
        mid_grad_ref[...] = mid_grad
        attn_grad = mid_grad.astype(bf16)
        total[...] = dot_tn(mix_s[...], attn_grad)
        store_rows((steps + 2) * depth)
        turned = dot_nt(attn_grad, wo_s[...])
        first, second = turned[:, :half], turned[:, half:]
        mix_own_ref[...] = jnp.where(me == 0, first, second).astype(bf16)
        mix_peer_ref[...] = jnp.where(me == 0, second, first).astype(bf16)


def fixed(*shape):
    return pl.BlockSpec(shape, lambda *_: (0,) * len(shape), pipeline_mode=pl.Buffered(1))


def direct_specs(depth, skip):
    by_step = lambda f: jnp.minimum(f, 1)
    in_spec = pl.BlockSpec((depth, depth), lambda f, s: (0, by_step(f) + skip))
    low_spec = pl.BlockSpec((depth // 2, depth), lambda f, s: (by_step(f), 2 + skip))
    high_spec = pl.BlockSpec((depth // 2, depth), lambda f, s: (by_step(f), 3 + skip))
    return [fixed(depth, depth)] * skip + [in_spec, low_spec, high_spec]


def feed_call(leading, direct, scal, inputs, in_specs, outputs, chunk, scratch, name):
    rows, depth = outputs[0][0]
    count = depth // (2 * BLOCKS)
    sums = jax.ShapeDtypeStruct((4, 4, count, chunk * depth), bf16)
    return pl.pallas_call(
        functools.partial(feed_body, leading, direct),
        out_shape=[jax.ShapeDtypeStruct(*o) for o in outputs] + [sums] * 2,
        grid_spec=pltpu.PrefetchScalarGridSpec(
            num_scalar_prefetch=1,
            grid=(2 if leading else 3,),
            in_specs=in_specs,
            out_specs=[fixed(*o[0]) for o in outputs] + [fixed(*sums.shape)] * 2,
            scratch_shapes=scratch
            + [
                pltpu.VMEM((depth, rows), bf16),
                pltpu.VMEM((depth, depth), bf16),
                pltpu.VMEM((depth, depth), bf16),
                pltpu.VMEM((depth, depth), f32),
            ],
        ),
        compiler_params=pltpu.CompilerParams(vmem_limit_bytes=40 * MiB),
        cost_estimate=pl.CostEstimate(
            flops=24 * rows * depth * depth,
            transcendentals=2 * rows * depth,
            bytes_accessed=20 * MiB,
        ),
        name=name,
    )(scal, *inputs)


def feed_first(scal, tokens, cotangent, mine, theirs, gains, weights, direct):
    rows, depth = tokens.shape
    inputs = [tokens, cotangent, mine, theirs, gains]
    specs = [fixed(*v.shape) for v in inputs]
    if direct:
        inputs += [weights] * 4
        specs += direct_specs(depth, 1)
    else:
        inputs += weights
        specs += [fixed(*w.shape) for w in weights]
    whole = [(rows, depth)] * 6 + [(depth, depth)]
    outputs = list(zip(whole, [bf16, f32, bf16, f32, f32, bf16, bf16]))
    return feed_call(True, direct, scal, inputs, specs, outputs, 4, [], "feed_first")


def feed_second(scal, state, gains, weights, direct):
    rows, depth = state[0].shape
    half = depth // 2
    inputs = list(state) + [gains]
    specs = [fixed(*v.shape) for v in inputs]
    if direct:
        inputs += [weights] * 3
        specs += direct_specs(depth, 0)
    else:
        inputs += weights
        specs += [fixed(*w.shape) for w in weights]
    whole = [(rows, depth), (rows, depth), (rows, half), (rows, half), (8, depth)]
    outputs = list(zip(whole, [bf16, f32, bf16, bf16, f32]))
    scratch = [pltpu.VMEM((rows, depth), f32)] * 2
    return feed_call(False, direct, scal, inputs, specs, outputs, 5, scratch, "feed_second")


def weight_back_body(
    scal, normed_ref, dq0_ref, dq1_ref, dk_ref, dv_ref, w_ref, gain_ref, ff_ref, table_ref,
    keep_ref, away_ref, total
):
    own_p, me = scal[2], scal[3]
    rows, width = dq0_ref.shape
    depth = w_ref.shape[0]
    near, far = aligned(me * rows, 16), aligned((1 - me) * rows, 16)
    for i, ref in enumerate((None, dk_ref, dv_ref)):
        own = dq0_ref[...] if ref is None else ref[pl.ds(near, rows), :]
        peer = dq1_ref[...] if ref is None else ref[pl.ds(far, rows), :]
        total[:, i * width : (i + 1) * width] = dot_tn(normed_ref[0], own) + dot_tn(normed_ref[1], peer)
    weighted = jnp.sum(total[:, : 3 * width] * w_ref[...].astype(f32), axis=1, keepdims=True)
    lane = lax.broadcasted_iota(jnp.int32, (depth, LANES), 1)
    gains = jnp.where(lane == 0, weighted / gain_ref[:, 0:1], 0.0)
    ff_gain = jnp.transpose(jnp.broadcast_to(ff_ref[0:1, :], (LANES, depth)))
    total[:, 3 * width :] = jnp.where(lane == 1, ff_gain, gains)
    shard = depth // BLOCKS
    for rel in range(BLOCKS):
        start = aligned((rel ^ own_p) * shard, 16)
        whole = jnp.concatenate(
            [
                total[pl.ds(start, shard), : 3 * width],
                total[pl.ds(start, shard), 3 * width :] + table_ref[...],
            ],
            axis=1,
        )
        target = away_ref if rel & 1 else keep_ref
        mid, low, high = (rel >> 1) & 1, (rel >> 2) & 1, rel >> 3
        target[(mid << 1) | low, high] = whole.astype(bf16)


def weight_back(scal, normed, dq_own, dq_peer, dk, dv, weights, gains, ff_gain, table):
    rows, width = dq_own.shape
    depth = weights.shape[0]
    shard = depth // BLOCKS
    inputs = [normed, dq_own, dq_peer, dk, dv, weights, gains, ff_gain, table]
    shape = (4, 2, shard, 3 * width + LANES)
    return pl.pallas_call(
        weight_back_body,
        out_shape=[jax.ShapeDtypeStruct(shape, bf16)] * 2,
        grid_spec=pltpu.PrefetchScalarGridSpec(
            num_scalar_prefetch=1,
            grid=(1,),
            in_specs=[fixed(*v.shape) for v in inputs],
            out_specs=[fixed(*shape)] * 2,
            scratch_shapes=[pltpu.VMEM((depth, 3 * width + LANES), f32)],
        ),
        compiler_params=pltpu.CompilerParams(vmem_limit_bytes=24 * MiB),
        cost_estimate=pl.CostEstimate(
            flops=12 * rows * depth * width, transcendentals=0, bytes_accessed=16 * MiB
        ),
        name="weight_back",
    )(scal, *inputs)


def project_back_body(scal, dq0_ref, dq1_ref, dk_ref, dv_ref, w_ref, own_ref, send_ref, joined):
    side = pl.program_id(0)
    width = dq0_ref.shape[1]
    joined[:, :width] = jnp.where(side == 0, dq1_ref[...].astype(f32), dq0_ref[...].astype(f32)).astype(bf16)
    joined[:, width : 2 * width] = dk_ref[...]
    joined[:, 2 * width :] = dv_ref[...]
    grads = dot_nt(joined[...], w_ref[...])

    @pl.when(side == 0)
    def outgoing():
        send_ref[...] = grads.astype(bf16)

    @pl.when(side == 1)
    def staying():
        own_ref[...] = grads


def project_back(scal, dq_own, dq_peer, dk, dv, weights):
    rows, width = dq_own.shape
    depth = weights.shape[0]
    place = pl.BlockSpec((rows, width), lambda h, s: (1 - h ^ s[3], 0))
    return pl.pallas_call(
        project_back_body,
        out_shape=(
            jax.ShapeDtypeStruct((rows, depth), f32),
            jax.ShapeDtypeStruct((rows, depth), bf16),
        ),
        grid_spec=pltpu.PrefetchScalarGridSpec(
            num_scalar_prefetch=1,
            grid=(2,),
            in_specs=[
                fixed(rows, width),
                fixed(rows, width),
                place,
                place,
                fixed(depth, 3 * width),
            ],
            out_specs=[fixed(rows, depth), fixed(rows, depth)],
            scratch_shapes=[pltpu.VMEM((rows, 3 * width), bf16)],
        ),
        compiler_params=pltpu.CompilerParams(vmem_limit_bytes=16 * MiB),
        cost_estimate=pl.CostEstimate(
            flops=12 * rows * depth * width, transcendentals=0, bytes_accessed=8 * MiB
        ),
        name="project_back",
    )(scal, dq_own, dq_peer, dk, dv, weights)


def last_body(tok_ref, mid_ref, own_ref, come_ref, gain_ref, out_ref):
    depth = tok_ref.shape[1]
    gain_row = jnp.transpose(gain_ref[...])[0:1, :]
    values = tok_ref[...].astype(f32)
    inverse = lax.rsqrt(jnp.mean(values * values, axis=-1, keepdims=True) + epsilon)
    scaled = (own_ref[...] + come_ref[...].astype(f32)) * gain_row
    inner = jnp.sum(scaled * values, axis=-1, keepdims=True)
    grads = inverse * scaled - values * (inverse * inverse * inverse) * (inner / depth)
    out_ref[...] = (mid_ref[...] + grads).astype(bf16)


def last(tokens, mid_grad, own, come, gains):
    rows, depth = tokens.shape
    block = min(256, rows)
    spec = pl.BlockSpec((block, depth), lambda b: (b, 0))
    return pl.pallas_call(
        last_body,
        out_shape=jax.ShapeDtypeStruct((rows, depth), bf16),
        grid=(rows // block,),
        in_specs=[spec, spec, spec, spec, pl.BlockSpec((depth, LANES), lambda b: (0, 0))],
        out_specs=spec,
        compiler_params=pltpu.CompilerParams(vmem_limit_bytes=60 * MiB),
        cost_estimate=pl.CostEstimate(
            flops=16 * rows * depth, transcendentals=0, bytes_accessed=12 * rows * depth
        ),
        name="last",
    )(tokens, mid_grad, own, come, gains)


def chosen(me, low, high):
    return jnp.where(me == 0, low.astype(f32), high.astype(f32)).astype(low.dtype)


def column_of(row):
    count = row.shape[1]
    square = lax.broadcasted_iota(jnp.int32, (count, count), 0)
    other = lax.broadcasted_iota(jnp.int32, (count, count), 1)
    return jnp.sum(jnp.where(square == other, row.astype(f32), 0.0), axis=1, keepdims=True)


def ready_first_body(scal, q_ref, k_ref, v_ref, attn_ref, ff_ref, out_ref):
    me = scal[3]
    width = q_ref.shape[1] // 2
    for i, ref in enumerate((q_ref, k_ref, v_ref)):
        half = chosen(me, ref[:, :width], ref[:, width:])
        out_ref[:, i * width : (i + 1) * width] = half
    lane = lax.broadcasted_iota(jnp.int32, (q_ref.shape[0], LANES), 1)
    gains = jnp.where(lane == 0, column_of(attn_ref[...]), 0.0)
    gains = jnp.where(lane == 1, column_of(ff_ref[...]), gains)
    out_ref[:, 3 * width :] = gains.astype(bf16)


def ready_first(scal, w_query, w_key, w_value, gain_attn, gain_ff):
    rows, depth = w_query.shape
    inputs = [w_query, w_key, w_value, gain_attn[None], gain_ff[None]]
    shape = (rows, 3 * (depth // 2) + LANES)
    return pl.pallas_call(
        ready_first_body,
        out_shape=jax.ShapeDtypeStruct(shape, bf16),
        grid_spec=pltpu.PrefetchScalarGridSpec(
            num_scalar_prefetch=1,
            grid=(1,),
            in_specs=[fixed(*v.shape) for v in inputs],
            out_specs=fixed(*shape),
        ),
        compiler_params=pltpu.CompilerParams(vmem_limit_bytes=60 * MiB),
        name="ready_first",
    )(scal, *inputs)


def ready_rest_body(scal, out_ref, in_ref, back_ref, one_ref, two_ref):
    me = scal[3]
    depth = out_ref.shape[1]
    half = depth // 2
    shard = back_ref.shape[0] // 4
    columns = in_ref[...].astype(f32)
    step = columns.shape[1] // (4 * BLOCKS)
    chunks = []
    for chunk in range(2):
        pieces = [columns[:, (2 * r + chunk) * step : (2 * r + chunk + 1) * step] for r in range(2 * BLOCKS)]
        chunks.append(jnp.concatenate(pieces, axis=1).astype(bf16))
    one_ref[:, :half] = chosen(me, out_ref[:, :half], out_ref[:, half:])
    for f in range(2):
        block = chunks[0][:, f * depth : (f + 1) * depth]
        one_ref[:, (f + 1) * half : (f + 2) * half] = chosen(me, block[:, :half], block[:, half:])
        block = chunks[1][:, f * depth : (f + 1) * depth]
        two_ref[:, f * half : (f + 1) * half] = chosen(me, block[:, :half], block[:, half:])
    for side in range(2):
        rows = back_ref[2 * side * shard : (2 * side + 1) * shard, :]
        one_ref[:, (side + 3) * half : (side + 4) * half] = chosen(me, rows[:, :half], rows[:, half:])
        rows = back_ref[(2 * side + 1) * shard : (2 * side + 2) * shard, :]
        two_ref[:, (side + 2) * half : (side + 3) * half] = chosen(me, rows[:, :half], rows[:, half:])


def ready_rest(scal, w_out, w_in, w_back):
    rows, depth = w_out.shape
    inputs = [w_out, w_in, w_back]
    shapes = [(rows, 5 * depth // 2), (rows, 2 * depth)]
    return pl.pallas_call(
        ready_rest_body,
        out_shape=[jax.ShapeDtypeStruct(s, bf16) for s in shapes],
        grid_spec=pltpu.PrefetchScalarGridSpec(
            num_scalar_prefetch=1,
            grid=(1,),
            in_specs=[fixed(*v.shape) for v in inputs],
            out_specs=[fixed(*s) for s in shapes],
        ),
        compiler_params=pltpu.CompilerParams(vmem_limit_bytes=60 * MiB),
        name="ready_rest",
    )(scal, *inputs)


def summed_refs(refs, start, stop):
    total = refs[0][:, start:stop].astype(f32)
    for ref in refs[1:]:
        total = total + ref[:, start:stop].astype(f32)
    return total


def place_grads_body(count_one, *refs):
    one_refs, two_refs = refs[:count_one], refs[count_one:-3]
    in_ref, back_ref, out_ref = refs[-3:]
    rows, depth = out_ref.shape
    parts = [summed_refs(r, 0, 2 * depth) for r in (one_refs, two_refs)]
    step = 2 * depth // (2 * BLOCKS)
    pieces = []
    for r in range(2 * BLOCKS):
        for part in parts:
            pieces.append(part[:, r * step : (r + 1) * step])
    in_ref[...] = jnp.concatenate(pieces, axis=1)
    for chunk, r in enumerate((one_refs, two_refs)):
        for side in range(2):
            row = (2 * chunk + side) * rows
            back_ref[row : row + rows, :] = summed_refs(r, (2 + side) * depth, (3 + side) * depth)
    out_ref[...] = summed_refs(two_refs, 4 * depth, 5 * depth)


def place_grads(one_parts, two_parts, depth):
    rows = one_parts[0].shape[0]
    inputs = one_parts + two_parts
    shapes = [(rows, 4 * depth), (4 * rows, depth), (rows, depth)]
    return pl.pallas_call(
        functools.partial(place_grads_body, len(one_parts)),
        out_shape=[jax.ShapeDtypeStruct(s, f32) for s in shapes],
        grid=(1,),
        in_specs=[fixed(*v.shape) for v in inputs],
        out_specs=[fixed(*s) for s in shapes],
        compiler_params=pltpu.CompilerParams(vmem_limit_bytes=16 * MiB),
        name="place_grads",
    )(*inputs)


def halve_first_body(column, scal, *refs):
    me = scal[3]
    parts, (mine_ref, theirs_ref, table_ref) = refs[:-3], refs[-3:]
    total = summed_refs(parts, 0, parts[0].shape[1])
    rows = total.shape[0] // 2
    mine_ref[...] = jnp.where(me == 0, total[:rows], total[rows:])
    theirs_ref[...] = jnp.where(me == 0, total[rows:], total[:rows])
    table_ref[...] = total[: table_ref.shape[0], column : column + table_ref.shape[1]]


def halve_first(scal, parts, buckets, heads):
    rows, wide = parts[0].shape
    shapes = [(rows // 2, wide), (rows // 2, wide), (buckets, heads)]
    return pl.pallas_call(
        functools.partial(halve_first_body, wide - LANES + 2),
        out_shape=[jax.ShapeDtypeStruct(s, f32) for s in shapes],
        grid_spec=pltpu.PrefetchScalarGridSpec(
            num_scalar_prefetch=1,
            grid=(1,),
            in_specs=[fixed(*v.shape) for v in parts],
            out_specs=[fixed(*s) for s in shapes],
        ),
        compiler_params=pltpu.CompilerParams(vmem_limit_bytes=16 * MiB),
        name="halve_first",
    )(scal, *parts)


def place_first_body(scal, mine_ref, theirs_ref, *out_refs):
    me = scal[3]
    width = out_refs[0].shape[1] // 2
    for i, ref in enumerate(out_refs[:3]):
        mine = mine_ref[:, i * width : (i + 1) * width]
        theirs = theirs_ref[:, i * width : (i + 1) * width]
        ref[:, :width] = jnp.where(me == 0, mine, theirs)
        ref[:, width:] = jnp.where(me == 0, theirs, mine)
    gains = mine_ref[:, 3 * width :] + theirs_ref[:, 3 * width :]
    rows = gains.shape[0]
    square = lax.broadcasted_iota(jnp.int32, (rows, rows), 0)
    other = lax.broadcasted_iota(jnp.int32, (rows, rows), 1)
    for i in range(2):
        spread_out = jnp.where(square == other, gains[:, i : i + 1], 0.0)
        out_refs[3 + i][...] = jnp.sum(spread_out, axis=0, keepdims=True)


def place_first(scal, mine, theirs):
    rows, wide = mine.shape
    depth = (wide - LANES) // 3 * 2
    shapes = [(rows, depth)] * 3 + [(1, rows)] * 2
    return pl.pallas_call(
        place_first_body,
        out_shape=[jax.ShapeDtypeStruct(s, f32) for s in shapes],
        grid_spec=pltpu.PrefetchScalarGridSpec(
            num_scalar_prefetch=1,
            grid=(1,),
            in_specs=[fixed(*mine.shape)] * 2,
            out_specs=[fixed(*s) for s in shapes],
        ),
        compiler_params=pltpu.CompilerParams(vmem_limit_bytes=16 * MiB),
        name="place_first",
    )(scal, mine, theirs)


def hop(value, mask):
    size = lax.axis_size("dp") * 2
    return lax.ppermute(value, ("dp", "seq"), [(i, i ^ mask) for i in range(size)])


def tied(*values):
    return lax.optimization_barrier(values)


LEVELS = (8, 16, 24)
PLANES = (1, 4, 5)
HEIGHTS = (8, 4, 12)
ENDS = (16, 1, 17)
CORE = 2


def spread(value, masks):
    return [hop(value, mask) for mask in masks]


def total_of(parts, kind):
    total = parts[0].astype(f32)
    for part in parts[1:]:
        total = total + part.astype(f32)
    return total.astype(kind)


def scatter_sums(parts, masks):
    sums = [total_of([p[i] for p in parts], bf16) for i in range(len(masks) + 1)]
    return sums[0], [hop(s, m) for s, m in zip(sums[1:], masks)]


def planes_of(mine, come):
    first = jnp.stack([mine[0], come[0]], axis=1)
    second = jnp.stack([mine[1], come[1]])
    parts = [v.reshape((4,) + v.shape[2:]) for v in (first, second)]
    return jnp.concatenate(parts, axis=1)


def whole_gather(shard):
    return lax.all_gather(shard, "dp", axis=0, tiled=True)


def join_grid(keep, send, axes):
    both = jnp.stack([keep, send])
    both = both.reshape((2,) * (len(axes) + 1) + both.shape[-2:])
    axes = ("c",) + axes
    order = ("z2", "z1", "y", "c") + (("x",) if "x" in axes else ())
    both = both.transpose([axes.index(n) for n in order] + [both.ndim - 2, both.ndim - 1])
    if "x" in axes:
        both = jnp.where(lax.axis_index("seq") == 1, jnp.flip(both, 4), both)
    return both.astype(f32)


def chunk_columns(weight, chunk):
    rows, hidden = weight.shape
    grid = weight.reshape(rows, BLOCKS * 2, 2, hidden // (4 * BLOCKS))
    return grid[:, :, chunk].reshape(rows, hidden // 2)


def chunk_rows(weight, chunk, shards):
    rows, depth = weight.shape
    grid = weight.reshape(shards, 2, 2, rows // (4 * shards), depth)[:, :, chunk]
    return [grid[:, side].reshape(-1, depth) for side in range(2)]


def halves(sums, depth):
    low, high = sums[..., 2 * depth : 3 * depth], sums[..., 3 * depth : 4 * depth]
    return sums[..., : 2 * depth], jnp.stack([low, high], -3)


def local(
    tokens,
    cotangent,
    lengths,
    rel_bucket,
    gain_attn,
    w_query,
    w_key,
    w_value,
    w_out,
    gain_ff,
    w_in,
    w_back,
    bias_table,
):
    place, me = lax.axis_index("dp"), lax.axis_index("seq")
    own, cot = tokens[0], cotangent[0]
    rows, depth = own.shape
    seq_len = rows * 2
    width = depth // 2
    near = lax.axis_size("dp") == BLOCKS
    length = lengths[0]
    part = place if near else jnp.int32(0)
    info = jnp.stack([me * rows, length, part, me]).astype(jnp.int32)
    far_info = jnp.stack([(1 - me) * rows, length, part, me]).astype(jnp.int32)

    if near:
        first = ready_first(info, w_query, w_key, w_value, gain_attn, gain_ff)
        come = spread(first, LEVELS)
    peer = hop(own, 1)

    padded = jnp.pad(rel_bucket, (0, 1), constant_values=-1)[::-1]
    padded = jnp.concatenate([padded[LANES:], padded[:LANES]])
    choice = jnp.arange(bias_table.shape[0], dtype=jnp.int32)[:, None] == padded[None, :]
    choice = choice.astype(f32)
    offsets = lax.dot_general(bias_table, choice, TN, precision=precise)
    offsets = offsets.reshape(-1, 2, 2 * seq_len)

    if near:
        one, two = ready_rest(info, w_out, w_in, w_back)
        first, come, one, two = tied(first, come, one, two)
        first = jnp.stack([first] + come)
        come = hop(first, 4)
        one_come = spread(one, LEVELS)
        first, come, peer, one, one_come, two = tied(first, come, peer, one, one_come, two)
        first = jnp.stack([first, come], axis=1)
        first = first.reshape((BLOCKS // 2,) + first.shape[2:])
        first = [first, hop(first, CORE)]
        one = [jnp.stack([one, one_come[0]]), jnp.stack(one_come[1:])]
        one_come = [hop(one[0], 4), hop(one[1], 1)]
        two_come = hop(two, 16)
    else:
        columns = [w_query, w_key, w_value]
        columns = [lax.dynamic_slice_in_dim(w, me * width, width, 1) for w in columns]
        gains = jnp.pad(jnp.stack([gain_attn, gain_ff], axis=1), ((0, 0), (0, LANES - 2)))
        first = whole_gather(jnp.concatenate(columns + [gains], axis=1))
        first = first.reshape(BLOCKS // 2, 2, -1, first.shape[1])
        first = [first[:, 0], first[:, 1]]
        in_all, back_all = whole_gather(w_in), whole_gather(w_back)
        one = [whole_gather(w_out), chunk_columns(in_all, 0)] + chunk_rows(back_all, 0, BLOCKS)
        one = jnp.concatenate(one, axis=1)
        two = jnp.concatenate([chunk_columns(in_all, 1)] + chunk_rows(back_all, 1, BLOCKS), axis=1)

    normed, query, keys, values, weights, gain_cols = project(info, own, peer, first, width)
    keys, values = keys.reshape(seq_len, width), values.reshape(seq_len, width)
    if near:
        query, one, one_come, two, two_come = tied(query, one, one_come, two, two_come)
        left = jnp.stack([one[0], one_come[0]])
        left_come = hop(left, 1)
        left, right, come = tied(left, one[1], one_come[1])
        one = [left, jnp.stack([right, come])]
        one_come = [left_come, hop(one[1], 4)]
        two = jnp.stack([two, two_come])
        two_come = hop(two, 8)
        query, one, two = tied(query, one, two)
    far_out, far_lse = attend(far_info, 1, query, keys, values, offsets)
    theirs = hop(far_out, 1)
    query, far_lse = tied(query, far_lse)
    near_out, near_lse = attend(info, 0, query, keys, values, offsets)
    if near:
        near_out, one, one_come, theirs, two, two_come = tied(
            near_out, one, one_come, theirs, two, two_come
        )
        one = planes_of(one, one_come)
        one_come = hop(one, CORE)
        two = jnp.stack([two, two_come], axis=1)
        two = two.reshape((4,) + two.shape[2:])
        two_come = spread(two, PLANES)
        one, two = tied(one, two)
        one = [one, one_come]
    made = feed_first(info, own, cot, near_out, theirs, gain_cols, one, not near)
    state, keep_one, send_one = made[:7], made[7], made[8]
    if near:
        come = hop(send_one, CORE)
        keep_one, two, two_come = tied(keep_one, two, two_come)
        two = jnp.stack([two] + two_come)
        two_come = hop(two, CORE)
        keep_one, two = tied(keep_one, two)
        keep_one, come_one = scatter_sums([keep_one, come], PLANES)
        state, keep_one = tied(state, keep_one)
        two = [two, two_come]
    made = feed_second(info, state, gain_cols, two, not near)
    result, mid_grad, mix_own, mix_peer, ff_gain, keep_two, send_two = made
    if near:
        keep_one, come_one, mix_peer, send_two = tied(keep_one, come_one, mix_peer, send_two)
        sums = [total_of([p[i] for p in [keep_one] + come_one], bf16) for i in range(4)]
        keep_one, away = jnp.stack([sums[0], sums[2]]), jnp.stack([sums[1], sums[3]])
        come_one = hop(away, LEVELS[0])
    far_grads = hop(mix_peer, 1)
    if near:
        come_two = hop(send_two, CORE)
        keep_one, keep_two, come_two = tied(keep_one, keep_two, come_two)
        keep_two, come_two = scatter_sums([keep_two, come_two], HEIGHTS)
        mix_own, keep_one, keep_two = tied(mix_own, keep_one, keep_two)
    dq_own, dk, dv, diag_own = attend_back(
        info, 0, query, keys, values, mix_own, near_out, near_lse, offsets, ()
    )
    if near:
        dk, keep_one, come_one, far_grads = tied(dk, keep_one, come_one, far_grads)
        keep_one, come_one = scatter_sums([keep_one, come_one], LEVELS[1:2])
        dk, keep_one = tied(dk, keep_one)
    dq_peer, dk, dv, diag_peer = attend_back(
        far_info, 1, query, keys, values, far_grads, far_out, far_lse, offsets, (dk, dv)
    )
    diag = (diag_own + diag_peer).reshape(-1, 2 * seq_len)
    table = lax.dot_general(choice, diag, NT, precision=precise)
    buckets, heads = table.shape
    shard = depth // BLOCKS
    table = jnp.pad(table, ((0, shard - buckets), (2, LANES - 2 - heads)))
    w_keep, w_send = weight_back(
        info, normed, dq_own, dq_peer, dk, dv, weights, gain_cols, ff_gain, table
    )
    if near:
        w_come = hop(w_send, CORE)
        keep_two, come_two, w_keep = tied(keep_two, come_two, w_keep)
        parts = [keep_two] + come_two
        away = total_of([p[2:] for p in parts], bf16)
        keep_two = total_of([p[:2] for p in parts], bf16)
        come_two = hop(away, 1)
        w_keep, w_come, keep_two = tied(w_keep, w_come, keep_two)
        w_keep, w_come = scatter_sums([w_keep, w_come], HEIGHTS)
        dk, w_keep = tied(dk, w_keep)
    stay, leave = project_back(info, dq_own, dq_peer, dk, dv, weights)
    come = hop(leave, 1)
    if near:
        keep_two, come_two, stay = tied(keep_two, come_two, stay)
        keep_two, come_two = scatter_sums([keep_two, come_two], (16,))
        w_keep, w_come, keep_two = tied(w_keep, w_come, keep_two)
        w_keep, w_come = scatter_sums([w_keep] + w_come, (16,))
        keep_two, come_two, w_keep = tied(keep_two, come_two, w_keep)
        grad_in, grad_back, grad_out = place_grads([keep_one] + come_one, [keep_two] + come_two, depth)
        w_keep, w_come, grad_in = tied(w_keep, w_come, grad_in)
        mine, theirs, table = halve_first(info, [w_keep] + w_come, buckets, heads)
        stay, come, mine = tied(stay, come, mine)
    grad_tokens = last(own, mid_grad, stay, come, gain_cols)
    if near:
        mine, grad_tokens = tied(mine, grad_tokens)
    else:
        scatter = functools.partial(lax.psum_scatter, scatter_dimension=0, tiled=True)
        both = ("dp", "seq")
        one_sum = join_grid(keep_one, send_one, ("y", "x", "z2", "z1"))
        two_sum = join_grid(keep_two, send_two, ("y", "z1", "x", "z2"))
        grad_first = join_grid(w_keep, w_send, ("y", "z1", "z2")).reshape(depth, -1)
        table = lax.psum(grad_first[:shard], "dp")
        table = table[:buckets, 3 * width + 2 : 3 * width + 2 + heads]
        grad_first = scatter(grad_first, "dp")
        in_one, back_one = halves(one_sum, depth)
        in_two, back_two = halves(two_sum, depth)
        grad_in = jnp.stack([in_one, in_two], axis=-2)
        grad_in = grad_in.reshape(-1, 2, 2 * BLOCKS, depth // BLOCKS).transpose(0, 2, 1, 3)
        grad_in = scatter(grad_in.reshape(-1, 4 * depth), both)
        grad_back = jnp.stack([back_one, back_two], axis=-4).reshape(-1, depth)
        grad_back = scatter(grad_back, both)
        grad_out = scatter(two_sum[..., 4 * depth :].reshape(-1, depth), both)
        count = grad_first.shape[0] // 2
        mine = lax.dynamic_slice_in_dim(grad_first, me * count, count, 0)
        theirs = lax.dynamic_slice_in_dim(grad_first, (1 - me) * count, count, 0)

    *full, attn_gain, ff_gain = place_first(info, mine, hop(theirs, 1))
    return (
        result[None],
        grad_tokens[None],
        attn_gain[0],
        full[0],
        full[1],
        full[2],
        grad_out,
        ff_gain[0],
        grad_in,
        grad_back,
        table,
    )


def solution(mesh):
    return jax.shard_map(
        local,
        mesh=mesh,
        in_specs=(
            P("dp", "seq", None),
            P("dp", "seq", None),
            P("dp"),
            P(),
            P("dp"),
            P("dp", None),
            P("dp", None),
            P("dp", None),
            P("dp", None),
            P("dp"),
            P("dp", None),
            P("dp", None),
            P(None, "seq"),
        ),
        out_specs=(
            P("dp", "seq", None),
            P("dp", "seq", None),
            P(("dp", "seq")),
            P(("dp", "seq"), None),
            P(("dp", "seq"), None),
            P(("dp", "seq"), None),
            P(("dp", "seq"), None),
            P(("dp", "seq")),
            P(("dp", "seq"), None),
            P(("dp", "seq"), None),
            P(None, "seq"),
        ),
        check_vma=False,
    )
```
